32 devices in a mesh: dp: 8 (over y, x, core), tp: 4 (over z).
Axes of the slice: x: 2, y: 2, z: 4, core: 2. Of those that a mesh axis runs over, the one named last changes fastest.
Arguments:
- block_in: bfloat16 [128, 4, 37632], P('dp', 'tp'), may hold values from -6 to 6
- ln1_gain: float32 [768], P('tp'), may hold values from 0.1 to 1.9
- ln1_shift: float32 [768], P('tp'), may hold values from -1.75 to 1.75
- tok_w1: float32 [196, 384], replicated, may hold values from -0.4375 to 0.4375
- tok_b1: float32 [384], replicated, may hold values from -1.75 to 1.75
- tok_w2: float32 [384, 196], replicated, may hold values from -0.3125 to 0.3125
- tok_b2: float32 [196], replicated, may hold values from -1.75 to 1.75
- ln2_gain: float32 [768], P('tp'), may hold values from 0.1 to 1.9
- ln2_shift: float32 [768], P('tp'), may hold values from -1.75 to 1.75
- ch_w1: float32 [768, 3072], P('dp', 'tp'), may hold values from -0.21875 to 0.21875
- ch_b1: float32 [3072], replicated, may hold values from -1.75 to 1.75
- ch_w2: float32 [3072, 768], P('tp', 'dp'), may hold values from -0.109375 to 0.109375
- ch_b2: float32 [768], replicated, may hold values from -1.75 to 1.75
- group_ids: int32 [128], P('dp'), may hold values from 0 to 63
- out_grad: bfloat16 [128, 4, 37632], P('dp', 'tp'), may hold values from -6 to 6
Outputs:
- block_out: bfloat16 [128, 4, 37632], P('dp', 'tp')
- dx: bfloat16 [128, 4, 37632], P('dp', 'tp')
- group_norms: float32 [64], replicated
- d_ln1_gain: float32 [768], P('tp')
- d_ln1_shift: float32 [768], P('tp')
- d_tok_w1: float32 [196, 384], replicated
- d_tok_b1: float32 [384], replicated
- d_tok_w2: float32 [384, 196], replicated
- d_tok_b2: float32 [196], replicated
- d_ln2_gain: float32 [768], P('tp')
- d_ln2_shift: float32 [768], P('tp')
- d_ch_w1: float32 [768, 3072], P('dp', 'tp')
- d_ch_b1: float32 [3072], replicated
- d_ch_w2: float32 [3072, 768], P('tp', 'dp')
- d_ch_b2: float32 [768], replicated
The draws below stay inside these ranges and needn't reach their ends.
All inputs are finite; a program needn't handle non-finite values.
Results may differ from the reference program's by a relative error of at most 0.01.
Values may be sent and summed in bfloat16 or wider, within the bound.
A program may use at most 128 MiB of HBM per device.

```python
import math
import jax
import jax.numpy as jnp
import numpy as np
from jax import lax

D = 768
DC = 3072
S = 196
DS = 384
GROUPS = 64
IMAGES = 128
CG = 4
CW = 192
N_TP = 4


def plant(array, rng, least, top_value):
    place = [jax.random.randint(jax.random.fold_in(rng, axis), (), 0, length) for axis, length in enumerate(array.shape)]
    longest = array.shape.index(max(array.shape))
    neighbour = place[:longest] + [(place[longest] + 1) % array.shape[longest]] + place[longest + 1:]
    return array.at[tuple(place)].set(least).at[tuple(neighbour)].set(top_value)


def block_levels(rng, shape, cuts, least, largest):
    loudness, own = 1.0, jax.random.fold_in(rng, 6)
    for position, shards_of in cuts:
        draws = jnp.exp(jax.random.uniform(jax.random.fold_in(own, position), (shards_of,), jnp.float32, least / len(cuts), largest / len(cuts)))
        loudness = loudness * jnp.repeat(draws, shape[position] // shards_of).reshape([-1 if axis == position else 1 for axis in range(len(shape))])
    return loudness


def rank_table(count, slope):
    loads = [(1 << 20) // math.isqrt(grade ** slope) + 1 for grade in range(1, count + 1)]
    scale = 1 + sum(loads) // (1 << 30)
    return np.cumsum(np.array([max(1, weight // scale) for weight in loads]))


def skewed_ids(key, extent, number_of, slope):
    listing = rank_table(number_of, slope)
    lot = jax.random.randint(jax.random.fold_in(key, 1), extent, 0, int(listing[number_of - 1]))
    rank = jnp.searchsorted(jnp.asarray(listing, jnp.int32), lot, side="right")
    return jax.random.permutation(jax.random.fold_in(key, 2), number_of)[rank].astype(jnp.int32)


def noise(rng, dims, width, limit, cuts=(), kind=jnp.bfloat16):
    result = width * jax.random.normal(rng, dims, jnp.float32)
    if cuts:
        result = result * block_levels(rng, dims, cuts, -0.22, 0.18)
    return jnp.clip(result, -limit, limit).astype(kind)


def setup_inputs(seed: int = 0) -> dict:
    keys = jax.random.split(jax.random.key(seed), 16)
    return {
        "block_in": noise(keys[0], (IMAGES, CG, S * CW), 1.0, 6.0, ((0, 8), (1, 4))),
        "ln1_gain": jnp.clip(1.0 + 0.18 * jax.random.normal(keys[1], (D,), jnp.float32), 0.1, 1.9),
        "ln1_shift": noise(keys[2], (D,), 0.3, 1.75, ((0, 4),), jnp.float32),
        "tok_w1": noise(keys[3], (S, DS), S ** -0.5, 0.4375, (), jnp.float32),
        "tok_b1": noise(keys[4], (DS,), 0.3, 1.75, (), jnp.float32),
        "tok_w2": noise(keys[5], (DS, S), DS ** -0.5, 0.3125, (), jnp.float32),
        "tok_b2": noise(keys[6], (S,), 0.3, 1.75, (), jnp.float32),
        "ln2_gain": jnp.clip(1.0 + 0.18 * jax.random.normal(keys[7], (D,), jnp.float32), 0.1, 1.9),
        "ln2_shift": noise(keys[8], (D,), 0.3, 1.75, ((0, 4),), jnp.float32),
        "ch_w1": noise(keys[9], (D, DC), D ** -0.5, 0.21875, ((0, 8), (1, 4)), jnp.float32),
        "ch_b1": noise(keys[10], (DC,), 0.3, 1.75, (), jnp.float32),
        "ch_w2": noise(keys[11], (DC, D), DC ** -0.5, 0.109375, ((0, 4), (1, 8)), jnp.float32),
        "ch_b2": noise(keys[12], (D,), 0.3, 1.75, (), jnp.float32),
        "group_ids": plant(skewed_ids(keys[13], (IMAGES,), GROUPS, 2), jax.random.fold_in(keys[13], 3), 0, GROUPS - 1).astype(jnp.int32),
        "out_grad": noise(keys[14], (IMAGES, CG, S * CW), 1.0, 6.0, ((0, 8), (1, 4))),
    }


@jax.custom_vjp
def low(v):
    return lax.optimization_barrier(v.astype(jnp.bfloat16)).astype(jnp.float32)

@jax.custom_vjp
def low_back(v):
    return v

def low_keep(v):
    return (low(v), None)

def low_pass(kept, grad):
    return (grad,)

def back_keep(v):
    return (v, None)

def back_low(kept, grad):
    return (low(grad),)
low.defvjp(low_keep, low_pass)
low_back.defvjp(back_keep, back_low)
highest = lax.Precision.HIGHEST
epsilon = 1e-06

def to_plain(stored):
    return stored.reshape(IMAGES, N_TP, S, D // N_TP).transpose(0, 2, 1, 3).reshape(IMAGES, S, D)

def to_stored(plain):
    return plain.reshape(IMAGES, S, N_TP, D // N_TP).transpose(0, 2, 1, 3).reshape(IMAGES, N_TP, S * (D // N_TP))

def layer_norm(values, gain, shift):
    average = lax.optimization_barrier(jnp.mean(values, -1, keepdims=True))
    variance = lax.optimization_barrier(jnp.mean(values * values, -1, keepdims=True)) - average * average
    return (values - average) * lax.rsqrt(variance + epsilon) * gain + shift

def forward(params, inputs, group_block):
    mixed = low(layer_norm(inputs, params['g1'], params['s1']))
    pre_act = low_back(jnp.einsum('nsc,sk->nck', mixed, low(params['tw1']), precision=highest) + params['tb1'])
    hidden = low(jax.nn.gelu(pre_act))
    token_out = low_back(jnp.einsum('nck,ks->nsc', hidden, low(params['tw2']), precision=highest) + params['tb2'][None, :, None])
    residual = inputs + token_out
    member = (group_block[:, None] == jnp.arange(GROUPS)[None, :]).astype(jnp.float32)
    gain_two = jnp.dot(member, params['g2'], precision=highest)[:, None, :]
    shift_two = jnp.dot(member, params['s2'], precision=highest)[:, None, :]
    branch_in = low(layer_norm(residual, gain_two, shift_two))
    inner_act = low_back(jnp.einsum('nsc,ch->nsh', branch_in, low(params['cw1']), precision=highest) + params['cb1'])
    activated = low(jax.nn.gelu(inner_act))
    branch_out = jnp.einsum('nsh,hc->nsc', activated, low(params['cw2']), precision=highest) + params['cb2']
    branch_out = low_back(low(branch_out))
    return residual + branch_out

def reference(block_in, ln1_gain, ln1_shift, tok_w1, tok_b1, tok_w2, tok_b2, ln2_gain, ln2_shift, ch_w1, ch_b1, ch_w2, ch_b2, group_ids, out_grad):
    params = {'g1': ln1_gain, 's1': ln1_shift, 'tw1': tok_w1, 'tb1': tok_b1, 'tw2': tok_w2, 'tb2': tok_b2, 'g2': jnp.broadcast_to(ln2_gain[None, :], (GROUPS, D)), 's2': jnp.broadcast_to(ln2_shift[None, :], (GROUPS, D)), 'cw1': ch_w1, 'cb1': ch_b1, 'cw2': ch_w2, 'cb2': ch_b2}
    block_size = math.gcd(IMAGES, 16)
    blocks = IMAGES // block_size
    inputs = to_plain(block_in.astype(jnp.float32)).reshape(blocks, block_size, S, D)
    groups = group_ids.reshape(blocks, block_size)
    cotangent = to_plain(out_grad.astype(jnp.float32)).reshape(blocks, block_size, S, D)

    def advance(running, item):
        input_block, group_block, grad_block = item
        output, pull_back = jax.vjp(lambda pr, xv: forward(pr, xv, group_block), params, input_block)
        grad_params, grad_input = pull_back(grad_block)
        running = jax.tree.map(lambda left, right: left + right, running, grad_params)
        return (running, (output.astype(jnp.bfloat16), grad_input.astype(jnp.bfloat16)))
    zeros = jax.tree.map(jnp.zeros_like, params)
    running, (outputs, grad_inputs) = lax.scan(advance, zeros, (inputs, groups, cotangent))
    group_gain = running['g2']
    group_shift = running['s2']
    group_norms = jnp.sqrt(lax.optimization_barrier(jnp.sum(group_gain * group_gain + group_shift * group_shift, 1)))
    clip_bound = 2.0 * math.sqrt(IMAGES * S * D / GROUPS)
    factor = clip_bound / jnp.maximum(group_norms, clip_bound)
    clipped_gain = lax.optimization_barrier(jnp.sum(factor[:, None] * group_gain, 0))
    clipped_shift = lax.optimization_barrier(jnp.sum(factor[:, None] * group_shift, 0))
    return (to_stored(outputs.reshape(IMAGES, S, D)), to_stored(grad_inputs.reshape(IMAGES, S, D)), group_norms, running['g1'], running['s1'], running['tw1'], running['tb1'], running['tw2'], running['tb2'], clipped_gain, clipped_shift, running['cw1'], running['cb1'], running['cw2'], running['cb2'])
```

```python
import functools
import math

import jax
import jax.numpy as jnp
from jax import lax
from jax.experimental import pallas as pl
from jax.experimental.pallas import tpu as pltpu
from jax.sharding import PartitionSpec as P

MESH = pl.DeviceIdType.MESH


def place():
    dp = lax.axis_index("dp"); t = lax.axis_index("tp")
    c = dp % 2; x = (dp // 2) % 2; y = dp // 4
    def at(yy, xx, cc): return (yy * 2 + xx) * 2 + cc
    return dp, t, dict(S=at(y, x, 1 - c), X=at(y, 1 - x, c), Y=at(1 - y, x, c), D=at(1 - y, 1 - x, c)), (y, x, c)

def others(t):
    first = jnp.where(t == 0, 1, jnp.where(t == 1, 0, jnp.where(t == 2, 3, 2)))
    second = jnp.where(t == 0, 2, jnp.where(t == 1, 2, 1))
    third = jnp.where(t < 2, 3, 0)
    return [first, second, third]

def meet(devices):
    barrier = pltpu.get_barrier_semaphore()
    for device in devices:
        pl.semaphore_signal(barrier, inc=1, device_id=device, device_id_type=MESH)
    pl.semaphore_wait(barrier, len(devices))

def gather_kernel(shard, out, send_sem, recv_sem, local_sem):
    dp, t, near, (y, x, c) = place()
    line = others(t)
    order = [t] + line
    meet([(near["S"], t), (near["X"], t), (near["Y"], t)] + [(dp, p) for p in line])
    started = []
    def send(src, owner, tt, device):
        k = len(started)
        copy = pltpu.make_async_remote_copy(src_ref=src, dst_ref=out.at[:, tt, owner], send_sem=send_sem.at[k],
            recv_sem=recv_sem.at[owner, tt], device_id=device, device_id_type=MESH)
        copy.start(); started.append(copy)
    def arrived(owner, tt):
        ref = out.at[:, tt, owner]
        pltpu.make_async_remote_copy(src_ref=ref, dst_ref=ref, send_sem=send_sem.at[0], recv_sem=recv_sem.at[owner, tt],
            device_id=(dp, t), device_id_type=MESH).wait_recv()
    own = pltpu.make_async_copy(shard, out.at[:, t, dp], local_sem); own.start()
    for p in line: send(shard, dp, t, (dp, p))
    def column(k):
        tt = order[k]
        if k: arrived(dp, tt)
        src = shard if k == 0 else out.at[:, tt, dp]
        send(src, dp, tt, (near["X"], t)); send(src, dp, tt, (near["Y"], t)); send(src, dp, tt, (near["S"], t))
    def neighbours(k):
        tt = order[k]
        first, second = ("X", "Y") if k % 2 == 0 else ("Y", "X")
        arrived(near[first], tt); src = out.at[:, tt, near[first]]
        send(src, near[first], tt, (near[second], t)); send(src, near[first], tt, (near["S"], t))
        arrived(near[second], tt); send(out.at[:, tt, near[second]], near[second], tt, (near["S"], t))
    def diagonal(k):
        tt = order[k]; arrived(near["D"], tt); send(out.at[:, tt, near["D"]], near["D"], tt, (near["S"], t))
    column(0); column(1); neighbours(0); column(2); neighbours(1); diagonal(0); column(3); neighbours(2); diagonal(1)
    neighbours(3); diagonal(2); diagonal(3)
    def at(yy, xx, cc): return (yy * 2 + xx) * 2 + cc
    for k in range(4):
        for yy, xx in ((y, x), (y, 1 - x), (1 - y, x), (1 - y, 1 - x)):
            arrived(at(yy, xx, 1 - c), order[k])
    own.wait()
    for copy in started: copy.wait_send()

def gather_weights(shard, cid=1):
    two, rows, cols = shard.shape
    return pl.pallas_call(gather_kernel,
        out_shape=jax.ShapeDtypeStruct((two, 4, 8, rows, cols), shard.dtype),
        in_specs=[pl.BlockSpec(memory_space=pl.ANY)], out_specs=pl.BlockSpec(memory_space=pl.ANY),
        scratch_shapes=[pltpu.SemaphoreType.DMA((31,)), pltpu.SemaphoreType.DMA((8, 4)), pltpu.SemaphoreType.DMA],
        compiler_params=pltpu.CompilerParams(collective_id=cid, has_side_effects=True))(shard)


def scatter_kernel(g, out, sib, acc, first, second, final, zbuf, sib_sem, sib_recv, a_send, a_recv, z_send, z_recv):
    dp, t, near, (y, x, c) = place()
    line = others(t)
    order = [line[2], line[1], line[0], t]
    meet([(near["S"], t), (near["X"], t), (near["Y"], t)] + [(dp, p) for p in line])
    def at(yy, xx, cc): return (yy * 2 + xx) * 2 + cc
    chips = {"O": (y, x), "X": (y, 1 - x), "Y": (1 - y, x), "D": (1 - y, 1 - x)}
    slot = {"O": 0, "X": 1, "Y": 2, "D": 3}
    started = []
    def remote(src, dst, ss, rs, device):
        return pltpu.make_async_remote_copy(src_ref=src, dst_ref=dst, send_sem=ss, recv_sem=rs, device_id=device, device_id_type=MESH)
    def go(copy):
        copy.start(); started.append(copy)
    for k in range(4):
        for name in "DXYO":
            n = slot[name]
            go(remote(g.at[:, order[k], at(*chips[name], 1 - c)], sib.at[k, n], sib_sem.at[k, n], sib_recv.at[k, n], (near["S"], t)))
    f32 = jnp.float32
    def chip_sum(k, name):
        n = slot[name]
        remote(sib.at[k, n], sib.at[k, n], sib_sem.at[k, n], sib_recv.at[k, n], (near["S"], t)).wait_recv()
        acc[k, n] = (g[:, order[k], at(*chips[name], c)].astype(f32) + sib[k, n].astype(f32)).astype(acc.dtype)
    def ways(k):
        return ("X", "Y") if k % 2 == 0 else ("Y", "X")
    def stage_one(k):
        f, s = ways(k)
        chip_sum(k, "D")
        go(remote(acc.at[k, 3], first.at[k], a_send.at[k, 0], a_recv.at[k, 0], (near[s], t)))
        chip_sum(k, s)
        go(remote(acc.at[k, slot[s]], second.at[k], a_send.at[k, 1], a_recv.at[k, 1], (near[s], t)))
    def stage_two(k):
        f, s = ways(k)
        chip_sum(k, f)
        remote(first.at[k], first.at[k], a_send.at[k, 0], a_recv.at[k, 0], (near[s], t)).wait_recv()
        n = slot[f]
        acc[k, n] = (acc[k, n].astype(f32) + first[k].astype(f32)).astype(acc.dtype)
        go(remote(acc.at[k, n], final.at[k], a_send.at[k, 2], a_recv.at[k, 2], (near[f], t)))
    def stage_three(k):
        f, s = ways(k)
        chip_sum(k, "O")
        remote(second.at[k], second.at[k], a_send.at[k, 1], a_recv.at[k, 1], (near[s], t)).wait_recv()
        remote(final.at[k], final.at[k], a_send.at[k, 2], a_recv.at[k, 2], (near[f], t)).wait_recv()
        total = acc[k, 0].astype(f32) + second[k].astype(f32) + final[k].astype(f32)
        if k < 3:
            acc[k, 0] = total.astype(acc.dtype)
            go(remote(acc.at[k, 0], zbuf.at[t], z_send.at[k], z_recv.at[t], (dp, order[k])))
        else:
            out[...] = total
    stage_one(0); stage_one(1)
    stage_two(0); stage_one(2)
    stage_two(1); stage_one(3)
    stage_three(0); stage_two(2)
    stage_three(1); stage_two(3)
    stage_three(2); stage_three(3)
    for p in line:
        remote(zbuf.at[p], zbuf.at[p], z_send.at[0], z_recv.at[p], (dp, t)).wait_recv()
        out[...] += zbuf[p].astype(f32)
    for copy in started: copy.wait_send()

def scatter_grads(g, cid=2):
    two, tp, dpn, rows, cols = g.shape
    piece = (two, rows, cols)
    bf = jnp.bfloat16
    return pl.pallas_call(scatter_kernel,
        out_shape=jax.ShapeDtypeStruct(piece, jnp.float32),
        in_specs=[pl.BlockSpec(memory_space=pltpu.VMEM)], out_specs=pl.BlockSpec(memory_space=pltpu.VMEM),
        scratch_shapes=[pltpu.VMEM((4, 4) + piece, bf), pltpu.VMEM((4, 4) + piece, bf), pltpu.VMEM((4,) + piece, bf), pltpu.VMEM((4,) + piece, bf),
            pltpu.VMEM((4,) + piece, bf), pltpu.VMEM((4,) + piece, bf),
            pltpu.SemaphoreType.DMA((4, 4)), pltpu.SemaphoreType.DMA((4, 4)), pltpu.SemaphoreType.DMA((4, 3)), pltpu.SemaphoreType.DMA((4, 3)),
            pltpu.SemaphoreType.DMA((4,)), pltpu.SemaphoreType.DMA((4,))],
        compiler_params=pltpu.CompilerParams(collective_id=cid, has_side_effects=True, vmem_limit_bytes=48 << 20))(g)


def total_kernel(buf, out, sib, half, cbuf, zbuf, p_send, p_recv, c_send, c_recv, z_send, z_recv, o_send, o_recv, s_send, s_recv):
    dp, t, near, (y, x, c) = place()
    line = others(t)
    meet([(near["S"], t), (near["X"], t), (near["Y"], t), (near["D"], t)] + [(dp, p) for p in line])
    chip = dp // 2
    far = [("X", near["X"] // 2), ("Y", near["Y"] // 2), ("D", near["D"] // 2)]
    started = []
    def remote(src, dst, ss, rs, device):
        return pltpu.make_async_remote_copy(src_ref=src, dst_ref=dst, send_sem=ss, recv_sem=rs, device_id=device, device_id_type=MESH)
    def go(copy):
        copy.start(); started.append(copy)
    go(remote(buf.at[1 - c], sib, p_send, p_recv, (near["S"], t)))
    remote(sib, sib, p_send, p_recv, (near["S"], t)).wait_recv()
    half[...] = buf[c] + sib[...]
    for n, (name, q) in enumerate(far):
        go(remote(half.at[q], cbuf.at[n], c_send.at[n], c_recv.at[n], (near[name], t)))
    total = half[chip]
    for n in range(3):
        remote(cbuf.at[n], cbuf.at[n], c_send.at[n], c_recv.at[n], (near["S"], t)).wait_recv()
        total = total + cbuf[n]
    zbuf[t] = total
    for n, p in enumerate(line):
        go(remote(zbuf.at[t], zbuf.at[t], z_send.at[n], z_recv.at[t], (dp, p)))
    for p in line:
        remote(zbuf.at[p], zbuf.at[p], z_send.at[0], z_recv.at[p], (dp, t)).wait_recv()
    out[c, chip] = ((zbuf[0] + zbuf[1]) + zbuf[2]) + zbuf[3]
    for n, (name, q) in enumerate(far):
        go(remote(out.at[c, chip], out.at[c, chip], o_send.at[n], o_recv.at[chip], (near[name], t)))
    go(remote(out.at[c, chip], out.at[c, chip], s_send.at[3], s_recv.at[chip], (near["S"], t)))
    for n, (name, q) in enumerate(far):
        remote(out.at[c, q], out.at[c, q], o_send.at[0], o_recv.at[q], (dp, t)).wait_recv()
        go(remote(out.at[c, q], out.at[c, q], s_send.at[n], s_recv.at[q], (near["S"], t)))
    for q in range(4):
        remote(out.at[1 - c, q], out.at[1 - c, q], s_send.at[0], s_recv.at[q], (dp, t)).wait_recv()
    for copy in started: copy.wait_send()

def total_all(buf, cid=3):
    rows, cols = buf.shape
    b = buf.reshape(2, 4, rows // 8, cols)
    piece = (rows // 8, cols)
    dma = pltpu.SemaphoreType.DMA
    out = pl.pallas_call(total_kernel,
        out_shape=jax.ShapeDtypeStruct(b.shape, b.dtype),
        in_specs=[pl.BlockSpec(memory_space=pltpu.VMEM)], out_specs=pl.BlockSpec(memory_space=pltpu.VMEM),
        scratch_shapes=[pltpu.VMEM((4,) + piece, b.dtype), pltpu.VMEM((4,) + piece, b.dtype), pltpu.VMEM((3,) + piece, b.dtype), pltpu.VMEM((4,) + piece, b.dtype),
            dma, dma, dma((3,)), dma((3,)), dma((3,)), dma((4,)), dma((3,)), dma((4,)), dma((4,)), dma((4,))],
        compiler_params=pltpu.CompilerParams(collective_id=cid, has_side_effects=True, vmem_limit_bytes=16 << 20))(b)
    return out.reshape(rows, cols)


S = 196
GROUPS = 64
epsilon = 1e-06
highest = lax.Precision.HIGHEST


def normalised(values):
    average = jnp.mean(values, -1, keepdims=True)
    inverse = lax.rsqrt(jnp.mean(values * values, -1, keepdims=True) - average * average + epsilon)
    return (values - average) * inverse, inverse


def norm_back(grad_hat, normed, inverse):
    return inverse * (
        grad_hat - jnp.mean(grad_hat, -1, keepdims=True) - normed * jnp.mean(grad_hat * normed, -1, keepdims=True)
    )


def per_device(block_in, ln1_gain, ln1_shift, tok_w1, tok_b1, tok_w2, tok_b2, ln2_gain, ln2_shift,
               ch_w1, ch_b1, ch_w2, ch_b2, group_ids, out_grad):
    f32 = jnp.float32
    bf16 = jnp.bfloat16
    tp = lax.axis_size("tp")
    dp = lax.axis_size("dp")
    held = block_in.shape[0]
    images = held // tp
    width = block_in.shape[2] // S
    full = width * tp
    t = lax.axis_index("tp")
    kernels = dp == 8 and tp == 4

    def whole_images(stored):
        got = lax.all_to_all(stored.reshape(tp, images, S * width), "tp", 0, 0, tiled=True)
        return got.reshape(tp, images, S, width).transpose(1, 2, 0, 3).reshape(images, S, full)

    def stored(values):
        parts = values.reshape(images, S, tp, width).transpose(2, 0, 1, 3).reshape(tp, images, S * width)
        return lax.all_to_all(parts, "tp", 0, 0, tiled=True).reshape(held, 1, S * width)

    rows = ch_w1.shape[0]
    shard = jnp.stack([ch_w1.astype(bf16), ch_w2.T.astype(bf16)])
    if kernels:
        gathered = gather_weights(shard)
    else:
        gathered = lax.all_gather(lax.all_gather(shard, "tp", axis=1), "dp", axis=2)
    gathered = gathered.reshape(2, tp, dp * rows, shard.shape[2])
    norms = lax.all_gather(jnp.stack([ln1_gain, ln1_shift, ln2_gain, ln2_shift]), "tp", axis=1, tiled=True)
    x = whole_images(block_in).astype(f32)
    dz_low = whole_images(out_grad)
    token_w1 = tok_w1.astype(bf16)
    token_w2 = tok_w2.astype(bf16)
    xhat, inv_x = normalised(x)
    mixed = (xhat * norms[0] + norms[1]).astype(bf16)
    pre = jnp.einsum("nsc,sk->nkc", mixed, token_w1, preferred_element_type=f32) + tok_b1[:, None]
    hidden, hidden_back = jax.vjp(jax.nn.gelu, pre)
    hidden = hidden.astype(bf16)
    u = x + jnp.einsum("nkc,ks->nsc", hidden, token_w2, preferred_element_type=f32) + tok_b2[:, None]
    uhat, inv_u = normalised(u)
    count = images * S
    hn = (uhat * norms[2] + norms[3]).astype(bf16).reshape(count, full)
    dz = dz_low.reshape(count, full)
    z = jnp.zeros((count, full), f32)
    dhn = jnp.zeros((count, full), f32)
    grads1, grads2, bias = [], [], []
    inner = shard.shape[2]
    for j in range(tp):
        q = jnp.dot(hn, gathered[0, j], preferred_element_type=f32) + ch_b1[j * inner : (j + 1) * inner]
        g, g_back = jax.vjp(jax.nn.gelu, q)
        g = g.astype(bf16)
        z = z + jnp.einsum("rh,ch->rc", g, gathered[1, j], preferred_element_type=f32)
        dg = jnp.dot(dz, gathered[1, j], preferred_element_type=f32)
        dq = g_back(dg)[0].astype(bf16)
        grads2.append(jnp.einsum("rc,rh->ch", dz, g, preferred_element_type=f32).astype(bf16))
        grads1.append(jnp.einsum("rc,rh->ch", hn, dq, preferred_element_type=f32).astype(bf16))
        bias.append(jnp.sum(dq.astype(f32), 0))
        dhn = dhn + jnp.einsum("rh,ch->rc", dq, gathered[0, j], preferred_element_type=f32)
    z = (z + ch_b2).astype(bf16).astype(f32).reshape(u.shape)
    block_out = stored((u + z).astype(bf16))
    dhn = dhn.reshape(u.shape)
    dz32 = dz_low.astype(f32)
    image_gain = jnp.sum(dhn * uhat, 1)
    image_shift = jnp.sum(dhn, 1)
    du = dz32 + norm_back(dhn * norms[2], uhat, inv_u)
    dp_low = du.astype(bf16)
    dh = jnp.einsum("nsc,ks->nkc", dp_low, token_w2, preferred_element_type=f32)
    d_tok_w2 = jnp.einsum("nkc,nsc->ks", hidden, dp_low, preferred_element_type=f32)
    d_tok_b2 = jnp.sum(dp_low.astype(f32), (0, 2))
    dpre = hidden_back(dh)[0].astype(bf16)
    d_tok_w1 = jnp.einsum("nsc,nkc->sk", mixed, dpre, preferred_element_type=f32)
    d_tok_b1 = jnp.sum(dpre.astype(f32), (0, 2))
    da = jnp.einsum("nkc,sk->nsc", dpre, token_w1, preferred_element_type=f32)
    d_gain1 = jnp.sum(da * xhat, (0, 1))
    d_shift1 = jnp.sum(da, (0, 1))
    dx = stored((du + norm_back(da * norms[0], xhat, inv_x)).astype(bf16))

    gradient = jnp.stack([jnp.stack(grads1), jnp.stack(grads2)]).reshape(2, tp, dp, rows, inner)
    if kernels:
        owned = scatter_grads(gradient)
    else:
        owned = lax.psum_scatter(lax.psum_scatter(gradient, "tp", scatter_dimension=1, tiled=True).astype(bf16), "dp", scatter_dimension=2, tiled=True)
        owned = owned.astype(f32).reshape(2, rows, inner)

    ids = lax.dynamic_slice_in_dim(group_ids, t * images, images)
    member = (ids[:, None] == jnp.arange(GROUPS)[None, :]).astype(f32)
    groups = jnp.dot(member.T, jnp.concatenate([image_gain, image_shift], 1), precision=highest)
    flat = [d_tok_w1, d_tok_w2, jnp.stack(bias), jnp.sum(dz32, (0, 1)), d_gain1, d_shift1, d_tok_b1, d_tok_b2, groups]
    sizes = [v.size for v in flat]
    need = sum(sizes)
    unit = 64 * full
    padded = -(-need // unit) * unit
    packed = jnp.concatenate([v.reshape(-1) for v in flat] + [jnp.zeros((padded - need,), f32)]).reshape(-1, full)
    if kernels:
        total = total_all(packed)
    else:
        total = lax.psum(packed, ("dp", "tp"))
    total = total.reshape(-1)
    pieces, start = [], 0
    for v in flat:
        pieces.append(total[start : start + v.size].reshape(v.shape))
        start += v.size
    tw1, tw2, cb1, cb2, g1, s1, tb1, tb2, gg = pieces
    gg = gg.reshape(GROUPS, 2, full)
    group_norms = jnp.sqrt(jnp.sum(gg * gg, (1, 2)))
    bound = 2.0 * math.sqrt(held * dp * S * full / GROUPS)
    factor = bound / jnp.maximum(group_norms, bound)
    clipped = jnp.sum(factor[:, None, None] * gg, 0)

    def mine(v):
        return lax.dynamic_slice_in_dim(v, t * width, width)

    return (block_out, dx, group_norms, mine(g1), mine(s1), tw1, tb1, tw2, tb2, mine(clipped[0]), mine(clipped[1]),
            owned[0], cb1.reshape(-1), owned[1].T, cb2)


def solution(mesh):
    stored, own, copied = P("dp", "tp", None), P("tp"), P()
    in_specs = (stored, own, own, copied, copied, copied, copied, own, own, P("dp", "tp"), copied, P("tp", "dp"), copied, P("dp"), stored)
    out_specs = (stored, stored, copied, own, own, copied, copied, copied, copied, own, own, P("dp", "tp"), copied, P("tp", "dp"), copied)
    return jax.shard_map(per_device, mesh=mesh, in_specs=in_specs, out_specs=out_specs, check_vma=False)
```

```python
import functools
import math

import jax
import jax.numpy as jnp
from jax import lax
from jax.experimental import pallas as pl
from jax.experimental.pallas import tpu as pltpu
from jax.sharding import PartitionSpec as P

MESH = pl.DeviceIdType.MESH


def place():
    dp = lax.axis_index("dp"); t = lax.axis_index("tp")
    c = dp % 2; x = (dp // 2) % 2; y = dp // 4
    def at(yy, xx, cc): return (yy * 2 + xx) * 2 + cc
    return dp, t, dict(S=at(y, x, 1 - c), X=at(y, 1 - x, c), Y=at(1 - y, x, c), D=at(1 - y, 1 - x, c)), (y, x, c)

def others(t):
    first = jnp.where(t == 0, 1, jnp.where(t == 1, 0, jnp.where(t == 2, 3, 2)))
    second = jnp.where(t == 0, 2, jnp.where(t == 1, 2, 1))
    third = jnp.where(t < 2, 3, 0)
    return [first, second, third]

def meet(devices):
    barrier = pltpu.get_barrier_semaphore()
    for device in devices:
        pl.semaphore_signal(barrier, inc=1, device_id=device, device_id_type=MESH)
    pl.semaphore_wait(barrier, len(devices))

def gather_kernel(shard, out, send_sem, recv_sem, local_sem):
    dp, t, near, (y, x, c) = place()
    line = others(t)
    order = [t] + line
    meet([(near["S"], t), (near["X"], t), (near["Y"], t)] + [(dp, p) for p in line])
    started = []
    def send(src, owner, tt, device):
        k = len(started)
        copy = pltpu.make_async_remote_copy(src_ref=src, dst_ref=out.at[:, tt, owner], send_sem=send_sem.at[k],
            recv_sem=recv_sem.at[owner, tt], device_id=device, device_id_type=MESH)
        copy.start(); started.append(copy)
    def arrived(owner, tt):
        ref = out.at[:, tt, owner]
        pltpu.make_async_remote_copy(src_ref=ref, dst_ref=ref, send_sem=send_sem.at[0], recv_sem=recv_sem.at[owner, tt],
            device_id=(dp, t), device_id_type=MESH).wait_recv()
    own = pltpu.make_async_copy(shard, out.at[:, t, dp], local_sem); own.start()
    for p in line: send(shard, dp, t, (dp, p))
    def column(k):
        tt = order[k]
        if k: arrived(dp, tt)
        src = shard if k == 0 else out.at[:, tt, dp]
        send(src, dp, tt, (near["X"], t)); send(src, dp, tt, (near["Y"], t)); send(src, dp, tt, (near["S"], t))
    def neighbours(k):
        tt = order[k]
        first, second = ("X", "Y") if k % 2 == 0 else ("Y", "X")
        arrived(near[first], tt); src = out.at[:, tt, near[first]]
        send(src, near[first], tt, (near[second], t)); send(src, near[first], tt, (near["S"], t))
        arrived(near[second], tt); send(out.at[:, tt, near[second]], near[second], tt, (near["S"], t))
    def diagonal(k):
        tt = order[k]; arrived(near["D"], tt); send(out.at[:, tt, near["D"]], near["D"], tt, (near["S"], t))
    column(0); column(1); neighbours(0); column(2); neighbours(1); diagonal(0); column(3); neighbours(2); diagonal(1)
    neighbours(3); diagonal(2); diagonal(3)
    def at(yy, xx, cc): return (yy * 2 + xx) * 2 + cc
    for k in range(4):
        for yy, xx in ((y, x), (y, 1 - x), (1 - y, x), (1 - y, 1 - x)):
            arrived(at(yy, xx, 1 - c), order[k])
    own.wait()
    for copy in started: copy.wait_send()

def gather_weights(shard, cid=1):
    two, rows, cols = shard.shape
    return pl.pallas_call(gather_kernel,
        out_shape=jax.ShapeDtypeStruct((two, 4, 8, rows, cols), shard.dtype),
        in_specs=[pl.BlockSpec(memory_space=pl.ANY)], out_specs=pl.BlockSpec(memory_space=pl.ANY),
        scratch_shapes=[pltpu.SemaphoreType.DMA((31,)), pltpu.SemaphoreType.DMA((8, 4)), pltpu.SemaphoreType.DMA],
        compiler_params=pltpu.CompilerParams(collective_id=cid, has_side_effects=True))(shard)


def scatter_kernel(g, out, sib, acc, first, second, final, zbuf, sib_sem, sib_recv, a_send, a_recv, z_send, z_recv):
    dp, t, near, (y, x, c) = place()
    line = others(t)
    order = [line[2], line[1], line[0], t]
    meet([(near["S"], t), (near["X"], t), (near["Y"], t)] + [(dp, p) for p in line])
    def at(yy, xx, cc): return (yy * 2 + xx) * 2 + cc
    chips = {"O": (y, x), "X": (y, 1 - x), "Y": (1 - y, x), "D": (1 - y, 1 - x)}
    slot = {"O": 0, "X": 1, "Y": 2, "D": 3}
    started = []
    def remote(src, dst, ss, rs, device):
        return pltpu.make_async_remote_copy(src_ref=src, dst_ref=dst, send_sem=ss, recv_sem=rs, device_id=device, device_id_type=MESH)
    def go(copy):
        copy.start(); started.append(copy)
    for k in range(4):
        for name in "DXYO":
            n = slot[name]
            go(remote(g.at[:, order[k], at(*chips[name], 1 - c)], sib.at[k, n], sib_sem.at[k, n], sib_recv.at[k, n], (near["S"], t)))
    f32 = jnp.float32
    def chip_sum(k, name):
        n = slot[name]
        remote(sib.at[k, n], sib.at[k, n], sib_sem.at[k, n], sib_recv.at[k, n], (near["S"], t)).wait_recv()
        acc[k, n] = (g[:, order[k], at(*chips[name], c)].astype(f32) + sib[k, n].astype(f32)).astype(acc.dtype)
    def ways(k):
        return ("X", "Y") if k % 2 == 0 else ("Y", "X")
    def stage_one(k):
        f, s = ways(k)
        chip_sum(k, "D")
        go(remote(acc.at[k, 3], first.at[k], a_send.at[k, 0], a_recv.at[k, 0], (near[s], t)))
        chip_sum(k, s)
        go(remote(acc.at[k, slot[s]], second.at[k], a_send.at[k, 1], a_recv.at[k, 1], (near[s], t)))
    def stage_two(k):
        f, s = ways(k)
        chip_sum(k, f)
        remote(first.at[k], first.at[k], a_send.at[k, 0], a_recv.at[k, 0], (near[s], t)).wait_recv()
        n = slot[f]
        acc[k, n] = (acc[k, n].astype(f32) + first[k].astype(f32)).astype(acc.dtype)
        go(remote(acc.at[k, n], final.at[k], a_send.at[k, 2], a_recv.at[k, 2], (near[f], t)))
    def stage_three(k):
        f, s = ways(k)
        chip_sum(k, "O")
        remote(second.at[k], second.at[k], a_send.at[k, 1], a_recv.at[k, 1], (near[s], t)).wait_recv()
        remote(final.at[k], final.at[k], a_send.at[k, 2], a_recv.at[k, 2], (near[f], t)).wait_recv()
        total = acc[k, 0].astype(f32) + second[k].astype(f32) + final[k].astype(f32)
        if k < 3:
            acc[k, 0] = total.astype(acc.dtype)
            go(remote(acc.at[k, 0], zbuf.at[t], z_send.at[k], z_recv.at[t], (dp, order[k])))
        else:
            out[...] = total
    stage_one(0); stage_one(1)
    stage_two(0); stage_one(2)
    stage_two(1); stage_one(3)
    stage_three(0); stage_two(2)
    stage_three(1); stage_two(3)
    stage_three(2); stage_three(3)
    for p in line:
        remote(zbuf.at[p], zbuf.at[p], z_send.at[0], z_recv.at[p], (dp, t)).wait_recv()
        out[...] += zbuf[p].astype(f32)
    for copy in started: copy.wait_send()

def scatter_grads(g, cid=2):
    two, tp, dpn, rows, cols = g.shape
    piece = (two, rows, cols)
    bf = jnp.bfloat16
    return pl.pallas_call(scatter_kernel,
        out_shape=jax.ShapeDtypeStruct(piece, jnp.float32),
        in_specs=[pl.BlockSpec(memory_space=pltpu.VMEM)], out_specs=pl.BlockSpec(memory_space=pltpu.VMEM),
        scratch_shapes=[pltpu.VMEM((4, 4) + piece, bf), pltpu.VMEM((4, 4) + piece, bf), pltpu.VMEM((4,) + piece, bf), pltpu.VMEM((4,) + piece, bf),
            pltpu.VMEM((4,) + piece, bf), pltpu.VMEM((4,) + piece, bf),
            pltpu.SemaphoreType.DMA((4, 4)), pltpu.SemaphoreType.DMA((4, 4)), pltpu.SemaphoreType.DMA((4, 3)), pltpu.SemaphoreType.DMA((4, 3)),
            pltpu.SemaphoreType.DMA((4,)), pltpu.SemaphoreType.DMA((4,))],
        compiler_params=pltpu.CompilerParams(collective_id=cid, has_side_effects=True, vmem_limit_bytes=48 << 20))(g)


def total_kernel(buf, out, sib, half, cbuf, zbuf, p_send, p_recv, c_send, c_recv, z_send, z_recv, o_send, o_recv, s_send, s_recv):
    dp, t, near, (y, x, c) = place()
    line = others(t)
    meet([(near["S"], t), (near["X"], t), (near["Y"], t), (near["D"], t)] + [(dp, p) for p in line])
    chip = dp // 2
    far = [("X", near["X"] // 2), ("Y", near["Y"] // 2), ("D", near["D"] // 2)]
    started = []
    def remote(src, dst, ss, rs, device):
        return pltpu.make_async_remote_copy(src_ref=src, dst_ref=dst, send_sem=ss, recv_sem=rs, device_id=device, device_id_type=MESH)
    def go(copy):
        copy.start(); started.append(copy)
    go(remote(buf.at[1 - c], sib, p_send, p_recv, (near["S"], t)))
    remote(sib, sib, p_send, p_recv, (near["S"], t)).wait_recv()
    half[...] = buf[c] + sib[...]
    for n, (name, q) in enumerate(far):
        go(remote(half.at[q], cbuf.at[n], c_send.at[n], c_recv.at[n], (near[name], t)))
    total = half[chip]
    for n in range(3):
        remote(cbuf.at[n], cbuf.at[n], c_send.at[n], c_recv.at[n], (near["S"], t)).wait_recv()
        total = total + cbuf[n]
    zbuf[t] = total
    for n, p in enumerate(line):
        go(remote(zbuf.at[t], zbuf.at[t], z_send.at[n], z_recv.at[t], (dp, p)))
    for p in line:
        remote(zbuf.at[p], zbuf.at[p], z_send.at[0], z_recv.at[p], (dp, t)).wait_recv()
    out[c, chip] = ((zbuf[0] + zbuf[1]) + zbuf[2]) + zbuf[3]
    for n, (name, q) in enumerate(far):
        go(remote(out.at[c, chip], out.at[c, chip], o_send.at[n], o_recv.at[chip], (near[name], t)))
    go(remote(out.at[c, chip], out.at[c, chip], s_send.at[3], s_recv.at[chip], (near["S"], t)))
    for n, (name, q) in enumerate(far):
        remote(out.at[c, q], out.at[c, q], o_send.at[0], o_recv.at[q], (dp, t)).wait_recv()
        go(remote(out.at[c, q], out.at[c, q], s_send.at[n], s_recv.at[q], (near["S"], t)))
    for q in range(4):
        remote(out.at[1 - c, q], out.at[1 - c, q], s_send.at[0], s_recv.at[q], (dp, t)).wait_recv()
    for copy in started: copy.wait_send()

def total_all(buf, cid=3):
    rows, cols = buf.shape
    b = buf.reshape(2, 4, rows // 8, cols)
    piece = (rows // 8, cols)
    dma = pltpu.SemaphoreType.DMA
    out = pl.pallas_call(total_kernel,
        out_shape=jax.ShapeDtypeStruct(b.shape, b.dtype),
        in_specs=[pl.BlockSpec(memory_space=pltpu.VMEM)], out_specs=pl.BlockSpec(memory_space=pltpu.VMEM),
        scratch_shapes=[pltpu.VMEM((4,) + piece, b.dtype), pltpu.VMEM((4,) + piece, b.dtype), pltpu.VMEM((3,) + piece, b.dtype), pltpu.VMEM((4,) + piece, b.dtype),
            dma, dma, dma((3,)), dma((3,)), dma((3,)), dma((4,)), dma((3,)), dma((4,)), dma((4,)), dma((4,))],
        compiler_params=pltpu.CompilerParams(collective_id=cid, has_side_effects=True, vmem_limit_bytes=16 << 20))(b)
    return out.reshape(rows, cols)


F32 = jnp.float32
BF16 = jnp.bfloat16
HALF = 98
GAP = 104
ROWS = 208
LOW = math.sqrt(2.0 / math.pi)
CUBE = 0.044715


def gelu_pair(v):
    square = v * v
    up = 0.5 * jnp.tanh(v * (LOW + (LOW * CUBE) * square)) + 0.5
    value = v * up
    slope = up + value * (1.0 - up) * (2.0 * LOW + (6.0 * LOW * CUBE) * square)
    return value, slope


def turn(v):
    return pltpu.roll(v, 64, 1)


def join_groups(flat, image, store):
    low = lax.broadcasted_iota(jnp.int32, (HALF, 128), 1) < 64
    for p in range(2):
        a = [flat[2 * p, pl.ds(image * HALF, HALF), 128 * j : 128 * j + 128] for j in range(3)]
        b = [flat[2 * p + 1, pl.ds(image * HALF, HALF), 128 * j : 128 * j + 128] for j in range(3)]
        a1, a2, b0, b1 = turn(a[1]), turn(a[2]), turn(b[0]), turn(b[1])
        even = [a[0], jnp.where(low, a[1], b0), jnp.where(low, b0, b1)]
        odd = [jnp.where(low, a1, a2), jnp.where(low, a2, b[1]), b[2]]
        for j in range(3):
            store(0, 384 * p + 128 * j, even[j])
            store(GAP, 384 * p + 128 * j, odd[j])


def split_groups(load, flat, image):
    low = lax.broadcasted_iota(jnp.int32, (HALF, 128), 1) < 64
    for p in range(2):
        e = [load(0, 384 * p + 128 * j) for j in range(3)]
        o = [load(GAP, 384 * p + 128 * j) for j in range(3)]
        e1, e2, o0, o1 = turn(e[1]), turn(e[2]), turn(o[0]), turn(o[1])
        a = [e[0], jnp.where(low, e[1], o0), jnp.where(low, o0, o1)]
        b = [jnp.where(low, e1, e2), jnp.where(low, e2, o[1]), o[2]]
        for j in range(3):
            flat[2 * p, pl.ds(image * HALF, HALF), 128 * j : 128 * j + 128] = a[j]
            flat[2 * p + 1, pl.ds(image * HALF, HALF), 128 * j : 128 * j + 128] = b[j]


def hat(v):
    average = jnp.mean(v, -1, keepdims=True)
    inverse = lax.rsqrt(jnp.mean(v * v, -1, keepdims=True) - average * average + 1e-06)
    return (v - average) * inverse, inverse


def dot(a, b):
    return jnp.dot(a, b, preferred_element_type=F32)


def dot_nt(a, b):
    return lax.dot_general(a, b, (((1,), (1,)), ((), ())), preferred_element_type=F32)


def forward_kernel(shard, xs, ds, lnp, w1t, w2t, b1, b2, cb1, cb2,
                   w_out, g_out, s_out, u_out, hn_out, x_out, dz_out, h_out, t_out, o_out, ln_out,
                   wv, xr, dr, flat, x, u, hn, g, s, h, ts, zs, op, dz, lr,
                   send_sem, recv_sem, x_send, x_recv, d_send, d_recv, l_send, l_recv, own_sem, keep_sem):
    dp, t, near, (y, xx, c) = place()
    line = others(t)
    order = [t] + line

    def at(yy, xxx, cc):
        return (yy * 2 + xxx) * 2 + cc

    started, kept = [], []

    def remote(src, dst, ss, rs, device):
        return pltpu.make_async_remote_copy(src_ref=src, dst_ref=dst, send_sem=ss, recv_sem=rs, device_id=device, device_id_type=MESH)

    def go(copy):
        copy.start()
        started.append(copy)

    def keep(src, dst):
        copy = pltpu.make_async_copy(src, dst, keep_sem.at[len(kept)])
        copy.start()
        kept.append(copy)

    meet([(near["S"], t), (near["X"], t), (near["Y"], t)] + [(dp, p) for p in line])
    sends = [0]

    def send(src, owner, tt, device):
        go(remote(src, wv.at[:, tt, owner], send_sem.at[sends[0]], recv_sem.at[owner, tt], device))
        sends[0] += 1

    def arrived(owner, tt):
        ref = wv.at[:, tt, owner]
        remote(ref, ref, send_sem.at[0], recv_sem.at[owner, tt], (dp, t)).wait_recv()

    own_w = pltpu.make_async_copy(shard, wv.at[:, t, dp], own_sem.at[0])
    own_x = pltpu.make_async_copy(xs.at[t], xr.at[t], own_sem.at[1])
    own_d = pltpu.make_async_copy(ds.at[t], dr.at[t], own_sem.at[2])
    own_l = pltpu.make_async_copy(lnp, lr.at[t], own_sem.at[3])
    for copy in (own_w, own_x, own_d, own_l):
        copy.start()
    for p in line:
        send(shard, dp, t, (dp, p))
    for n, p in enumerate(line):
        go(remote(lnp, lr.at[t], l_send.at[n], l_recv.at[t], (dp, p)))

    def column(k):
        tt = order[k]
        if k:
            arrived(dp, tt)
        src = wv.at[:, tt, dp] if k else shard
        for name in "XYS":
            send(src, dp, tt, (near[name], t))

    def neighbours(k):
        tt = order[k]
        first, second = ("X", "Y") if k % 2 == 0 else ("Y", "X")
        arrived(near[first], tt)
        src = wv.at[:, tt, near[first]]
        send(src, near[first], tt, (near[second], t))
        send(src, near[first], tt, (near["S"], t))
        arrived(near[second], tt)
        send(wv.at[:, tt, near[second]], near[second], tt, (near["S"], t))

    def diagonal(k):
        tt = order[k]
        arrived(near["D"], tt)
        send(wv.at[:, tt, near["D"]], near["D"], tt, (near["S"], t))

    column(0)
    column(1)
    neighbours(0)
    for n, p in enumerate(line):
        go(remote(xs.at[p], xr.at[t], x_send.at[n], x_recv.at[t], (dp, p)))
    column(2)
    neighbours(1)
    diagonal(0)
    column(3)
    neighbours(2)
    diagonal(1)
    neighbours(3)
    diagonal(2)
    diagonal(3)

    own_l.wait()
    for p in line:
        remote(lr.at[p], lr.at[p], l_send.at[0], l_recv.at[p], (dp, t)).wait_recv()
    params = (lr[0] + lr[1]) + (lr[2] + lr[3])
    lr[0] = params
    keep(lr.at[0], ln_out)
    zero = jnp.zeros((GAP - HALF, 768), F32)
    for n in range(4):
        for start in (HALF, GAP + HALF):
            x[n, start : start + GAP - HALF, :] = zero
    own_x.wait()
    for p in line:
        remote(xr.at[p], xr.at[p], x_send.at[0], x_recv.at[p], (dp, t)).wait_recv()
    for n, p in enumerate(line):
        go(remote(ds.at[p], dr.at[t], d_send.at[n], d_recv.at[t], (dp, p)))
    for k in range(4):
        flat[k] = xr[k].astype(F32)
    for n in range(4):
        def put(row, lane, v, n=n):
            x[n, row : row + HALF, lane : lane + 128] = v
        join_groups(flat, n, put)
    keep(x, x_out)
    g1, s1, g2, s2 = params[0:1], params[1:2], params[2:3], params[3:4]

    def token(n, carry):
        v = x[n]
        xhat, _ = hat(v)
        a = (xhat * g1 + s1).astype(BF16)
        value, slope = gelu_pair(dot(w1t[...], a) + b1[...])
        low = value.astype(BF16)
        h[n] = low
        ts[n] = slope.astype(BF16)
        r = v + dot(w2t[...], low) + b2[...]
        u[n] = r
        uhat, _ = hat(r)
        hn[n] = (uhat * g2 + s2).astype(BF16)
        return carry

    lax.fori_loop(0, 4, token, 0)
    keep(u, u_out)
    keep(hn, hn_out)
    keep(h, h_out)
    keep(ts, t_out)

    own_w.wait()
    for k in range(4):
        tt = order[k]
        for yy, xxx in ((y, xx), (y, 1 - xx), (1 - y, xx), (1 - y, 1 - xx)):
            arrived(at(yy, xxx, 1 - c), tt)
        keep(wv.at[:, tt], w_out.at[:, tt])

        def block(n, carry, tt=tt, k=k):
            value, slope = gelu_pair(dot(hn[n], wv[0, tt].reshape(768, 768)) + cb1[tt])
            low = value.astype(BF16)
            g[tt, n] = low
            s[tt, n] = slope.astype(BF16)
            part = dot_nt(low, wv[1, tt].reshape(768, 768))
            if k == 0:
                zs[n] = part
            elif k < 3:
                zs[n] += part
            else:
                z = (zs[n] + part + cb2[...]).astype(BF16).astype(F32)
                zs[n] = u[n] + z
            return carry

        lax.fori_loop(0, 4, block, 0)
        keep(g.at[tt], g_out.at[tt])
        keep(s.at[tt], s_out.at[tt])
    for n in range(4):
        split_groups(lambda row, lane, n=n: zs[n, row : row + HALF, lane : lane + 128], flat, n)
    for k in range(4):
        op[k] = flat[k].astype(BF16)
    keep(op, o_out)
    own_d.wait()
    for p in line:
        remote(dr.at[p], dr.at[p], d_send.at[0], d_recv.at[p], (dp, t)).wait_recv()
    for k in range(4):
        flat[k] = dr[k].astype(F32)
    for n in range(4):
        for start in (HALF, GAP + HALF):
            zs[n, start : start + GAP - HALF, :] = zero

        def put_grad(row, lane, v, n=n):
            zs[n, row : row + HALF, lane : lane + 128] = v

        join_groups(flat, n, put_grad)
        dz[n] = zs[n].astype(BF16)
    keep(dz, dz_out)
    for copy in started:
        copy.wait_send()
    for copy in kept:
        copy.wait()


def forward_pass(shard, xs, ds, lnp, w1t, w2t, b1, b2, cb1, cb2):
    any_, vmem = pl.BlockSpec(memory_space=pl.ANY), pl.BlockSpec(memory_space=pltpu.VMEM)
    sds = jax.ShapeDtypeStruct
    dma = pltpu.SemaphoreType.DMA
    wshape = (2, 4, 8, 96, 768)
    act, tok = (4, ROWS, 768), (4, 384, 768)
    packed = (4, 4 * HALF, 384)
    shapes = [(wshape, BF16), ((4,) + act, BF16), ((4,) + act, BF16), (act, F32), (act, BF16), (act, F32), (act, BF16), (tok, BF16), (tok, BF16), (packed, BF16), ((8, 768), F32)]
    V = pltpu.VMEM
    return pl.pallas_call(forward_kernel,
        out_shape=[sds(*v) for v in shapes],
        in_specs=[any_] * 4 + [vmem] * 6, out_specs=[any_] * len(shapes),
        scratch_shapes=[V(wshape, BF16), V(packed, BF16), V(packed, BF16), V(packed, F32), V(act, F32), V(act, F32), V(act, BF16),
            V((4,) + act, BF16), V((4,) + act, BF16), V(tok, BF16), V(tok, BF16), V(act, F32), V(packed, BF16), V(act, BF16), V((4, 8, 768), F32),
            dma((31,)), dma((8, 4)), dma((3,)), dma((4,)), dma((3,)), dma((4,)), dma((3,)), dma((4,)), dma((4,)), dma((24,))],
        compiler_params=pltpu.CompilerParams(collective_id=1, has_side_effects=True, vmem_limit_bytes=60 << 20))(
            shard, xs, ds, lnp, w1t, w2t, b1, b2, cb1, cb2)


def halves(v, axis):
    shape = v.shape
    pairs = v.reshape(shape[:axis] + (HALF, 2) + shape[axis + 1 :])
    pads = [(0, 0)] * v.ndim
    pads[axis] = (0, GAP - HALF)
    parts = [jnp.pad(lax.index_in_dim(pairs, k, axis + 1, keepdims=False), pads) for k in range(2)]
    return jnp.concatenate(parts, axis)


def whole(v, axis):
    parts = [lax.slice_in_dim(v, start, start + HALF, axis=axis) for start in (0, GAP)]
    return jnp.stack(parts, axis + 1).reshape(v.shape[:axis] + (2 * HALF,) + v.shape[axis + 1 :])


S = 196
GROUPS = 64
epsilon = 1e-06
highest = lax.Precision.HIGHEST


def normalised(values):
    average = jnp.mean(values, -1, keepdims=True)
    inverse = lax.rsqrt(jnp.mean(values * values, -1, keepdims=True) - average * average + epsilon)
    return (values - average) * inverse, inverse


def norm_back(grad_hat, normed, inverse):
    return inverse * (
        grad_hat - jnp.mean(grad_hat, -1, keepdims=True) - normed * jnp.mean(grad_hat * normed, -1, keepdims=True)
    )


def general(block_in, ln1_gain, ln1_shift, tok_w1, tok_b1, tok_w2, tok_b2, ln2_gain, ln2_shift,
               ch_w1, ch_b1, ch_w2, ch_b2, group_ids, out_grad):
    f32 = jnp.float32
    bf16 = jnp.bfloat16
    tp = lax.axis_size("tp")
    dp = lax.axis_size("dp")
    held = block_in.shape[0]
    images = held // tp
    width = block_in.shape[2] // S
    full = width * tp
    t = lax.axis_index("tp")

    def whole_images(stored):
        got = lax.all_to_all(stored.reshape(tp, images, S * width), "tp", 0, 0, tiled=True)
        return got.reshape(tp, images, S, width).transpose(1, 2, 0, 3).reshape(images, S, full)

    def stored(values):
        parts = values.reshape(images, S, tp, width).transpose(2, 0, 1, 3).reshape(tp, images, S * width)
        return lax.all_to_all(parts, "tp", 0, 0, tiled=True).reshape(held, 1, S * width)

    rows = ch_w1.shape[0]
    shard = jnp.stack([ch_w1.astype(bf16), ch_w2.T.astype(bf16)])
    gathered = lax.all_gather(lax.all_gather(shard, "tp", axis=1), "dp", axis=2)
    gathered = gathered.reshape(2, tp, dp * rows, shard.shape[2])
    norms = lax.all_gather(jnp.stack([ln1_gain, ln1_shift, ln2_gain, ln2_shift]), "tp", axis=1, tiled=True)
    x = whole_images(block_in).astype(f32)
    dz_low = whole_images(out_grad)
    token_w1 = tok_w1.astype(bf16)
    token_w2 = tok_w2.astype(bf16)
    xhat, inv_x = normalised(x)
    mixed = (xhat * norms[0] + norms[1]).astype(bf16)
    pre = jnp.einsum("nsc,sk->nkc", mixed, token_w1, preferred_element_type=f32) + tok_b1[:, None]
    hidden, hidden_back = jax.vjp(jax.nn.gelu, pre)
    hidden = hidden.astype(bf16)
    u = x + jnp.einsum("nkc,ks->nsc", hidden, token_w2, preferred_element_type=f32) + tok_b2[:, None]
    uhat, inv_u = normalised(u)
    count = images * S
    hn = (uhat * norms[2] + norms[3]).astype(bf16).reshape(count, full)
    dz = dz_low.reshape(count, full)
    z = jnp.zeros((count, full), f32)
    dhn = jnp.zeros((count, full), f32)
    grads1, grads2, bias = [], [], []
    inner = shard.shape[2]
    for j in range(tp):
        q = jnp.dot(hn, gathered[0, j], preferred_element_type=f32) + ch_b1[j * inner : (j + 1) * inner]
        g, g_back = jax.vjp(jax.nn.gelu, q)
        g = g.astype(bf16)
        z = z + jnp.einsum("rh,ch->rc", g, gathered[1, j], preferred_element_type=f32)
        dg = jnp.dot(dz, gathered[1, j], preferred_element_type=f32)
        dq = g_back(dg)[0].astype(bf16)
        grads2.append(jnp.einsum("rc,rh->ch", dz, g, preferred_element_type=f32).astype(bf16))
        grads1.append(jnp.einsum("rc,rh->ch", hn, dq, preferred_element_type=f32).astype(bf16))
        bias.append(jnp.sum(dq.astype(f32), 0))
        dhn = dhn + jnp.einsum("rh,ch->rc", dq, gathered[0, j], preferred_element_type=f32)
    z = (z + ch_b2).astype(bf16).astype(f32).reshape(u.shape)
    block_out = stored((u + z).astype(bf16))
    dhn = dhn.reshape(u.shape)
    dz32 = dz_low.astype(f32)
    image_gain = jnp.sum(dhn * uhat, 1)
    image_shift = jnp.sum(dhn, 1)
    du = dz32 + norm_back(dhn * norms[2], uhat, inv_u)
    dp_low = du.astype(bf16)
    dh = jnp.einsum("nsc,ks->nkc", dp_low, token_w2, preferred_element_type=f32)
    d_tok_w2 = jnp.einsum("nkc,nsc->ks", hidden, dp_low, preferred_element_type=f32)
    d_tok_b2 = jnp.sum(dp_low.astype(f32), (0, 2))
    dpre = hidden_back(dh)[0].astype(bf16)
    d_tok_w1 = jnp.einsum("nsc,nkc->sk", mixed, dpre, preferred_element_type=f32)
    d_tok_b1 = jnp.sum(dpre.astype(f32), (0, 2))
    da = jnp.einsum("nkc,sk->nsc", dpre, token_w1, preferred_element_type=f32)
    d_gain1 = jnp.sum(da * xhat, (0, 1))
    d_shift1 = jnp.sum(da, (0, 1))
    dx = stored((du + norm_back(da * norms[0], xhat, inv_x)).astype(bf16))

    gradient = jnp.stack([jnp.stack(grads1), jnp.stack(grads2)]).reshape(2, tp, dp, rows, inner)
    owned = lax.psum_scatter(lax.psum_scatter(gradient, "tp", scatter_dimension=1, tiled=True).astype(bf16), "dp", scatter_dimension=2, tiled=True)
    owned = owned.astype(f32).reshape(2, rows, inner)

    ids = lax.dynamic_slice_in_dim(group_ids, t * images, images)
    member = (ids[:, None] == jnp.arange(GROUPS)[None, :]).astype(f32)
    groups = jnp.dot(member.T, jnp.concatenate([image_gain, image_shift], 1), precision=highest)
    flat = [d_tok_w1, d_tok_w2, jnp.stack(bias), jnp.sum(dz32, (0, 1)), d_gain1, d_shift1, d_tok_b1, d_tok_b2, groups]
    sizes = [v.size for v in flat]
    need = sum(sizes)
    unit = 64 * full
    padded = -(-need // unit) * unit
    packed = jnp.concatenate([v.reshape(-1) for v in flat] + [jnp.zeros((padded - need,), f32)]).reshape(-1, full)
    total = lax.psum(packed, ("dp", "tp"))
    total = total.reshape(-1)
    pieces, start = [], 0
    for v in flat:
        pieces.append(total[start : start + v.size].reshape(v.shape))
        start += v.size
    tw1, tw2, cb1, cb2, g1, s1, tb1, tb2, gg = pieces
    gg = gg.reshape(GROUPS, 2, full)
    group_norms = jnp.sqrt(jnp.sum(gg * gg, (1, 2)))
    bound = 2.0 * math.sqrt(held * dp * S * full / GROUPS)
    factor = bound / jnp.maximum(group_norms, bound)
    clipped = jnp.sum(factor[:, None, None] * gg, 0)

    def mine(v):
        return lax.dynamic_slice_in_dim(v, t * width, width)

    return (block_out, dx, group_norms, mine(g1), mine(s1), tw1, tb1, tw2, tb2, mine(clipped[0]), mine(clipped[1]),
            owned[0], cb1.reshape(-1), owned[1].T, cb2)


def small_totals(total, flat):
    pieces, start = [], 0
    total = total.reshape(-1)
    for v in flat:
        pieces.append(total[start : start + v.size].reshape(v.shape))
        start += v.size
    return pieces


def blocked(block_in, ln1_gain, ln1_shift, tok_w1, tok_b1, tok_w2, tok_b2, ln2_gain, ln2_shift,
            ch_w1, ch_b1, ch_w2, ch_b2, group_ids, out_grad):
    t = lax.axis_index("tp")
    held = block_in.shape[0]
    shard = jnp.stack([ch_w1.astype(BF16), ch_w2.T.astype(BF16)])
    xs, ds = block_in.reshape(4, 4 * HALF, 384), out_grad.reshape(4, 4 * HALF, 384)
    lnp = jnp.zeros((8, 4, 192), F32).at[:4, t].set(jnp.stack([ln1_gain, ln1_shift, ln2_gain, ln2_shift])).reshape(8, 768)
    w1t, w2t = halves(tok_w1, 0).T.astype(BF16), halves(tok_w2, 1).T.astype(BF16)
    w, g, s, u, hn, x, dz, h, ts, op, norms = forward_pass(
        shard, xs, ds, lnp, w1t, w2t, tok_b1[:, None], halves(tok_b2, 0)[:, None], ch_b1.reshape(4, 1, 768), ch_b2[None])
    w = w.reshape(2, 4, 768, 768)
    dz32 = dz.astype(F32)
    xhat, inv_x = normalised(x)
    mixed = (xhat * norms[0] + norms[1]).astype(BF16)
    uhat, inv_u = normalised(u)
    dhn = jnp.zeros(u.shape, F32)
    grads1, grads2, bias = [], [], []
    for j in range(4):
        dg = jnp.einsum("nsc,ch->nsh", dz, w[1, j], preferred_element_type=F32)
        dq = (dg * s[j].astype(F32)).astype(BF16)
        grads2.append(jnp.einsum("nsc,nsh->ch", dz, g[j], preferred_element_type=F32).astype(BF16))
        grads1.append(jnp.einsum("nsc,nsh->ch", hn, dq, preferred_element_type=F32).astype(BF16))
        bias.append(jnp.sum(dq.astype(F32), (0, 1)))
        dhn = dhn + jnp.einsum("nsh,ch->nsc", dq, w[0, j], preferred_element_type=F32)
    image_gain = jnp.sum(dhn * uhat, 1)
    image_shift = jnp.sum(dhn, 1)
    du = dz32 + norm_back(dhn * norms[2], uhat, inv_u)
    dp_low = du.astype(BF16)
    dh = jnp.einsum("nsc,sk->nkc", dp_low, w2t, preferred_element_type=F32)
    d_tok_w2 = whole(jnp.einsum("nkc,nsc->ks", h, dp_low, preferred_element_type=F32), 1)
    d_tok_b2 = whole(jnp.sum(dp_low.astype(F32), (0, 2)), 0)
    dpre = (dh * ts.astype(F32)).astype(BF16)
    d_tok_w1 = whole(jnp.einsum("nsc,nkc->sk", mixed, dpre, preferred_element_type=F32), 0)
    d_tok_b1 = jnp.sum(dpre.astype(F32), (0, 2))
    da = jnp.einsum("nkc,ks->nsc", dpre, w1t, preferred_element_type=F32)
    d_gain1 = jnp.sum(da * xhat, (0, 1))
    d_shift1 = jnp.sum(da, (0, 1))
    dx = whole((du + norm_back(da * norms[0], xhat, inv_x)).astype(BF16), 1)

    def stored(packed):
        return lax.all_to_all(packed, "tp", 0, 0, tiled=True).reshape(block_in.shape)

    block_out = stored(op)
    dx = stored(dx.reshape(4, S, 4, 192).transpose(2, 0, 1, 3).reshape(4, 4 * HALF, 384))
    owned = scatter_grads(jnp.stack([jnp.stack(grads1), jnp.stack(grads2)]).reshape(2, 4, 8, 96, 768))
    ids = lax.dynamic_slice_in_dim(group_ids, t * 4, 4)
    member = (ids[:, None] == jnp.arange(GROUPS)[None, :]).astype(F32)
    groups = jnp.dot(member.T, jnp.concatenate([image_gain, image_shift], 1), precision=highest)
    flat = [d_tok_w1, d_tok_w2, jnp.stack(bias), jnp.sum(dz32, (0, 1)), d_gain1, d_shift1, d_tok_b1, d_tok_b2, groups]
    need = sum(v.size for v in flat)
    unit = 64 * 768
    padded = -(-need // unit) * unit
    packed = jnp.concatenate([v.reshape(-1) for v in flat] + [jnp.zeros((padded - need,), F32)]).reshape(-1, 768)
    tw1, tw2, cb1, cb2, g1, s1, tb1, tb2, gg = small_totals(total_all(packed), flat)
    gg = gg.reshape(GROUPS, 2, 768)
    group_norms = jnp.sqrt(jnp.sum(gg * gg, (1, 2)))
    bound = 2.0 * math.sqrt(held * 8 * S * 768 / GROUPS)
    factor = bound / jnp.maximum(group_norms, bound)
    clipped = jnp.sum(factor[:, None, None] * gg, 0)

    def mine(v):
        return lax.dynamic_slice_in_dim(v, t * 192, 192)

    return (block_out, dx, group_norms, mine(g1), mine(s1), tw1, tb1, tw2, tb2, mine(clipped[0]), mine(clipped[1]),
            owned[0], cb1.reshape(-1), owned[1].T, cb2)


def solution(mesh):
    stored, own, copied = P("dp", "tp", None), P("tp"), P()
    in_specs = (stored, own, own, copied, copied, copied, copied, own, own, P("dp", "tp"), copied, P("tp", "dp"), copied, P("dp"), stored)
    out_specs = (stored, stored, copied, own, own, copied, copied, copied, copied, own, own, P("dp", "tp"), copied, P("tp", "dp"), copied)
    step = blocked if (mesh.shape["dp"], mesh.shape["tp"]) == (8, 4) else general
    return jax.shard_map(step, mesh=mesh, in_specs=in_specs, out_specs=out_specs, check_vma=False)
```

```python
import functools
import math

import jax
import jax.numpy as jnp
from jax import lax
from jax.experimental import pallas as pl
from jax.experimental.pallas import tpu as pltpu
from jax.sharding import PartitionSpec as P

MESH = pl.DeviceIdType.MESH


def place():
    dp = lax.axis_index("dp"); t = lax.axis_index("tp")
    c = dp % 2; x = (dp // 2) % 2; y = dp // 4
    def at(yy, xx, cc): return (yy * 2 + xx) * 2 + cc
    return dp, t, dict(S=at(y, x, 1 - c), X=at(y, 1 - x, c), Y=at(1 - y, x, c), D=at(1 - y, 1 - x, c)), (y, x, c)

def others(t):
    first = jnp.where(t == 0, 1, jnp.where(t == 1, 0, jnp.where(t == 2, 3, 2)))
    second = jnp.where(t == 0, 2, jnp.where(t == 1, 2, 1))
    third = jnp.where(t < 2, 3, 0)
    return [first, second, third]

def meet(devices):
    barrier = pltpu.get_barrier_semaphore()
    for device in devices:
        pl.semaphore_signal(barrier, inc=1, device_id=device, device_id_type=MESH)
    pl.semaphore_wait(barrier, len(devices))

def gather_kernel(shard, out, send_sem, recv_sem, local_sem):
    dp, t, near, (y, x, c) = place()
    line = others(t)
    order = [t] + line
    meet([(near["S"], t), (near["X"], t), (near["Y"], t)] + [(dp, p) for p in line])
    started = []
    def send(src, owner, tt, device):
        k = len(started)
        copy = pltpu.make_async_remote_copy(src_ref=src, dst_ref=out.at[:, tt, owner], send_sem=send_sem.at[k],
            recv_sem=recv_sem.at[owner, tt], device_id=device, device_id_type=MESH)
        copy.start(); started.append(copy)
    def arrived(owner, tt):
        ref = out.at[:, tt, owner]
        pltpu.make_async_remote_copy(src_ref=ref, dst_ref=ref, send_sem=send_sem.at[0], recv_sem=recv_sem.at[owner, tt],
            device_id=(dp, t), device_id_type=MESH).wait_recv()
    own = pltpu.make_async_copy(shard, out.at[:, t, dp], local_sem); own.start()
    for p in line: send(shard, dp, t, (dp, p))
    def column(k):
        tt = order[k]
        if k: arrived(dp, tt)
        src = shard if k == 0 else out.at[:, tt, dp]
        send(src, dp, tt, (near["X"], t)); send(src, dp, tt, (near["Y"], t)); send(src, dp, tt, (near["S"], t))
    def neighbours(k):
        tt = order[k]
        first, second = ("X", "Y") if k % 2 == 0 else ("Y", "X")
        arrived(near[first], tt); src = out.at[:, tt, near[first]]
        send(src, near[first], tt, (near[second], t)); send(src, near[first], tt, (near["S"], t))
        arrived(near[second], tt); send(out.at[:, tt, near[second]], near[second], tt, (near["S"], t))
    def diagonal(k):
        tt = order[k]; arrived(near["D"], tt); send(out.at[:, tt, near["D"]], near["D"], tt, (near["S"], t))
    column(0); column(1); neighbours(0); column(2); neighbours(1); diagonal(0); column(3); neighbours(2); diagonal(1)
    neighbours(3); diagonal(2); diagonal(3)
    def at(yy, xx, cc): return (yy * 2 + xx) * 2 + cc
    for k in range(4):
        for yy, xx in ((y, x), (y, 1 - x), (1 - y, x), (1 - y, 1 - x)):
            arrived(at(yy, xx, 1 - c), order[k])
    own.wait()
    for copy in started: copy.wait_send()

def gather_weights(shard, cid=1):
    two, rows, cols = shard.shape
    return pl.pallas_call(gather_kernel,
        out_shape=jax.ShapeDtypeStruct((two, 4, 8, rows, cols), shard.dtype),
        in_specs=[pl.BlockSpec(memory_space=pl.ANY)], out_specs=pl.BlockSpec(memory_space=pl.ANY),
        scratch_shapes=[pltpu.SemaphoreType.DMA((31,)), pltpu.SemaphoreType.DMA((8, 4)), pltpu.SemaphoreType.DMA],
        compiler_params=pltpu.CompilerParams(collective_id=cid, has_side_effects=True))(shard)


F32 = jnp.float32
BF16 = jnp.bfloat16
HALF = 98
GAP = 104
ROWS = 208
LOW = math.sqrt(2.0 / math.pi)
CUBE = 0.044715


def gelu_pair(v):
    square = v * v
    up = 0.5 * jnp.tanh(v * (LOW + (LOW * CUBE) * square)) + 0.5
    value = v * up
    slope = up + value * (1.0 - up) * (2.0 * LOW + (6.0 * LOW * CUBE) * square)
    return value, slope


def turn(v):
    return pltpu.roll(v, 64, 1)


def join_groups(flat, image, store):
    low = lax.broadcasted_iota(jnp.int32, (HALF, 128), 1) < 64
    for p in range(2):
        a = [flat[2 * p, pl.ds(image * HALF, HALF), 128 * j : 128 * j + 128] for j in range(3)]
        b = [flat[2 * p + 1, pl.ds(image * HALF, HALF), 128 * j : 128 * j + 128] for j in range(3)]
        a1, a2, b0, b1 = turn(a[1]), turn(a[2]), turn(b[0]), turn(b[1])
        even = [a[0], jnp.where(low, a[1], b0), jnp.where(low, b0, b1)]
        odd = [jnp.where(low, a1, a2), jnp.where(low, a2, b[1]), b[2]]
        for j in range(3):
            store(0, 384 * p + 128 * j, even[j])
            store(GAP, 384 * p + 128 * j, odd[j])


def split_groups(load, flat, image):
    low = lax.broadcasted_iota(jnp.int32, (HALF, 128), 1) < 64
    for p in range(2):
        e = [load(0, 384 * p + 128 * j) for j in range(3)]
        o = [load(GAP, 384 * p + 128 * j) for j in range(3)]
        e1, e2, o0, o1 = turn(e[1]), turn(e[2]), turn(o[0]), turn(o[1])
        a = [e[0], jnp.where(low, e[1], o0), jnp.where(low, o0, o1)]
        b = [jnp.where(low, e1, e2), jnp.where(low, e2, o[1]), o[2]]
        for j in range(3):
            flat[2 * p, pl.ds(image * HALF, HALF), 128 * j : 128 * j + 128] = a[j]
            flat[2 * p + 1, pl.ds(image * HALF, HALF), 128 * j : 128 * j + 128] = b[j]


def hat(v):
    average = jnp.mean(v, -1, keepdims=True)
    inverse = lax.rsqrt(jnp.mean(v * v, -1, keepdims=True) - average * average + 1e-06)
    return (v - average) * inverse, inverse


def dot(a, b):
    return jnp.dot(a, b, preferred_element_type=F32)


def dot_nt(a, b):
    return lax.dot_general(a, b, (((1,), (1,)), ((), ())), preferred_element_type=F32)


def forward_kernel(shard, xs, ds, lnp, w1t, w2t, b1, b2, cb1, cb2,
                   w_out, g_out, s_out, u_out, hn_out, x_out, dz_out, h_out, t_out, o_out, ln_out,
                   wv, xr, dr, flat, x, xb, u, hn, g, s, h, ts, zs, op, dz, lr,
                   send_sem, recv_sem, x_send, x_recv, d_send, d_recv, l_send, l_recv, own_sem, keep_sem):
    dp, t, near, (y, xx, c) = place()
    line = others(t)
    order = [t] + line

    def at(yy, xxx, cc):
        return (yy * 2 + xxx) * 2 + cc

    started, kept = [], []

    def remote(src, dst, ss, rs, device):
        return pltpu.make_async_remote_copy(src_ref=src, dst_ref=dst, send_sem=ss, recv_sem=rs, device_id=device, device_id_type=MESH)

    def go(copy):
        copy.start()
        started.append(copy)

    def keep(src, dst):
        copy = pltpu.make_async_copy(src, dst, keep_sem.at[len(kept)])
        copy.start()
        kept.append(copy)

    meet([(near["S"], t), (near["X"], t), (near["Y"], t)] + [(dp, p) for p in line])
    sends = [0]

    def send(src, owner, tt, device):
        go(remote(src, wv.at[:, tt, owner], send_sem.at[sends[0]], recv_sem.at[owner, tt], device))
        sends[0] += 1

    def arrived(owner, tt):
        ref = wv.at[:, tt, owner]
        remote(ref, ref, send_sem.at[0], recv_sem.at[owner, tt], (dp, t)).wait_recv()

    own_w = pltpu.make_async_copy(shard, wv.at[:, t, dp], own_sem.at[0])
    own_x = pltpu.make_async_copy(xs.at[t], xr.at[t], own_sem.at[1])
    own_d = pltpu.make_async_copy(ds.at[t], dr.at[t], own_sem.at[2])
    own_l = pltpu.make_async_copy(lnp, lr.at[t], own_sem.at[3])
    for copy in (own_w, own_x, own_d, own_l):
        copy.start()
    for p in line:
        send(shard, dp, t, (dp, p))
    for n, p in enumerate(line):
        go(remote(lnp, lr.at[t], l_send.at[n], l_recv.at[t], (dp, p)))

    def column(k):
        tt = order[k]
        if k:
            arrived(dp, tt)
        src = wv.at[:, tt, dp] if k else shard
        for name in "XYS":
            send(src, dp, tt, (near[name], t))

    def neighbours(k):
        tt = order[k]
        first, second = ("X", "Y") if k % 2 == 0 else ("Y", "X")
        arrived(near[first], tt)
        src = wv.at[:, tt, near[first]]
        send(src, near[first], tt, (near[second], t))
        send(src, near[first], tt, (near["S"], t))
        arrived(near[second], tt)
        send(wv.at[:, tt, near[second]], near[second], tt, (near["S"], t))

    def diagonal(k):
        tt = order[k]
        arrived(near["D"], tt)
        send(wv.at[:, tt, near["D"]], near["D"], tt, (near["S"], t))

    column(0)
    column(1)
    neighbours(0)
    for n, p in enumerate(line):
        go(remote(xs.at[p], xr.at[t], x_send.at[n], x_recv.at[t], (dp, p)))
    column(2)
    neighbours(1)
    diagonal(0)
    column(3)
    neighbours(2)
    diagonal(1)
    neighbours(3)
    diagonal(2)
    diagonal(3)

    own_l.wait()
    for p in line:
        remote(lr.at[p], lr.at[p], l_send.at[0], l_recv.at[p], (dp, t)).wait_recv()
    params = (lr[0] + lr[1]) + (lr[2] + lr[3])
    lr[0] = params
    keep(lr.at[0], ln_out)
    zero = jnp.zeros((GAP - HALF, 768), F32)
    for n in range(4):
        for start in (HALF, GAP + HALF):
            x[n, start : start + GAP - HALF, :] = zero
    own_x.wait()
    for p in line:
        remote(xr.at[p], xr.at[p], x_send.at[0], x_recv.at[p], (dp, t)).wait_recv()
    for n, p in enumerate(line):
        go(remote(ds.at[p], dr.at[t], d_send.at[n], d_recv.at[t], (dp, p)))
    for k in range(4):
        flat[k] = xr[k].astype(F32)
    for n in range(4):
        def put(row, lane, v, n=n):
            x[n, row : row + HALF, lane : lane + 128] = v
        join_groups(flat, n, put)
        xb[n] = x[n].astype(BF16)
    keep(xb, x_out)
    g1, s1, g2, s2 = params[0:1], params[1:2], params[2:3], params[3:4]

    def token(n, carry):
        v = x[n]
        xhat, _ = hat(v)
        a = (xhat * g1 + s1).astype(BF16)
        value, slope = gelu_pair(dot(w1t[...], a) + b1[...])
        low = value.astype(BF16)
        h[n] = low
        ts[n] = slope.astype(BF16)
        r = v + dot(w2t[...], low) + b2[...]
        u[n] = r
        uhat, _ = hat(r)
        hn[n] = (uhat * g2 + s2).astype(BF16)
        return carry

    lax.fori_loop(0, 4, token, 0)
    keep(u, u_out)
    keep(hn, hn_out)
    keep(h, h_out)
    keep(ts, t_out)

    own_w.wait()
    for k in range(4):
        tt = order[k]
        for yy, xxx in ((y, xx), (y, 1 - xx), (1 - y, xx), (1 - y, 1 - xx)):
            arrived(at(yy, xxx, 1 - c), tt)
        keep(wv.at[:, tt], w_out.at[:, tt])

        def block(n, carry, tt=tt, k=k):
            value, slope = gelu_pair(dot(hn[n], wv[0, tt].reshape(768, 768)) + cb1[tt])
            low = value.astype(BF16)
            g[tt, n] = low
            s[tt, n] = slope.astype(BF16)
            part = dot_nt(low, wv[1, tt].reshape(768, 768))
            if k == 0:
                zs[n] = part
            elif k < 3:
                zs[n] += part
            else:
                z = (zs[n] + part + cb2[...]).astype(BF16).astype(F32)
                zs[n] = u[n] + z
            return carry

        lax.fori_loop(0, 4, block, 0)
        keep(g.at[tt], g_out.at[tt])
        keep(s.at[tt], s_out.at[tt])
    for n in range(4):
        split_groups(lambda row, lane, n=n: zs[n, row : row + HALF, lane : lane + 128], flat, n)
    for k in range(4):
        op[k] = flat[k].astype(BF16)
    keep(op, o_out)
    own_d.wait()
    for p in line:
        remote(dr.at[p], dr.at[p], d_send.at[0], d_recv.at[p], (dp, t)).wait_recv()
    for k in range(4):
        flat[k] = dr[k].astype(F32)
    for n in range(4):
        for start in (HALF, GAP + HALF):
            zs[n, start : start + GAP - HALF, :] = zero

        def put_grad(row, lane, v, n=n):
            zs[n, row : row + HALF, lane : lane + 128] = v

        join_groups(flat, n, put_grad)
        dz[n] = zs[n].astype(BF16)
    keep(dz, dz_out)
    for copy in started:
        copy.wait_send()
    for copy in kept:
        copy.wait()


def forward_pass(shard, xs, ds, lnp, w1t, w2t, b1, b2, cb1, cb2):
    any_, vmem = pl.BlockSpec(memory_space=pl.ANY), pl.BlockSpec(memory_space=pltpu.VMEM)
    sds = jax.ShapeDtypeStruct
    dma = pltpu.SemaphoreType.DMA
    wshape = (2, 4, 8, 96, 768)
    act, tok = (4, ROWS, 768), (4, 384, 768)
    packed = (4, 4 * HALF, 384)
    shapes = [(wshape, BF16), ((4,) + act, BF16), ((4,) + act, BF16), (act, F32), (act, BF16), (act, BF16), (act, BF16), (tok, BF16), (tok, BF16), (packed, BF16), ((8, 768), F32)]
    V = pltpu.VMEM
    return pl.pallas_call(forward_kernel,
        out_shape=[sds(*v) for v in shapes],
        in_specs=[any_] * 4 + [vmem] * 6, out_specs=[any_] * len(shapes),
        scratch_shapes=[V(wshape, BF16), V(packed, BF16), V(packed, BF16), V(packed, F32), V(act, F32), V(act, BF16), V(act, F32), V(act, BF16),
            V((4,) + act, BF16), V((4,) + act, BF16), V(tok, BF16), V(tok, BF16), V(act, F32), V(packed, BF16), V(act, BF16), V((4, 8, 768), F32),
            dma((31,)), dma((8, 4)), dma((3,)), dma((4,)), dma((3,)), dma((4,)), dma((3,)), dma((4,)), dma((4,)), dma((24,))],
        compiler_params=pltpu.CompilerParams(collective_id=1, has_side_effects=True, vmem_limit_bytes=60 << 20))(
            shard, xs, ds, lnp, w1t, w2t, b1, b2, cb1, cb2)


PIECE = 48
SMALL = 8 * PIECE


def backward_kernel(bound, w_in, g_in, s_in, u_in, hn_in, x_in, dz_in, h_in, t_in, op, norms, w1, w2, member,
                    o_out, dx_out, w_grad, total_out, fin, group_norms,
                    wv, g, s, u, hn, x, dz, h, ts, hnt, dzt, dq, dhn, gr, flat, dxp,
                    sib, first, second, final, zbuf, small, t_sib, t_chip, t_line,
                    load_sem, slot_sem, own_sem, o_send, o_recv, x_send, x_recv, sib_sem, sib_recv, a_send, a_recv, z_send, z_recv,
                    p_send, p_recv, c_send, c_recv, l_send, l_recv, b_send, b_recv, e_send, e_recv):
    dp, t, near, (y, xx, c) = place()
    line = others(t)
    order = [line[2], line[1], line[0], t]

    def at(yy, xxx, cc):
        return (yy * 2 + xxx) * 2 + cc

    chips = {"O": (y, xx), "X": (y, 1 - xx), "Y": (1 - y, xx), "D": (1 - y, 1 - xx)}
    slot = {"O": 0, "X": 1, "Y": 2, "D": 3}
    started = []

    def remote(src, dst, ss, rs, device):
        return pltpu.make_async_remote_copy(src_ref=src, dst_ref=dst, send_sem=ss, recv_sem=rs, device_id=device, device_id_type=MESH)

    def go(copy):
        copy.start()
        started.append(copy)

    def load(src, dst, n):
        copy = pltpu.make_async_copy(src, dst, load_sem.at[n])
        copy.start()
        return copy

    def fetch(k):
        tt, n = order[k], k % 2
        copies = [pltpu.make_async_copy(w_in.at[:, tt], wv.at[n], slot_sem.at[n, 0]),
                  pltpu.make_async_copy(g_in.at[tt], g.at[n], slot_sem.at[n, 1]),
                  pltpu.make_async_copy(s_in.at[tt], s.at[n], slot_sem.at[n, 2])]
        for copy in copies:
            copy.start()
        return copies

    load_dz = load(dz_in, dz, 0)
    load_hn = load(hn_in, hn, 1)
    slots = {0: fetch(0), 1: fetch(1)}
    later = [load(u_in, u, 2), load(x_in, x, 3), load(h_in, h, 4), load(t_in, ts, 5)]
    meet([(near["S"], t), (near["X"], t), (near["Y"], t), (near["D"], t)] + [(dp, p) for p in line])
    own_o = pltpu.make_async_copy(op.at[t], o_out.at[t], own_sem.at[0])
    own_o.start()
    for n, p in enumerate(line):
        go(remote(op.at[p], o_out.at[t], o_send.at[n], o_recv.at[t], (dp, p)))

    load_dz.wait()
    zero = jnp.zeros((1, 768), F32)
    small[...] = jnp.zeros((SMALL, 768), F32)
    for n in range(4):
        dzt[:, n * ROWS : (n + 1) * ROWS] = dz[n].T
    load_hn.wait()
    for n in range(4):
        hnt[:, n * ROWS : (n + 1) * ROWS] = hn[n].T

    def channel(k):
        n2 = k % 2
        for copy in slots[k]:
            copy.wait()

        def image(n, bias):
            slope = s[n2, n].astype(F32)
            low = (dot(dz[n], wv[n2, 1].reshape(768, 768)) * slope).astype(BF16)
            dq[pl.ds(pl.multiple_of(n * ROWS, 16), ROWS), :] = low
            part = dot_nt(low, wv[n2, 0].reshape(768, 768))
            if k == 0:
                dhn[n] = part
            else:
                dhn[n] += part
            return bias + jnp.sum(low.astype(F32), 0, keepdims=True)

        bias = lax.fori_loop(0, 4, image, zero)
        small[pl.ds(HALF + 1 + order[k], 1), :] = bias
        gr[0, k] = dot(hnt[...], dq[...]).astype(BF16).reshape(8, 96, 768)
        gr[1, k] = dot(dzt[...], g[n2].reshape(4 * ROWS, 768)).astype(BF16).reshape(8, 96, 768)
        if k < 2:
            slots[k + 2] = fetch(k + 2)
        for name in "DXYO":
            n = slot[name]
            go(remote(gr.at[:, k, at(*chips[name], 1 - c)], sib.at[k, n], sib_sem.at[k, n], sib_recv.at[k, n], (near["S"], t)))

    def chip_sum(k, name):
        n = slot[name]
        remote(sib.at[k, n], sib.at[k, n], sib_sem.at[k, n], sib_recv.at[k, n], (near["S"], t)).wait_recv()
        sib[k, n] = (gr[:, k, at(*chips[name], c)].astype(F32) + sib[k, n].astype(F32)).astype(BF16)

    def ways(k):
        return ("X", "Y") if k % 2 == 0 else ("Y", "X")

    def stage_one(k):
        f, s2 = ways(k)
        chip_sum(k, "D")
        go(remote(sib.at[k, 3], first.at[k], a_send.at[k, 0], a_recv.at[k, 0], (near[s2], t)))
        chip_sum(k, s2)
        go(remote(sib.at[k, slot[s2]], second.at[k], a_send.at[k, 1], a_recv.at[k, 1], (near[s2], t)))

    def stage_two(k):
        f, s2 = ways(k)
        chip_sum(k, f)
        remote(first.at[k], first.at[k], a_send.at[k, 0], a_recv.at[k, 0], (near[s2], t)).wait_recv()
        n = slot[f]
        sib[k, n] = (sib[k, n].astype(F32) + first[k].astype(F32)).astype(BF16)
        go(remote(sib.at[k, n], final.at[k], a_send.at[k, 2], a_recv.at[k, 2], (near[f], t)))

    def stage_three(k):
        f, s2 = ways(k)
        chip_sum(k, "O")
        remote(second.at[k], second.at[k], a_send.at[k, 1], a_recv.at[k, 1], (near[s2], t)).wait_recv()
        remote(final.at[k], final.at[k], a_send.at[k, 2], a_recv.at[k, 2], (near[f], t)).wait_recv()
        total = sib[k, 0].astype(F32) + second[k].astype(F32) + final[k].astype(F32)
        if k < 3:
            sib[k, 0] = total.astype(BF16)
            go(remote(sib.at[k, 0], zbuf.at[t], z_send.at[k], z_recv.at[t], (dp, order[k])))
        else:
            w_grad[...] = total

    channel(0)
    channel(1)
    stage_one(0)
    channel(2)
    stage_one(1)
    stage_two(0)
    channel(3)
    stage_one(2)
    stage_two(1)
    stage_three(0)

    for copy in later:
        copy.wait()
    g1, s1, g2 = norms[0:1], norms[1:2], norms[2:3]
    row = lax.broadcasted_iota(jnp.int32, (ROWS, 768), 0)
    ones = jnp.ones((8, 768), BF16)

    def token(n, carry):
        sum_g1, sum_s1, sum_b2 = carry
        d, grad = dhn[n], dz[n].astype(F32)
        uhat, inv_u = hat(u[n])
        pg = jnp.sum(d * uhat, 0, keepdims=True)
        pb = jnp.sum(d, 0, keepdims=True)
        small[208:272, :] += member[n] * pg
        small[272:336, :] += member[n] * pb
        e = d * g2
        du = grad + inv_u * (e - jnp.mean(e, -1, keepdims=True) - uhat * jnp.mean(e * uhat, -1, keepdims=True))
        low = du.astype(BF16)
        dpre = (dot(w2[...], low) * ts[n].astype(F32)).astype(BF16)
        xhat, inv_x = hat(x[n].astype(F32))
        a = jnp.where(row == HALF, 1.0, xhat * g1 + s1).astype(BF16)
        tok1 = dot_nt(a, dpre)
        tok2 = dot_nt(low, h[n])
        for start, size in ((0, HALF + 1), (GAP, HALF)):
            small[start : start + size, 0:384] += tok1[start : start + size]
        for start, size in ((0, HALF), (GAP, HALF)):
            small[start : start + size, 384:768] += tok2[start : start + size]
        da = dot(w1[...], dpre)
        e1 = da * g1
        dhn[n] = du + inv_x * (e1 - jnp.mean(e1, -1, keepdims=True) - xhat * jnp.mean(e1 * xhat, -1, keepdims=True))
        return (sum_g1 + jnp.sum(da * xhat, 0, keepdims=True), sum_s1 + jnp.sum(da, 0, keepdims=True), sum_b2 + dot_nt(ones, low))

    carry = (zero, zero, jnp.zeros((8, ROWS), F32))
    carry = lax.fori_loop(0, 2, token, carry)
    stage_one(3)
    stage_two(2)
    stage_three(1)
    carry = lax.fori_loop(2, 4, token, carry)
    for n in range(4):
        split_groups(lambda r, lane, n=n: dhn[n, r : r + HALF, lane : lane + 128], flat, n)
    for k in range(4):
        dxp[k] = flat[k].astype(BF16)
    own_x = pltpu.make_async_copy(dxp.at[t], dx_out.at[t], own_sem.at[1])
    own_x.start()
    for n, p in enumerate(line):
        go(remote(dxp.at[p], dx_out.at[t], x_send.at[n], x_recv.at[t], (dp, p)))
    small[202:203, :] = carry[0]
    small[203:204, :] = carry[1]
    small[204:205, 0:ROWS] = carry[2][0:1]
    total_dz = zero
    for n in range(4):
        total_dz += jnp.sum(dz[n].astype(F32), 0, keepdims=True)
    small[205:206, :] = total_dz

    chip = dp // 2
    far = [("X", near["X"] // 2), ("Y", near["Y"] // 2), ("D", near["D"] // 2)]

    def part(ref, core, q):
        return ref.at[pl.ds(pl.multiple_of((core * 4 + q) * PIECE, 8), PIECE)]

    def half(ref, core):
        return ref.at[pl.ds(pl.multiple_of(core * 4 * PIECE, 8), 4 * PIECE)]

    go(remote(half(small, 1 - c), t_sib, p_send, p_recv, (near["S"], t)))
    stage_two(3)
    stage_three(2)
    remote(t_sib, t_sib, p_send, p_recv, (near["S"], t)).wait_recv()
    half(small, c)[...] += t_sib[...]
    for n, (name, q) in enumerate(far):
        go(remote(part(small, c, q), t_chip.at[n], c_send.at[n], c_recv.at[n], (near[name], t)))
    stage_three(3)
    total = part(small, c, chip)[...]
    for n in range(3):
        remote(t_chip.at[n], t_chip.at[n], c_send.at[n], c_recv.at[n], (near["S"], t)).wait_recv()
        total = total + t_chip[n]
    t_line[t] = total
    for n, p in enumerate(line):
        go(remote(t_line.at[t], t_line.at[t], l_send.at[n], l_recv.at[t], (dp, p)))
    for p in line:
        remote(t_line.at[p], t_line.at[p], l_send.at[0], l_recv.at[p], (dp, t)).wait_recv()
    own = part(total_out, c, chip)
    own[...] = ((t_line[0] + t_line[1]) + t_line[2]) + t_line[3]
    for n, (name, q) in enumerate(far):
        go(remote(own, own, b_send.at[n], b_recv.at[chip], (near[name], t)))
    go(remote(own, own, e_send.at[3], e_recv.at[chip], (near["S"], t)))
    for p in line:
        remote(zbuf.at[p], zbuf.at[p], z_send.at[0], z_recv.at[p], (dp, t)).wait_recv()
        w_grad[...] += zbuf[p].astype(F32)
    for n, (name, q) in enumerate(far):
        there = part(total_out, c, q)
        remote(there, there, b_send.at[0], b_recv.at[q], (dp, t)).wait_recv()
        go(remote(there, there, e_send.at[n], e_recv.at[q], (near["S"], t)))
    for q in range(4):
        there = part(total_out, 1 - c, q)
        remote(there, there, e_send.at[0], e_recv.at[q], (dp, t)).wait_recv()
    gg, gb = total_out[208:272, :], total_out[272:336, :]
    size = jnp.sqrt(jnp.sum(gg * gg + gb * gb, -1, keepdims=True))
    factor = bound / jnp.maximum(size, bound)
    group_norms[...] = size
    fin[0:1, :] = total_out[202:203, :]
    fin[1:2, :] = total_out[203:204, :]
    fin[2:3, :] = jnp.sum(factor * gg, 0, keepdims=True)
    fin[3:4, :] = jnp.sum(factor * gb, 0, keepdims=True)
    own_o.wait()
    own_x.wait()
    for p in line:
        remote(o_out.at[p], o_out.at[p], o_send.at[0], o_recv.at[p], (dp, t)).wait_recv()
        remote(dx_out.at[p], dx_out.at[p], x_send.at[0], x_recv.at[p], (dp, t)).wait_recv()
    for copy in started:
        copy.wait_send()


def backward_pass(bound, *operands):
    any_, vmem = pl.BlockSpec(memory_space=pl.ANY), pl.BlockSpec(memory_space=pltpu.VMEM)
    sds = jax.ShapeDtypeStruct
    dma = pltpu.SemaphoreType.DMA
    V = pltpu.VMEM
    act, tok, packed, piece = (4, ROWS, 768), (4, 384, 768), (4, 4 * HALF, 384), (2, 96, 768)
    return pl.pallas_call(functools.partial(backward_kernel, bound),
        out_shape=[sds(packed, BF16), sds(packed, BF16), sds(piece, F32), sds((SMALL, 768), F32), sds((8, 768), F32), sds((64, 1), F32)],
        in_specs=[any_] * 10 + [vmem] * 4, out_specs=[any_] * 2 + [vmem] * 4,
        scratch_shapes=[V((2, 2, 8, 96, 768), BF16), V((2,) + act, BF16), V((2,) + act, BF16), V(act, F32), V(act, BF16), V(act, BF16), V(act, BF16),
            V(tok, BF16), V(tok, BF16), V((768, 4 * ROWS), BF16), V((768, 4 * ROWS), BF16), V((4 * ROWS, 768), BF16), V(act, F32),
            V((2, 4, 8, 96, 768), BF16), V(packed, F32), V(packed, BF16),
            V((4, 4) + piece, BF16), V((4,) + piece, BF16), V((4,) + piece, BF16), V((4,) + piece, BF16), V((4,) + piece, BF16),
            V((SMALL, 768), F32), V((4 * PIECE, 768), F32), V((3, PIECE, 768), F32), V((4, PIECE, 768), F32),
            dma((6,)), dma((2, 3)), dma((2,)), dma((3,)), dma((4,)), dma((3,)), dma((4,)), dma((4, 4)), dma((4, 4)), dma((4, 3)), dma((4, 3)), dma((4,)), dma((4,)),
            dma, dma, dma((3,)), dma((3,)), dma((3,)), dma((4,)), dma((3,)), dma((4,)), dma((4,)), dma((4,))],
        compiler_params=pltpu.CompilerParams(collective_id=2, has_side_effects=True, vmem_limit_bytes=62 << 20))(*operands)


def halves(v, axis):
    shape = v.shape
    pairs = v.reshape(shape[:axis] + (HALF, 2) + shape[axis + 1 :])
    pads = [(0, 0)] * v.ndim
    pads[axis] = (0, GAP - HALF)
    parts = [jnp.pad(lax.index_in_dim(pairs, k, axis + 1, keepdims=False), pads) for k in range(2)]
    return jnp.concatenate(parts, axis)


def whole(v, axis):
    parts = [lax.slice_in_dim(v, start, start + HALF, axis=axis) for start in (0, GAP)]
    return jnp.stack(parts, axis + 1).reshape(v.shape[:axis] + (2 * HALF,) + v.shape[axis + 1 :])


S = 196
GROUPS = 64
epsilon = 1e-06
highest = lax.Precision.HIGHEST


def normalised(values):
    average = jnp.mean(values, -1, keepdims=True)
    inverse = lax.rsqrt(jnp.mean(values * values, -1, keepdims=True) - average * average + epsilon)
    return (values - average) * inverse, inverse


def norm_back(grad_hat, normed, inverse):
    return inverse * (
        grad_hat - jnp.mean(grad_hat, -1, keepdims=True) - normed * jnp.mean(grad_hat * normed, -1, keepdims=True)
    )


def general(block_in, ln1_gain, ln1_shift, tok_w1, tok_b1, tok_w2, tok_b2, ln2_gain, ln2_shift,
               ch_w1, ch_b1, ch_w2, ch_b2, group_ids, out_grad):
    f32 = jnp.float32
    bf16 = jnp.bfloat16
    tp = lax.axis_size("tp")
    dp = lax.axis_size("dp")
    held = block_in.shape[0]
    images = held // tp
    width = block_in.shape[2] // S
    full = width * tp
    t = lax.axis_index("tp")

    def whole_images(stored):
        got = lax.all_to_all(stored.reshape(tp, images, S * width), "tp", 0, 0, tiled=True)
        return got.reshape(tp, images, S, width).transpose(1, 2, 0, 3).reshape(images, S, full)

    def stored(values):
        parts = values.reshape(images, S, tp, width).transpose(2, 0, 1, 3).reshape(tp, images, S * width)
        return lax.all_to_all(parts, "tp", 0, 0, tiled=True).reshape(held, 1, S * width)

    rows = ch_w1.shape[0]
    shard = jnp.stack([ch_w1.astype(bf16), ch_w2.T.astype(bf16)])
    gathered = lax.all_gather(lax.all_gather(shard, "tp", axis=1), "dp", axis=2)
    gathered = gathered.reshape(2, tp, dp * rows, shard.shape[2])
    norms = lax.all_gather(jnp.stack([ln1_gain, ln1_shift, ln2_gain, ln2_shift]), "tp", axis=1, tiled=True)
    x = whole_images(block_in).astype(f32)
    dz_low = whole_images(out_grad)
    token_w1 = tok_w1.astype(bf16)
    token_w2 = tok_w2.astype(bf16)
    xhat, inv_x = normalised(x)
    mixed = (xhat * norms[0] + norms[1]).astype(bf16)
    pre = jnp.einsum("nsc,sk->nkc", mixed, token_w1, preferred_element_type=f32) + tok_b1[:, None]
    hidden, hidden_back = jax.vjp(jax.nn.gelu, pre)
    hidden = hidden.astype(bf16)
    u = x + jnp.einsum("nkc,ks->nsc", hidden, token_w2, preferred_element_type=f32) + tok_b2[:, None]
    uhat, inv_u = normalised(u)
    count = images * S
    hn = (uhat * norms[2] + norms[3]).astype(bf16).reshape(count, full)
    dz = dz_low.reshape(count, full)
    z = jnp.zeros((count, full), f32)
    dhn = jnp.zeros((count, full), f32)
    grads1, grads2, bias = [], [], []
    inner = shard.shape[2]
    for j in range(tp):
        q = jnp.dot(hn, gathered[0, j], preferred_element_type=f32) + ch_b1[j * inner : (j + 1) * inner]
        g, g_back = jax.vjp(jax.nn.gelu, q)
        g = g.astype(bf16)
        z = z + jnp.einsum("rh,ch->rc", g, gathered[1, j], preferred_element_type=f32)
        dg = jnp.dot(dz, gathered[1, j], preferred_element_type=f32)
        dq = g_back(dg)[0].astype(bf16)
        grads2.append(jnp.einsum("rc,rh->ch", dz, g, preferred_element_type=f32).astype(bf16))
        grads1.append(jnp.einsum("rc,rh->ch", hn, dq, preferred_element_type=f32).astype(bf16))
        bias.append(jnp.sum(dq.astype(f32), 0))
        dhn = dhn + jnp.einsum("rh,ch->rc", dq, gathered[0, j], preferred_element_type=f32)
    z = (z + ch_b2).astype(bf16).astype(f32).reshape(u.shape)
    block_out = stored((u + z).astype(bf16))
    dhn = dhn.reshape(u.shape)
    dz32 = dz_low.astype(f32)
    image_gain = jnp.sum(dhn * uhat, 1)
    image_shift = jnp.sum(dhn, 1)
    du = dz32 + norm_back(dhn * norms[2], uhat, inv_u)
    dp_low = du.astype(bf16)
    dh = jnp.einsum("nsc,ks->nkc", dp_low, token_w2, preferred_element_type=f32)
    d_tok_w2 = jnp.einsum("nkc,nsc->ks", hidden, dp_low, preferred_element_type=f32)
    d_tok_b2 = jnp.sum(dp_low.astype(f32), (0, 2))
    dpre = hidden_back(dh)[0].astype(bf16)
    d_tok_w1 = jnp.einsum("nsc,nkc->sk", mixed, dpre, preferred_element_type=f32)
    d_tok_b1 = jnp.sum(dpre.astype(f32), (0, 2))
    da = jnp.einsum("nkc,sk->nsc", dpre, token_w1, preferred_element_type=f32)
    d_gain1 = jnp.sum(da * xhat, (0, 1))
    d_shift1 = jnp.sum(da, (0, 1))
    dx = stored((du + norm_back(da * norms[0], xhat, inv_x)).astype(bf16))

    gradient = jnp.stack([jnp.stack(grads1), jnp.stack(grads2)]).reshape(2, tp, dp, rows, inner)
    owned = lax.psum_scatter(lax.psum_scatter(gradient, "tp", scatter_dimension=1, tiled=True).astype(bf16), "dp", scatter_dimension=2, tiled=True)
    owned = owned.astype(f32).reshape(2, rows, inner)

    ids = lax.dynamic_slice_in_dim(group_ids, t * images, images)
    member = (ids[:, None] == jnp.arange(GROUPS)[None, :]).astype(f32)
    groups = jnp.dot(member.T, jnp.concatenate([image_gain, image_shift], 1), precision=highest)
    flat = [d_tok_w1, d_tok_w2, jnp.stack(bias), jnp.sum(dz32, (0, 1)), d_gain1, d_shift1, d_tok_b1, d_tok_b2, groups]
    sizes = [v.size for v in flat]
    need = sum(sizes)
    unit = 64 * full
    padded = -(-need // unit) * unit
    packed = jnp.concatenate([v.reshape(-1) for v in flat] + [jnp.zeros((padded - need,), f32)]).reshape(-1, full)
    total = lax.psum(packed, ("dp", "tp"))
    total = total.reshape(-1)
    pieces, start = [], 0
    for v in flat:
        pieces.append(total[start : start + v.size].reshape(v.shape))
        start += v.size
    tw1, tw2, cb1, cb2, g1, s1, tb1, tb2, gg = pieces
    gg = gg.reshape(GROUPS, 2, full)
    group_norms = jnp.sqrt(jnp.sum(gg * gg, (1, 2)))
    bound = 2.0 * math.sqrt(held * dp * S * full / GROUPS)
    factor = bound / jnp.maximum(group_norms, bound)
    clipped = jnp.sum(factor[:, None, None] * gg, 0)

    def mine(v):
        return lax.dynamic_slice_in_dim(v, t * width, width)

    return (block_out, dx, group_norms, mine(g1), mine(s1), tw1, tb1, tw2, tb2, mine(clipped[0]), mine(clipped[1]),
            owned[0], cb1.reshape(-1), owned[1].T, cb2)


def blocked(block_in, ln1_gain, ln1_shift, tok_w1, tok_b1, tok_w2, tok_b2, ln2_gain, ln2_shift,
            ch_w1, ch_b1, ch_w2, ch_b2, group_ids, out_grad):
    t = lax.axis_index("tp")
    held = block_in.shape[0]
    shard = jnp.stack([ch_w1.astype(BF16), ch_w2.T.astype(BF16)])
    xs, ds = block_in.reshape(4, 4 * HALF, 384), out_grad.reshape(4, 4 * HALF, 384)
    lnp = jnp.zeros((8, 4, 192), F32).at[:4, t].set(jnp.stack([ln1_gain, ln1_shift, ln2_gain, ln2_shift])).reshape(8, 768)
    w1, w2 = halves(tok_w1, 0).astype(BF16), halves(tok_w2, 1).astype(BF16)
    w, g, s, u, hn, x, dz, h, ts, op, norms = forward_pass(
        shard, xs, ds, lnp, w1.T, w2.T, tok_b1[:, None], halves(tok_b2, 0)[:, None], ch_b1.reshape(4, 1, 768), ch_b2[None])
    ids = lax.dynamic_slice_in_dim(group_ids, t * 4, 4)
    member = (ids[:, None] == jnp.arange(GROUPS)[None, :]).astype(F32)[:, :, None]
    bound = 2.0 * math.sqrt(held * 8 * S * 768 / GROUPS)
    out, dx, owned, total, fin, sizes = backward_pass(bound, w, g, s, u, hn, x, dz, h, ts, op, norms, w1, w2, member)
    own = lax.dynamic_index_in_dim(fin.reshape(8, 4, 192), t, 1, keepdims=False)
    tw1, tw2 = whole(total[:ROWS, :384], 0), whole(total[:ROWS, 384:], 0).T
    cb1 = total[HALF + 1 : HALF + 5].reshape(-1)
    tb2 = whole(total[204, :ROWS], 0)
    return (out.reshape(block_in.shape), dx.reshape(block_in.shape), sizes.reshape(-1), own[0], own[1], tw1, total[HALF, :384], tw2, tb2,
            own[2], own[3], owned[0], cb1, owned[1].T, total[205])


def solution(mesh):
    stored, own, copied = P("dp", "tp", None), P("tp"), P()
    in_specs = (stored, own, own, copied, copied, copied, copied, own, own, P("dp", "tp"), copied, P("tp", "dp"), copied, P("dp"), stored)
    out_specs = (stored, stored, copied, own, own, copied, copied, copied, copied, own, own, P("dp", "tp"), copied, P("tp", "dp"), copied)
    step = blocked if (mesh.shape["dp"], mesh.shape["tp"]) == (8, 4) else general
    return jax.shard_map(step, mesh=mesh, in_specs=in_specs, out_specs=out_specs, check_vma=False)
```

```python
import functools
import math

import jax
import jax.numpy as jnp
from jax import lax
from jax.experimental import pallas as pl
from jax.experimental.pallas import tpu as pltpu
from jax.sharding import PartitionSpec as P

MESH = pl.DeviceIdType.MESH


S = 196
GROUPS = 64
F32 = jnp.float32
BF16 = jnp.bfloat16
HALF = 98
GAP = 104
ROWS = 208
BLOCK = 4 * HALF
LOW = math.sqrt(2.0 / math.pi)
CUBE = 0.044715


def place():
    dp = lax.axis_index("dp")
    t = lax.axis_index("tp")
    c, x, y = dp % 2, (dp // 2) % 2, dp // 4
    near = dict(S=owner(y, x, 1 - c), X=owner(y, 1 - x, c), Y=owner(1 - y, x, c), D=owner(1 - y, 1 - x, c))
    return dp, t, near, (y, x, c)


def owner(y, x, c):
    return (y * 2 + x) * 2 + c


def others(t):
    first = jnp.where(t == 0, 1, jnp.where(t == 1, 0, jnp.where(t == 2, 3, 2)))
    second = jnp.where(t == 0, 2, jnp.where(t == 1, 2, 1))
    third = jnp.where(t < 2, 3, 0)
    return [first, second, third]


def meet(devices):
    barrier = pltpu.get_barrier_semaphore()
    for device in devices:
        pl.semaphore_signal(barrier, inc=1, device_id=device, device_id_type=MESH)
    pl.semaphore_wait(barrier, len(devices))


def remote(src, dst, ss, rs, device):
    return pltpu.make_async_remote_copy(src_ref=src, dst_ref=dst, send_sem=ss, recv_sem=rs, device_id=device, device_id_type=MESH)


def gelu_pair(v):
    square = v * v
    up = 0.5 * jnp.tanh(v * (LOW + (LOW * CUBE) * square)) + 0.5
    value = v * up
    slope = up + value * (1.0 - up) * (2.0 * LOW + (6.0 * LOW * CUBE) * square)
    return value, slope


def turn(v):
    return pltpu.roll(v, 64, 1)


def lane_low():
    return lax.broadcasted_iota(jnp.int32, (HALF, 128), 1) < 64


def join_groups(flat, image, store):
    low = lane_low()
    for p in range(2):
        a = [flat[j, pl.ds(2 * p * BLOCK + image * HALF, HALF), :] for j in range(3)]
        b = [flat[j, pl.ds((2 * p + 1) * BLOCK + image * HALF, HALF), :] for j in range(3)]
        a1, a2, b0, b1 = turn(a[1]), turn(a[2]), turn(b[0]), turn(b[1])
        even = [a[0], jnp.where(low, a[1], b0), jnp.where(low, b0, b1)]
        odd = [jnp.where(low, a1, a2), jnp.where(low, a2, b[1]), b[2]]
        for j in range(3):
            store(0, 384 * p + 128 * j, even[j])
            store(GAP, 384 * p + 128 * j, odd[j])


def split_groups(load, flat, image):
    low = lane_low()
    for p in range(2):
        e = [load(0, 384 * p + 128 * j) for j in range(3)]
        o = [load(GAP, 384 * p + 128 * j) for j in range(3)]
        e1, e2, o0, o1 = turn(e[1]), turn(e[2]), turn(o[0]), turn(o[1])
        a = [e[0], jnp.where(low, e[1], o0), jnp.where(low, o0, o1)]
        b = [jnp.where(low, e1, e2), jnp.where(low, e2, o[1]), o[2]]
        for j in range(3):
            flat[j, pl.ds(2 * p * BLOCK + image * HALF, HALF), :] = a[j]
            flat[j, pl.ds((2 * p + 1) * BLOCK + image * HALF, HALF), :] = b[j]


def spread(packed, flat):
    for k in range(4):
        for j in range(3):
            flat[j, pl.ds(k * BLOCK, BLOCK), :] = packed[k, :, 128 * j : 128 * j + 128].astype(F32)


def pack(flat, packed):
    for k in range(4):
        for j in range(3):
            packed[k, :, 128 * j : 128 * j + 128] = flat[j, pl.ds(k * BLOCK, BLOCK), :].astype(BF16)


def to_rows(stored, flat):
    for i in range(HALF):
        for j in range(3):
            start = 384 * i + 128 * j
            flat[j, pl.ds(i, 16, stride=HALF), :] = stored[:, start : start + 128].astype(F32)


def to_stored(flat, stored):
    for i in range(HALF):
        for j in range(3):
            start = 384 * i + 128 * j
            stored[:, start : start + 128] = flat[j, pl.ds(i, 16, stride=HALF), :].astype(BF16)


def hat(v):
    average = jnp.mean(v, -1, keepdims=True)
    inverse = lax.rsqrt(jnp.mean(v * v, -1, keepdims=True) - average * average + 1e-06)
    return (v - average) * inverse, inverse


def dot(a, b):
    return jnp.dot(a, b, preferred_element_type=F32)


def dot_nt(a, b):
    return lax.dot_general(a, b, (((1,), (1,)), ((), ())), preferred_element_type=F32)


def forward_kernel(cw1, cw2, xin, din, p0, p1, p2, p3, tw1, tw2, b1, b2, cb1, cb2,
                   w_out, g_out, s_out, u_out, hn_out, x_out, dz_out, h_out, t_out, o_out, ln_out, w1_out, w2_out,
                   wf, shard, wv, stored, xs, ds, xr, dr, flat, x, xb, u, hn, hnt, g, s, h, ts, zs, op, dz, lr, lall, t3, c2, w1, w2, w1t, w2t,
                   send_sem, recv_sem, line_sem, x_send, x_recv, d_send, d_recv, l_send, l_recv, in_sem, keep_sem):
    dp, t, near, (y, xx, c) = place()
    line = others(t)
    order = [t] + line
    started, kept, maybe = [], [], []

    def go(copy):
        copy.start()
        started.append(copy)

    def keep(src, dst):
        copy = pltpu.make_async_copy(src, dst, keep_sem.at[len(kept)])
        copy.start()
        kept.append(copy)

    def bring(src, dst, n):
        copy = pltpu.make_async_copy(src, dst, in_sem.at[n])
        copy.start()
        return copy

    in_w1, in_w2 = bring(cw1, wf.at[0], 0), bring(cw2, wf.at[1], 1)
    in_x, in_d = bring(xin, stored.at[0], 2), bring(din, stored.at[1], 3)
    meet([(near["S"], t), (near["X"], t), (near["Y"], t)] + [(dp, p) for p in line])
    sends = [0]

    def send(src, who, tt, device):
        go(remote(src, wv.at[:, tt, who], send_sem.at[sends[0]], recv_sem.at[who, tt], device))
        sends[0] += 1

    def along(src, tt, target):
        n = len(maybe)
        inside = (target >= 0) & (target <= 3)
        copy = remote(src, wv.at[:, tt, dp], line_sem.at[n], recv_sem.at[dp, tt], (dp, jnp.clip(target, 0, 3)))
        pl.when(inside)(copy.start)
        maybe.append((inside, copy))

    def arrived(who, tt):
        ref = wv.at[:, tt, who]
        remote(ref, ref, send_sem.at[0], recv_sem.at[who, tt], (dp, t)).wait_recv()

    in_w1.wait()
    in_w2.wait()
    shard[...] = wf[...].astype(BF16)
    along(shard, t, t + 1)
    along(shard, t, t - 1)
    for name in "XYS":
        send(shard, dp, t, (near[name], t))
    wv[:, t, dp] = shard[...]
    for n, ref in enumerate((p0, p1, p2, p3)):
        row = ref[...].reshape(1, 192)
        wide = jnp.concatenate([row, row, row, row], 1)
        lane = lax.broadcasted_iota(jnp.int32, (1, 768), 1)
        lr[t, n : n + 1, :] = jnp.where((lane >= 192 * t) & (lane < 192 * t + 192), wide, 0.0)
    for n, p in enumerate(line):
        go(remote(lr.at[t], lr.at[t], l_send.at[n], l_recv.at[t], (dp, p)))

    def column(k):
        tt = order[k]
        arrived(dp, tt)
        src = wv.at[:, tt, dp]
        along(src, tt, jnp.where(tt < t, t + 1, t - 1))
        for name in "XYS":
            send(src, dp, tt, (near[name], t))

    def neighbours(k):
        tt = order[k]
        first, second = ("X", "Y") if k % 2 == 0 else ("Y", "X")
        arrived(near[first], tt)
        src = wv.at[:, tt, near[first]]
        send(src, near[first], tt, (near[second], t))
        send(src, near[first], tt, (near["S"], t))
        arrived(near[second], tt)
        send(wv.at[:, tt, near[second]], near[second], tt, (near["S"], t))

    def diagonal(k):
        tt = order[k]
        arrived(near["D"], tt)
        send(wv.at[:, tt, near["D"]], near["D"], tt, (near["S"], t))

    def exchange(src, dst, ss, rs):
        for n, p in enumerate(line):
            go(remote(src.at[p], dst.at[t], ss.at[n], rs.at[t], (dp, p)))

    in_x.wait()
    to_rows(stored.at[0], flat)
    pack(flat, xs)
    column(1)
    neighbours(0)
    column(2)
    exchange(xs, xr, x_send, x_recv)
    xr[t] = xs[t]
    neighbours(1)
    diagonal(0)
    column(3)
    in_d.wait()
    to_rows(stored.at[1], flat)
    pack(flat, ds)
    dr[t] = ds[t]
    gap = jnp.zeros((GAP - HALF, 128), F32)
    for n, (src, dst) in enumerate(((tw1, w1), (tw2, w2t))):
        for j in range(3):
            t3[j] = src[:, 128 * j : 128 * j + 128]
        for j in range(3):
            even, odd = t3[j, pl.ds(0, HALF, stride=2), :], t3[j, pl.ds(1, HALF, stride=2), :]
            dst[:, 128 * j : 128 * j + 128] = jnp.concatenate([even, gap, odd, gap], 0).astype(BF16)
    w1t[...] = w1[...].T
    w2[...] = w2t[...].T
    keep(w1, w1_out)
    keep(w2, w2_out)
    c2[...] = jnp.broadcast_to(b2[...].reshape(1, S), (128, S)).T
    few = jnp.zeros((GAP - HALF, 1), F32)
    shift2 = jnp.concatenate([c2[pl.ds(0, HALF, stride=2), :][:, 0:1], few, c2[pl.ds(1, HALF, stride=2), :][:, 0:1], few], 0)
    shift1 = jnp.broadcast_to(b1[...].reshape(1, 384), (8, 384)).T[:, 0:1]
    neighbours(2)
    diagonal(1)
    neighbours(3)
    diagonal(2)
    diagonal(3)

    for p in line:
        remote(lr.at[p], lr.at[p], l_send.at[0], l_recv.at[p], (dp, t)).wait_recv()
    params = (lr[0] + lr[1]) + (lr[2] + lr[3])
    lall[...] = params
    keep(lall, ln_out)
    zero = jnp.zeros((GAP - HALF, 768), F32)
    for n in range(4):
        for start in (HALF, GAP + HALF):
            x[n, start : start + GAP - HALF, :] = zero
    for p in line:
        remote(xr.at[p], xr.at[p], x_send.at[0], x_recv.at[p], (dp, t)).wait_recv()
    exchange(ds, dr, d_send, d_recv)
    spread(xr, flat)
    for n in range(4):
        def put(row, lane, v, n=n):
            x[n, row : row + HALF, lane : lane + 128] = v
        join_groups(flat, n, put)
        xb[n] = x[n].astype(BF16)
    keep(xb, x_out)
    g1, s1, g2, s2 = params[0:1], params[1:2], params[2:3], params[3:4]

    def token(n, carry):
        v = x[n]
        xhat, _ = hat(v)
        a = (xhat * g1 + s1).astype(BF16)
        value, slope = gelu_pair(dot(w1t[...], a) + shift1)
        low = value.astype(BF16)
        h[n] = low
        ts[n] = slope.astype(BF16)
        r = v + dot(w2t[...], low) + shift2
        u[n] = r
        uhat, _ = hat(r)
        hn[n] = (uhat * g2 + s2).astype(BF16)
        return carry

    lax.fori_loop(0, 4, token, 0)
    keep(u, u_out)
    keep(h, h_out)
    keep(ts, t_out)

    for k in range(4):
        tt = order[k]
        for yy, xxx in ((y, xx), (y, 1 - xx), (1 - y, xx), (1 - y, 1 - xx)):
            arrived(owner(yy, xxx, 1 - c), tt)
        keep(wv.at[:, tt], w_out.at[:, tt])

        def block(n, carry, tt=tt, k=k):
            value, slope = gelu_pair(dot(hn[n], wv[0, tt].reshape(768, 768)) + cb1[pl.ds(pl.multiple_of(tt * 768, 128), 768)].reshape(1, 768))
            low = value.astype(BF16)
            g[tt, n] = low
            s[tt, n] = slope.astype(BF16)
            part = dot_nt(low, wv[1, tt].reshape(768, 768))
            if k == 0:
                zs[n] = part
            elif k < 3:
                zs[n] += part
            else:
                z = (zs[n] + part + cb2[...].reshape(1, 768)).astype(BF16).astype(F32)
                zs[n] = u[n] + z
            return carry

        lax.fori_loop(0, 4, block, 0)
        keep(g.at[tt], g_out.at[tt])
        keep(s.at[tt], s_out.at[tt])
    for n in range(4):
        split_groups(lambda row, lane, n=n: zs[n, row : row + HALF, lane : lane + 128], flat, n)
    pack(flat, op)
    keep(op, o_out)
    for n in range(4):
        hnt[:, n * ROWS : (n + 1) * ROWS] = hn[n].T
    keep(hnt, hn_out)
    for p in line:
        remote(dr.at[p], dr.at[p], d_send.at[0], d_recv.at[p], (dp, t)).wait_recv()
    spread(dr, flat)
    for n in range(4):
        for start in (HALF, GAP + HALF):
            zs[n, start : start + GAP - HALF, :] = zero

        def put_grad(row, lane, v, n=n):
            zs[n, row : row + HALF, lane : lane + 128] = v

        join_groups(flat, n, put_grad)
        dz[n] = zs[n].astype(BF16)
    keep(dz, dz_out)
    for copy in started:
        copy.wait_send()
    for inside, copy in maybe:
        pl.when(inside)(copy.wait_send)
    for copy in kept:
        copy.wait()


def forward_pass(*operands):
    any_, vmem = pl.BlockSpec(memory_space=pl.ANY), pl.BlockSpec(memory_space=pltpu.VMEM)
    sds = jax.ShapeDtypeStruct
    dma = pltpu.SemaphoreType.DMA
    wshape, act, tok, packed = (2, 4, 8, 96, 768), (4, ROWS, 768), (4, 384, 768), (4, BLOCK, 384)
    shapes = [(wshape, BF16), ((4,) + act, BF16), ((4,) + act, BF16), (act, F32), ((768, 4 * ROWS), BF16), (act, BF16), (act, BF16),
              (tok, BF16), (tok, BF16), (packed, BF16), ((8, 768), F32), ((ROWS, 384), BF16), ((384, ROWS), BF16)]
    V = pltpu.VMEM
    return pl.pallas_call(forward_kernel,
        out_shape=[sds(*v) for v in shapes],
        in_specs=[any_] * 4 + [vmem] * 10, out_specs=[any_] * len(shapes),
        scratch_shapes=[V((2, 96, 768), F32), V((2, 96, 768), BF16), V(wshape, BF16), V((2, 16, HALF * 384), BF16), V(packed, BF16), V(packed, BF16),
            V(packed, BF16), V(packed, BF16), V((3, 4 * BLOCK, 128), F32), V(act, F32), V(act, BF16), V(act, F32), V(act, BF16), V((768, 4 * ROWS), BF16),
            V((4,) + act, BF16), V((4,) + act, BF16), V(tok, BF16), V(tok, BF16), V(act, F32), V(packed, BF16), V(act, BF16), V((4, 8, 768), F32), V((8, 768), F32),
            V((3, S, 128), F32), V((S, 128), F32), V((ROWS, 384), BF16), V((384, ROWS), BF16), V((384, ROWS), BF16), V((ROWS, 384), BF16),
            dma((28,)), dma((8, 4)), dma((5,)), dma((3,)), dma((4,)), dma((3,)), dma((4,)), dma((3,)), dma((4,)), dma((4,)), dma((24,))],
        compiler_params=pltpu.CompilerParams(collective_id=1, has_side_effects=True, vmem_limit_bytes=60 << 20))(*operands)


PIECE = 48
SMALL = 8 * PIECE


def backward_kernel(w_in, g_in, s_in, u_in, hn_in, x_in, dz_in, h_in, t_in, op, norms, w1, w2, ids,
                    o_out, dx_out, w_grad, total_out,
                    wv, g, s, u, x, dz, h, ts, hnt, dzt, dhn, gr, flat, dxp,
                    sib, first, second, final, zbuf, small, t_sib, t_chip, t_line, t_full,
                    load_sem, slot_sem, own_sem, o_send, o_recv, x_send, x_recv, sib_sem, sib_recv, a_send, a_recv, z_send, z_recv,
                    p_send, p_recv, c_send, c_recv, l_send, l_recv, m_send, m_recv, b_send, b_recv, e_send, e_recv):
    dp, t, near, (y, xx, c) = place()
    line = others(t)
    order = [line[2], line[1], line[0], t]
    chips = {"O": (y, xx), "X": (y, 1 - xx), "Y": (1 - y, xx), "D": (1 - y, 1 - xx)}
    slot = {"O": 0, "X": 1, "Y": 2, "D": 3}
    started = []

    def go(copy):
        copy.start()
        started.append(copy)

    def load(src, dst, sem):
        copy = pltpu.make_async_copy(src, dst, sem)
        copy.start()
        return copy

    def fetch(k):
        return load(w_in.at[:, order[k]], wv.at[k % 2], slot_sem.at[k % 2])

    load_dz = load(dz_in, dz, load_sem.at[0])
    load_g = [load(g_in.at[order[k]], g.at[k], load_sem.at[1 + k]) for k in range(4)]
    slots = {0: fetch(0), 1: fetch(1)}
    load_s = [load(s_in.at[order[k]], s.at[k], load_sem.at[5 + k]) for k in range(4)]
    later = [load(u_in, u, load_sem.at[9]), load(x_in, x, load_sem.at[10]), load(h_in, h, load_sem.at[11]), load(t_in, ts, load_sem.at[12])]
    load_hn = load(hn_in, hnt, load_sem.at[13])
    meet([(near["S"], t), (near["X"], t), (near["Y"], t), (near["D"], t)] + [(dp, p) for p in line])
    own_o = load(op.at[t], o_out.at[t], own_sem.at[0])
    for n, p in enumerate(line):
        go(remote(op.at[p], o_out.at[t], o_send.at[n], o_recv.at[t], (dp, p)))

    def hand_over(j, k):
        for name in "DXYO":
            n = slot[name]
            go(remote(gr.at[j, k, owner(*chips[name], 1 - c)], sib.at[j, k, n], sib_sem.at[j, k, n], sib_recv.at[j, k, n], (near["S"], t)))

    def chip_sum(j, k, name):
        n = slot[name]
        remote(sib.at[j, k, n], sib.at[j, k, n], sib_sem.at[j, k, n], sib_recv.at[j, k, n], (near["S"], t)).wait_recv()
        sib[j, k, n] = (gr[j, k, owner(*chips[name], c)].astype(F32) + sib[j, k, n].astype(F32)).astype(BF16)

    def ways(k):
        return ("X", "Y") if k % 2 == 0 else ("Y", "X")

    def hop(j, k, src, dst, n, name):
        go(remote(src, dst, a_send.at[j, k, n], a_recv.at[j, k, n], (near[name], t)))

    def landed(j, k, dst, n):
        remote(dst, dst, a_send.at[j, k, n], a_recv.at[j, k, n], (near["S"], t)).wait_recv()

    def stage_one(j, k):
        f, s2 = ways(k)
        chip_sum(j, k, "D")
        hop(j, k, sib.at[j, k, 3], first.at[j, k], 0, s2)
        chip_sum(j, k, s2)
        hop(j, k, sib.at[j, k, slot[s2]], second.at[j, k], 1, s2)

    def stage_two(j, k):
        f, s2 = ways(k)
        n = slot[f]
        chip_sum(j, k, f)
        landed(j, k, first.at[j, k], 0)
        sib[j, k, n] = (sib[j, k, n].astype(F32) + first[j, k].astype(F32)).astype(BF16)
        hop(j, k, sib.at[j, k, n], final.at[j, k], 2, f)

    def stage_three(j, k):
        chip_sum(j, k, "O")
        landed(j, k, second.at[j, k], 1)
        landed(j, k, final.at[j, k], 2)
        total = sib[j, k, 0].astype(F32) + second[j, k].astype(F32) + final[j, k].astype(F32)
        if k < 3:
            sib[j, k, 0] = total.astype(BF16)
            go(remote(sib.at[j, k, 0], zbuf.at[j, t], z_send.at[j, k], z_recv.at[j, t], (dp, order[k])))
        else:
            w_grad[j] = total

    zero = jnp.zeros((1, 768), F32)
    load_dz.wait()
    for n in range(4):
        dzt[:, n * ROWS : (n + 1) * ROWS] = dz[n].T

    def second_weight(k):
        load_g[k].wait()
        gr[1, k] = dot(dzt[...], g[k].reshape(4 * ROWS, 768)).astype(BF16).reshape(8, 96, 768)
        hand_over(1, k)

    def data(k):
        n2 = k % 2
        slots[k].wait()
        load_s[k].wait()

        def image(n, bias):
            low = (dot(dz[n], wv[n2, 1].reshape(768, 768)) * s[k, n].astype(F32)).astype(BF16)
            s[k, n] = low
            part = dot_nt(low, wv[n2, 0].reshape(768, 768))
            if k == 0:
                dhn[n] = part
            else:
                dhn[n] += part
            return bias + jnp.sum(low.astype(F32), 0, keepdims=True)

        bias = lax.fori_loop(0, 4, image, zero)
        small[pl.ds(HALF + 1 + order[k], 1), :] = bias
        if k < 2:
            slots[k + 2] = fetch(k + 2)

    def first_weight(k):
        gr[0, k] = dot(hnt[...], s[k].reshape(4 * ROWS, 768)).astype(BF16).reshape(8, 96, 768)
        hand_over(0, k)

    g1, s1, g2 = norms[0:1], norms[1:2], norms[2:3]
    row = lax.broadcasted_iota(jnp.int32, (ROWS, 768), 0)
    ones = jnp.ones((8, 768), BF16)
    groups = lax.broadcasted_iota(jnp.int32, (GROUPS, 16), 0) == ids[...].reshape(1, 16)
    lane = lax.broadcasted_iota(jnp.int32, (GROUPS, 16), 1)

    def token(n, carry):
        sum_g1, sum_s1, sum_b2 = carry
        d, grad = dhn[n], dz[n].astype(F32)
        uhat, inv_u = hat(u[n])
        member = jnp.sum(jnp.where(groups & (lane == 4 * t + n), 1.0, 0.0), -1, keepdims=True)
        small[208:272, :] += member * jnp.sum(d * uhat, 0, keepdims=True)
        small[272:336, :] += member * jnp.sum(d, 0, keepdims=True)
        e = d * g2
        du = grad + inv_u * (e - jnp.mean(e, -1, keepdims=True) - uhat * jnp.mean(e * uhat, -1, keepdims=True))
        low = du.astype(BF16)
        dpre = (dot(w2[...], low) * ts[n].astype(F32)).astype(BF16)
        xhat, inv_x = hat(x[n].astype(F32))
        a = jnp.where(row == HALF, 1.0, xhat * g1 + s1).astype(BF16)
        tok1 = dot_nt(a, dpre)
        tok2 = dot_nt(low, h[n])
        for start, size in ((0, HALF + 1), (GAP, HALF)):
            small[start : start + size, 0:384] += tok1[start : start + size]
        for start, size in ((0, HALF), (GAP, HALF)):
            small[start : start + size, 384:768] += tok2[start : start + size]
        da = dot(w1[...], dpre)
        e1 = da * g1
        dhn[n] = du + inv_x * (e1 - jnp.mean(e1, -1, keepdims=True) - xhat * jnp.mean(e1 * xhat, -1, keepdims=True))
        return (sum_g1 + jnp.sum(da * xhat, 0, keepdims=True), sum_s1 + jnp.sum(da, 0, keepdims=True), sum_b2 + dot_nt(ones, low))

    small[...] = jnp.zeros((SMALL, 768), F32)
    second_weight(0)
    second_weight(1)
    stage_one(1, 0)
    second_weight(2)
    stage_one(1, 1)
    second_weight(3)
    stage_one(1, 2)
    stage_one(1, 3)
    data(0)
    stage_two(1, 0)
    stage_two(1, 1)
    data(1)
    stage_two(1, 2)
    stage_two(1, 3)
    data(2)
    stage_three(1, 0)
    stage_three(1, 1)
    data(3)
    stage_three(1, 2)
    stage_three(1, 3)
    for copy in later:
        copy.wait()
    carry = lax.fori_loop(0, 4, token, (zero, zero, jnp.zeros((8, ROWS), F32)))
    for n in range(4):
        split_groups(lambda r, lane, n=n: dhn[n, r : r + HALF, lane : lane + 128], flat, n)
    pack(flat, dxp)
    own_x = load(dxp.at[t], dx_out.at[t], own_sem.at[1])
    for n, p in enumerate(line):
        go(remote(dxp.at[p], dx_out.at[t], x_send.at[n], x_recv.at[t], (dp, p)))
    small[202:203, :] = carry[0]
    small[203:204, :] = carry[1]
    small[204:205, 0:ROWS] = carry[2][0:1]
    total_dz = zero
    for n in range(4):
        total_dz += jnp.sum(dz[n].astype(F32), 0, keepdims=True)
    small[205:206, :] = total_dz

    chip = dp // 2
    far = [("X", near["X"] // 2), ("Y", near["Y"] // 2), ("D", near["D"] // 2)]

    def part(ref, core, q):
        return ref.at[pl.ds(pl.multiple_of((core * 4 + q) * PIECE, 8), PIECE)]

    def half(ref, core):
        return ref.at[pl.ds(pl.multiple_of(core * 4 * PIECE, 8), 4 * PIECE)]

    def quarter(ref, p):
        return ref.at[pl.ds(pl.multiple_of((p // 2) * (PIECE // 2), 8), PIECE // 2), pl.ds(pl.multiple_of((p % 2) * 384, 128), 384)]

    go(remote(half(small, 1 - c), t_sib, p_send, p_recv, (near["S"], t)))
    load_hn.wait()
    first_weight(0)
    remote(t_sib, t_sib, p_send, p_recv, (near["S"], t)).wait_recv()
    half(small, c)[...] += t_sib[...]
    for n, (name, q) in enumerate(far):
        go(remote(part(small, c, q), t_chip.at[n], c_send.at[n], c_recv.at[n], (near[name], t)))
    first_weight(1)
    stage_one(0, 0)
    first_weight(2)
    stage_one(0, 1)
    first_weight(3)
    stage_one(0, 2)
    stage_one(0, 3)
    total = part(small, c, chip)[...]
    for n in range(3):
        remote(t_chip.at[n], t_chip.at[n], c_send.at[n], c_recv.at[n], (near["S"], t)).wait_recv()
        total = total + t_chip[n]
    t_full[...] = total
    for n, p in enumerate(line):
        go(remote(quarter(t_full, p), t_line.at[t], l_send.at[n], l_recv.at[t], (dp, p)))
    t_line[t] = quarter(t_full, t)[...]
    stage_two(0, 0)
    stage_two(0, 1)
    for p in line:
        remote(t_line.at[p], t_line.at[p], l_send.at[0], l_recv.at[p], (dp, t)).wait_recv()
    own = part(total_out, c, chip)
    mine = quarter(own, t)
    mine[...] = ((t_line[0] + t_line[1]) + t_line[2]) + t_line[3]
    for n, p in enumerate(line):
        go(remote(mine, mine, m_send.at[n], m_recv.at[t], (dp, p)))
    stage_two(0, 2)
    stage_two(0, 3)
    stage_three(0, 0)
    for p in line:
        there = quarter(own, p)
        remote(there, there, m_send.at[0], m_recv.at[p], (dp, t)).wait_recv()
    for n, (name, q) in enumerate(far):
        go(remote(own, own, b_send.at[n], b_recv.at[chip], (near[name], t)))
    go(remote(own, own, e_send.at[3], e_recv.at[chip], (near["S"], t)))
    stage_three(0, 1)
    stage_three(0, 2)
    stage_three(0, 3)
    for n, (name, q) in enumerate(far):
        there = part(total_out, c, q)
        remote(there, there, b_send.at[0], b_recv.at[q], (dp, t)).wait_recv()
        go(remote(there, there, e_send.at[n], e_recv.at[q], (near["S"], t)))
    for j in (1, 0):
        for p in line:
            remote(zbuf.at[j, p], zbuf.at[j, p], z_send.at[j, 0], z_recv.at[j, p], (dp, t)).wait_recv()
            w_grad[j] += zbuf[j, p].astype(F32)
    for q in range(4):
        there = part(total_out, 1 - c, q)
        remote(there, there, e_send.at[0], e_recv.at[q], (dp, t)).wait_recv()
    own_o.wait()
    own_x.wait()
    for p in line:
        remote(o_out.at[p], o_out.at[p], o_send.at[0], o_recv.at[p], (dp, t)).wait_recv()
        remote(dx_out.at[p], dx_out.at[p], x_send.at[0], x_recv.at[p], (dp, t)).wait_recv()
    for copy in started:
        copy.wait_send()


def backward_pass(*operands):
    any_, vmem = pl.BlockSpec(memory_space=pl.ANY), pl.BlockSpec(memory_space=pltpu.VMEM)
    sds = jax.ShapeDtypeStruct
    dma = pltpu.SemaphoreType.DMA
    V = pltpu.VMEM
    act, tok, packed, piece = (4, ROWS, 768), (4, 384, 768), (4, BLOCK, 384), (96, 768)
    return pl.pallas_call(backward_kernel,
        out_shape=[sds(packed, BF16), sds(packed, BF16), sds((2,) + piece, F32), sds((SMALL, 768), F32)],
        in_specs=[any_] * 10 + [vmem] * 4, out_specs=[any_] * 2 + [vmem] * 2,
        scratch_shapes=[V((2, 2, 8, 96, 768), BF16), V((4,) + act, BF16), V((4,) + act, BF16), V(act, F32), V(act, BF16), V(act, BF16),
            V(tok, BF16), V(tok, BF16), V((768, 4 * ROWS), BF16), V((768, 4 * ROWS), BF16), V(act, F32),
            V((2, 4, 8, 96, 768), BF16), V((3, 4 * BLOCK, 128), F32), V(packed, BF16),
            V((2, 4, 4) + piece, BF16), V((2, 4) + piece, BF16), V((2, 4) + piece, BF16), V((2, 4) + piece, BF16), V((2, 4) + piece, BF16),
            V((SMALL, 768), F32), V((4 * PIECE, 768), F32), V((3, PIECE, 768), F32), V((4, PIECE // 2, 384), F32), V((PIECE, 768), F32),
            dma((14,)), dma((2,)), dma((2,)), dma((3,)), dma((4,)), dma((3,)), dma((4,)), dma((2, 4, 4)), dma((2, 4, 4)), dma((2, 4, 3)), dma((2, 4, 3)),
            dma((2, 4)), dma((2, 4)), dma, dma, dma((3,)), dma((3,)), dma((3,)), dma((4,)), dma((3,)), dma((4,)), dma((3,)), dma((4,)), dma((4,)), dma((4,))],
        compiler_params=pltpu.CompilerParams(collective_id=2, has_side_effects=True, vmem_limit_bytes=62 << 20))(*operands)


def finish_kernel(bound, o, dx, grads, total, o_stored, dx_stored, d1, d2, tok1, tok2, bias1, bias2, inner, outer, sizes, gain1, shift1, gain2, shift2, flat, wide, t3):
    t = lax.axis_index("tp")
    spread(o, flat)
    to_stored(flat, o_stored)
    spread(dx, wide)
    to_stored(wide, dx_stored)
    d1[...] = grads[0]
    d2[...] = grads[1]
    for start, dst in ((0, tok1), (384, tok2)):
        for j in range(3):
            lanes = slice(start + 128 * j, start + 128 * j + 128)
            t3[j, pl.ds(0, HALF, stride=2), :] = total[0:HALF, lanes]
            t3[j, pl.ds(1, HALF, stride=2), :] = total[GAP : GAP + HALF, lanes]
        for j in range(3):
            dst[:, 128 * j : 128 * j + 128] = t3[j]
    bias1[...] = total[HALF : HALF + 1, 0:384].reshape(384)
    for k in range(4):
        inner[pl.ds(768 * k, 768)] = total[HALF + 1 + k : HALF + 2 + k, :].reshape(768)
    column = jnp.broadcast_to(total[204:205, 0:ROWS], (128, ROWS)).T
    t3[0, pl.ds(0, HALF, stride=2), :] = column[0:HALF]
    t3[0, pl.ds(1, HALF, stride=2), :] = column[GAP : GAP + HALF]
    bias2[...] = t3[0].T[0:1].reshape(S)
    outer[...] = total[205:206, :].reshape(768)
    gg, gb = total[208:272, :], total[272:336, :]
    size = jnp.sqrt(jnp.sum(gg * gg + gb * gb, -1, keepdims=True))
    factor = bound / jnp.maximum(size, bound)
    sizes[...] = jnp.broadcast_to(size, (GROUPS, 128)).T[0:1].reshape(GROUPS)

    def own(v, dst):
        picked = jnp.zeros((1, 192), F32)
        for q in range(4):
            picked = jnp.where(t == q, v[:, 192 * q : 192 * q + 192], picked)
        dst[...] = picked.reshape(192)

    own(total[202:203, :], gain1)
    own(total[203:204, :], shift1)
    own(jnp.sum(factor * gg, 0, keepdims=True), gain2)
    own(jnp.sum(factor * gb, 0, keepdims=True), shift2)


def finish(bound, *operands):
    vmem = pl.BlockSpec(memory_space=pltpu.VMEM)
    shapes = [(16, HALF * 384)] * 2 + [(96, 768)] * 2 + [(S, 384)] * 2 + [(384,), (S,), (3072,), (768,), (GROUPS,)] + [(192,)] * 4
    return pl.pallas_call(functools.partial(finish_kernel, bound),
        out_shape=[jax.ShapeDtypeStruct(v, BF16 if n < 2 else F32) for n, v in enumerate(shapes)],
        in_specs=[vmem] * 4, out_specs=[vmem] * len(shapes),
        scratch_shapes=[pltpu.VMEM((3, 4 * BLOCK, 128), F32), pltpu.VMEM((3, 4 * BLOCK, 128), F32), pltpu.VMEM((3, S, 128), F32)],
        compiler_params=pltpu.CompilerParams(vmem_limit_bytes=32 << 20))(*operands)


epsilon = 1e-06
highest = lax.Precision.HIGHEST


def normalised(values):
    average = jnp.mean(values, -1, keepdims=True)
    inverse = lax.rsqrt(jnp.mean(values * values, -1, keepdims=True) - average * average + epsilon)
    return (values - average) * inverse, inverse


def norm_back(grad_hat, normed, inverse):
    return inverse * (
        grad_hat - jnp.mean(grad_hat, -1, keepdims=True) - normed * jnp.mean(grad_hat * normed, -1, keepdims=True)
    )


def general(block_in, ln1_gain, ln1_shift, tok_w1, tok_b1, tok_w2, tok_b2, ln2_gain, ln2_shift,
               ch_w1, ch_b1, ch_w2, ch_b2, group_ids, out_grad):
    f32 = jnp.float32
    bf16 = jnp.bfloat16
    tp = lax.axis_size("tp")
    dp = lax.axis_size("dp")
    held = block_in.shape[0]
    images = held // tp
    width = block_in.shape[2] // S
    full = width * tp
    t = lax.axis_index("tp")

    def whole_images(stored):
        got = lax.all_to_all(stored.reshape(tp, images, S * width), "tp", 0, 0, tiled=True)
        return got.reshape(tp, images, S, width).transpose(1, 2, 0, 3).reshape(images, S, full)

    def stored(values):
        parts = values.reshape(images, S, tp, width).transpose(2, 0, 1, 3).reshape(tp, images, S * width)
        return lax.all_to_all(parts, "tp", 0, 0, tiled=True).reshape(held, 1, S * width)

    rows = ch_w1.shape[0]
    shard = jnp.stack([ch_w1.astype(bf16), ch_w2.T.astype(bf16)])
    gathered = lax.all_gather(lax.all_gather(shard, "tp", axis=1), "dp", axis=2)
    gathered = gathered.reshape(2, tp, dp * rows, shard.shape[2])
    norms = lax.all_gather(jnp.stack([ln1_gain, ln1_shift, ln2_gain, ln2_shift]), "tp", axis=1, tiled=True)
    x = whole_images(block_in).astype(f32)
    dz_low = whole_images(out_grad)
    token_w1 = tok_w1.astype(bf16)
    token_w2 = tok_w2.astype(bf16)
    xhat, inv_x = normalised(x)
    mixed = (xhat * norms[0] + norms[1]).astype(bf16)
    pre = jnp.einsum("nsc,sk->nkc", mixed, token_w1, preferred_element_type=f32) + tok_b1[:, None]
    hidden, hidden_back = jax.vjp(jax.nn.gelu, pre)
    hidden = hidden.astype(bf16)
    u = x + jnp.einsum("nkc,ks->nsc", hidden, token_w2, preferred_element_type=f32) + tok_b2[:, None]
    uhat, inv_u = normalised(u)
    count = images * S
    hn = (uhat * norms[2] + norms[3]).astype(bf16).reshape(count, full)
    dz = dz_low.reshape(count, full)
    z = jnp.zeros((count, full), f32)
    dhn = jnp.zeros((count, full), f32)
    grads1, grads2, bias = [], [], []
    inner = shard.shape[2]
    for j in range(tp):
        q = jnp.dot(hn, gathered[0, j], preferred_element_type=f32) + ch_b1[j * inner : (j + 1) * inner]
        g, g_back = jax.vjp(jax.nn.gelu, q)
        g = g.astype(bf16)
        z = z + jnp.einsum("rh,ch->rc", g, gathered[1, j], preferred_element_type=f32)
        dg = jnp.dot(dz, gathered[1, j], preferred_element_type=f32)
        dq = g_back(dg)[0].astype(bf16)
        grads2.append(jnp.einsum("rc,rh->ch", dz, g, preferred_element_type=f32).astype(bf16))
        grads1.append(jnp.einsum("rc,rh->ch", hn, dq, preferred_element_type=f32).astype(bf16))
        bias.append(jnp.sum(dq.astype(f32), 0))
        dhn = dhn + jnp.einsum("rh,ch->rc", dq, gathered[0, j], preferred_element_type=f32)
    z = (z + ch_b2).astype(bf16).astype(f32).reshape(u.shape)
    block_out = stored((u + z).astype(bf16))
    dhn = dhn.reshape(u.shape)
    dz32 = dz_low.astype(f32)
    image_gain = jnp.sum(dhn * uhat, 1)
    image_shift = jnp.sum(dhn, 1)
    du = dz32 + norm_back(dhn * norms[2], uhat, inv_u)
    dp_low = du.astype(bf16)
    dh = jnp.einsum("nsc,ks->nkc", dp_low, token_w2, preferred_element_type=f32)
    d_tok_w2 = jnp.einsum("nkc,nsc->ks", hidden, dp_low, preferred_element_type=f32)
    d_tok_b2 = jnp.sum(dp_low.astype(f32), (0, 2))
    dpre = hidden_back(dh)[0].astype(bf16)
    d_tok_w1 = jnp.einsum("nsc,nkc->sk", mixed, dpre, preferred_element_type=f32)
    d_tok_b1 = jnp.sum(dpre.astype(f32), (0, 2))
    da = jnp.einsum("nkc,sk->nsc", dpre, token_w1, preferred_element_type=f32)
    d_gain1 = jnp.sum(da * xhat, (0, 1))
    d_shift1 = jnp.sum(da, (0, 1))
    dx = stored((du + norm_back(da * norms[0], xhat, inv_x)).astype(bf16))

    gradient = jnp.stack([jnp.stack(grads1), jnp.stack(grads2)]).reshape(2, tp, dp, rows, inner)
    owned = lax.psum_scatter(lax.psum_scatter(gradient, "tp", scatter_dimension=1, tiled=True).astype(bf16), "dp", scatter_dimension=2, tiled=True)
    owned = owned.astype(f32).reshape(2, rows, inner)

    ids = lax.dynamic_slice_in_dim(group_ids, t * images, images)
    member = (ids[:, None] == jnp.arange(GROUPS)[None, :]).astype(f32)
    groups = jnp.dot(member.T, jnp.concatenate([image_gain, image_shift], 1), precision=highest)
    flat = [d_tok_w1, d_tok_w2, jnp.stack(bias), jnp.sum(dz32, (0, 1)), d_gain1, d_shift1, d_tok_b1, d_tok_b2, groups]
    sizes = [v.size for v in flat]
    need = sum(sizes)
    unit = 64 * full
    padded = -(-need // unit) * unit
    packed = jnp.concatenate([v.reshape(-1) for v in flat] + [jnp.zeros((padded - need,), f32)]).reshape(-1, full)
    total = lax.psum(packed, ("dp", "tp"))
    total = total.reshape(-1)
    pieces, start = [], 0
    for v in flat:
        pieces.append(total[start : start + v.size].reshape(v.shape))
        start += v.size
    tw1, tw2, cb1, cb2, g1, s1, tb1, tb2, gg = pieces
    gg = gg.reshape(GROUPS, 2, full)
    group_norms = jnp.sqrt(jnp.sum(gg * gg, (1, 2)))
    bound = 2.0 * math.sqrt(held * dp * S * full / GROUPS)
    factor = bound / jnp.maximum(group_norms, bound)
    clipped = jnp.sum(factor[:, None, None] * gg, 0)

    def mine(v):
        return lax.dynamic_slice_in_dim(v, t * width, width)

    return (block_out, dx, group_norms, mine(g1), mine(s1), tw1, tb1, tw2, tb2, mine(clipped[0]), mine(clipped[1]),
            owned[0], cb1.reshape(-1), owned[1].T, cb2)


def blocked(block_in, ln1_gain, ln1_shift, tok_w1, tok_b1, tok_w2, tok_b2, ln2_gain, ln2_shift,
            ch_w1, ch_b1, ch_w2, ch_b2, group_ids, out_grad):
    held = block_in.shape[0]
    bound = 2.0 * math.sqrt(held * 8 * S * 768 / GROUPS)
    flat = (held, HALF * 384)
    w, g, s, u, hn, x, dz, h, ts, op, norms, w1, w2 = forward_pass(
        ch_w1, ch_w2.T, block_in.reshape(flat), out_grad.reshape(flat), ln1_gain, ln1_shift, ln2_gain, ln2_shift,
        tok_w1, tok_w2.T, tok_b1, tok_b2, ch_b1, ch_b2)
    out, dx, grads, total = backward_pass(w, g, s, u, hn, x, dz, h, ts, op, norms, w1, w2, group_ids)
    out, dx, d1, d2, tok1, tok2, bias1, bias2, inner, outer, sizes, gain1, shift1, gain2, shift2 = finish(bound, out, dx, grads, total)
    shape = block_in.shape
    return (out.reshape(shape), dx.reshape(shape), sizes, gain1, shift1, tok1, bias1, tok2.T, bias2,
            gain2, shift2, d1, inner, d2.T, outer)


def solution(mesh):
    stored, own, copied = P("dp", "tp", None), P("tp"), P()
    in_specs = (stored, own, own, copied, copied, copied, copied, own, own, P("dp", "tp"), copied, P("tp", "dp"), copied, P("dp"), stored)
    out_specs = (stored, stored, copied, own, own, copied, copied, copied, copied, own, own, P("dp", "tp"), copied, P("tp", "dp"), copied)
    step = blocked if (mesh.shape["dp"], mesh.shape["tp"]) == (8, 4) else general
    return jax.shard_map(step, mesh=mesh, in_specs=in_specs, out_specs=out_specs, check_vma=False)
```

```python
import functools
import math

import jax
import jax.numpy as jnp
from jax import lax
from jax.experimental import pallas as pl
from jax.experimental.pallas import tpu as pltpu
from jax.sharding import PartitionSpec as P

MESH = pl.DeviceIdType.MESH


S = 196
GROUPS = 64
F32 = jnp.float32
BF16 = jnp.bfloat16
HALF = 98
GAP = 104
ROWS = 208
BLOCK = 4 * HALF
LOW = math.sqrt(2.0 / math.pi)
CUBE = 0.044715


def place():
    dp = lax.axis_index("dp")
    t = lax.axis_index("tp")
    c, x, y = dp % 2, (dp // 2) % 2, dp // 4
    near = dict(S=owner(y, x, 1 - c), X=owner(y, 1 - x, c), Y=owner(1 - y, x, c), D=owner(1 - y, 1 - x, c))
    return dp, t, near, (y, x, c)


def owner(y, x, c):
    return (y * 2 + x) * 2 + c


def others(t):
    first = jnp.where(t == 0, 1, jnp.where(t == 1, 0, jnp.where(t == 2, 3, 2)))
    second = jnp.where(t == 0, 2, jnp.where(t == 1, 2, 1))
    third = jnp.where(t < 2, 3, 0)
    return [first, second, third]


def meet(devices):
    barrier = pltpu.get_barrier_semaphore()
    for device in devices:
        pl.semaphore_signal(barrier, inc=1, device_id=device, device_id_type=MESH)
    pl.semaphore_wait(barrier, len(devices))


def remote(src, dst, ss, rs, device):
    return pltpu.make_async_remote_copy(src_ref=src, dst_ref=dst, send_sem=ss, recv_sem=rs, device_id=device, device_id_type=MESH)


def gelu_pair(v):
    square = v * v
    up = 0.5 * jnp.tanh(v * (LOW + (LOW * CUBE) * square)) + 0.5
    value = v * up
    slope = up + value * (1.0 - up) * (2.0 * LOW + (6.0 * LOW * CUBE) * square)
    return value, slope


def turn(v):
    return pltpu.roll(v, 64, 1)


def lane_low():
    return lax.broadcasted_iota(jnp.int32, (HALF, 128), 1) < 64


def join_groups(flat, image, store):
    low = lane_low()
    for p in range(2):
        a = [flat[j, pl.ds(2 * p * BLOCK + image * HALF, HALF), :] for j in range(3)]
        b = [flat[j, pl.ds((2 * p + 1) * BLOCK + image * HALF, HALF), :] for j in range(3)]
        a1, a2, b0, b1 = turn(a[1]), turn(a[2]), turn(b[0]), turn(b[1])
        even = [a[0], jnp.where(low, a[1], b0), jnp.where(low, b0, b1)]
        odd = [jnp.where(low, a1, a2), jnp.where(low, a2, b[1]), b[2]]
        for j in range(3):
            store(0, 384 * p + 128 * j, even[j])
            store(GAP, 384 * p + 128 * j, odd[j])


def split_groups(load, flat, image):
    low = lane_low()
    for p in range(2):
        e = [load(0, 384 * p + 128 * j) for j in range(3)]
        o = [load(GAP, 384 * p + 128 * j) for j in range(3)]
        e1, e2, o0, o1 = turn(e[1]), turn(e[2]), turn(o[0]), turn(o[1])
        a = [e[0], jnp.where(low, e[1], o0), jnp.where(low, o0, o1)]
        b = [jnp.where(low, e1, e2), jnp.where(low, e2, o[1]), o[2]]
        for j in range(3):
            flat[j, pl.ds(2 * p * BLOCK + image * HALF, HALF), :] = a[j]
            flat[j, pl.ds((2 * p + 1) * BLOCK + image * HALF, HALF), :] = b[j]


def spread(packed, flat):
    for k in range(4):
        for j in range(3):
            flat[j, pl.ds(k * BLOCK, BLOCK), :] = packed[k, :, 128 * j : 128 * j + 128].astype(F32)


def pack(flat, packed):
    for k in range(4):
        for j in range(3):
            packed[k, :, 128 * j : 128 * j + 128] = flat[j, pl.ds(k * BLOCK, BLOCK), :].astype(BF16)


def to_rows(stored, flat):
    for i in range(HALF):
        for j in range(3):
            start = 384 * i + 128 * j
            flat[j, pl.ds(i, 16, stride=HALF), :] = stored[:, start : start + 128].astype(F32)


def to_stored(flat, stored):
    for i in range(HALF):
        for j in range(3):
            start = 384 * i + 128 * j
            stored[:, start : start + 128] = flat[j, pl.ds(i, 16, stride=HALF), :].astype(BF16)


def hat(v):
    average = jnp.mean(v, -1, keepdims=True)
    inverse = lax.rsqrt(jnp.mean(v * v, -1, keepdims=True) - average * average + 1e-06)
    return (v - average) * inverse, inverse


def dot(a, b):
    return jnp.dot(a, b, preferred_element_type=F32)


def dot_nt(a, b):
    return lax.dot_general(a, b, (((1,), (1,)), ((), ())), preferred_element_type=F32)


PIECE = 48
SMALL = 8 * PIECE
DIRECT = (0, 1)


def step_kernel(cw1, cw2, xin, din, p0, p1, p2, p3, tw1, tw2, b1, b2, cb1, cb2, ids,
                o_out, dx_out, w_grad, total_out,
                wf, shard, wv, stored, xs, ds, xr, dr, flat, xb, u, act, hnt, dzt, g, s, h, ts, zs, lr, lall, t3, c2, w1, w2, w1t, w2t,
                sib, first, second, final, zz, small, low, t_sib, t_chip, t_line,
                send_sem, recv_sem, line_sem, x_send, x_recv, d_send, d_recv, ln_send, ln_recv, in_sem, own_sem,
                o_send, o_recv, y_send, y_recv, sib_sem, sib_recv, a_send, a_recv, z_send, z_recv,
                p_send, p_recv, c_send, c_recv, l_send, l_recv, b_send, b_recv, e_send, e_recv):
    dp, t, near, (y, xx, c) = place()
    line = others(t)
    order = [t] + line
    back = [line[2], line[1], line[0], t]
    chips = {"O": (y, xx), "X": (y, 1 - xx), "Y": (1 - y, xx), "D": (1 - y, 1 - xx)}
    slot = {"O": 0, "X": 1, "Y": 2, "D": 3}
    started = {"w": [], "x": [], "y": [], "": []}
    maybe = []
    state = {}
    zero = jnp.zeros((1, 768), F32)

    def go(copy, kind=""):
        copy.start()
        started[kind].append(copy)

    def local(src, dst, sem):
        copy = pltpu.make_async_copy(src, dst, sem)
        copy.start()
        return copy

    def sent(kind):
        for copy in started[kind]:
            copy.wait_send()
        started[kind] = []

    in_w1, in_w2 = local(cw1, wf.at[0], in_sem.at[0]), local(cw2, wf.at[1], in_sem.at[1])
    state["in"] = local(xin, stored, in_sem.at[2])
    meet([(near["S"], t), (near["X"], t), (near["Y"], t), (near["D"], t)] + [(dp, p) for p in line])
    sends = [0, 0]


    def send(src, who, tt, device):
        go(remote(src, wv.at[:, tt, who], send_sem.at[sends[0]], recv_sem.at[who, tt], device), "w")
        sends[0] += 1

    def along(src, tt, target):
        inside = (target >= 0) & (target <= 3)
        copy = remote(src, wv.at[:, tt, dp], line_sem.at[sends[1]], recv_sem.at[dp, tt], (dp, jnp.clip(target, 0, 3)))
        sends[1] += 1
        pl.when(inside)(copy.start)
        maybe.append((inside, copy))

    def arrived(who, tt):
        ref = wv.at[:, tt, who]
        remote(ref, ref, send_sem.at[0], recv_sem.at[who, tt], (dp, t)).wait_recv()

    def weights():
        in_w1.wait()
        in_w2.wait()
        shard[...] = wf[...].astype(BF16)
        along(shard, t, t + 1)
        along(shard, t, t - 1)
        for name in "XYS":
            send(shard, dp, t, (near[name], t))
        wv[:, t, dp] = shard[...]
        for n, ref in enumerate((p0, p1, p2, p3)):
            row = ref[...].reshape(1, 192)
            wide = jnp.concatenate([row, row, row, row], 1)
            lane = lax.broadcasted_iota(jnp.int32, (1, 768), 1)
            lr[t, n : n + 1, :] = jnp.where((lane >= 192 * t) & (lane < 192 * t + 192), wide, 0.0)
        for n, p in enumerate(line):
            go(remote(lr.at[t], lr.at[t], ln_send.at[n], ln_recv.at[t], (dp, p)))

    def column(k):
        tt = order[k]
        arrived(dp, tt)
        src = wv.at[:, tt, dp]
        along(src, tt, jnp.where(tt < t, t + 1, t - 1))
        for name in "XYS":
            send(src, dp, tt, (near[name], t))

    def neighbours(k):
        tt = order[k]
        one, two = ("X", "Y") if k % 2 == 0 else ("Y", "X")
        arrived(near[one], tt)
        src = wv.at[:, tt, near[one]]
        send(src, near[one], tt, (near[two], t))
        send(src, near[one], tt, (near["S"], t))
        arrived(near[two], tt)
        send(wv.at[:, tt, near[two]], near[two], tt, (near["S"], t))

    def diagonal(k):
        tt = order[k]
        arrived(near["D"], tt)
        send(wv.at[:, tt, near["D"]], near["D"], tt, (near["S"], t))


    def pack_input():
        state["in"].wait()
        to_rows(stored, flat)
        pack(flat, xs)
        state["in"] = local(din, stored, in_sem.at[3])

    def send_input(n):
        p = line[n]
        go(remote(xs.at[p], xr.at[t], x_send.at[n], x_recv.at[t], (dp, p)), "x")

    def pack_grad():
        state["in"].wait()
        to_rows(stored, flat)
        pack(flat, ds)

    def send_grad(n):
        p = line[n]
        go(remote(ds.at[p], dr.at[t], d_send.at[n], d_recv.at[t], (dp, p)), "y")

    def token_weights():
        gap = jnp.zeros((GAP - HALF, 128), F32)
        for n, (src, dst) in enumerate(((tw1, w1), (tw2, w2t))):
            for j in range(3):
                t3[j] = src[:, 128 * j : 128 * j + 128]
            for j in range(3):
                even, odd = t3[j, pl.ds(0, HALF, stride=2), :], t3[j, pl.ds(1, HALF, stride=2), :]
                dst[:, 128 * j : 128 * j + 128] = jnp.concatenate([even, gap, odd, gap], 0).astype(BF16)
        w1t[...] = w1[...].T
        w2[...] = w2t[...].T
        c2[...] = jnp.broadcast_to(b2[...].reshape(1, S), (128, S)).T
        few = jnp.zeros((GAP - HALF, 1), F32)
        state["shift2"] = jnp.concatenate([c2[pl.ds(0, HALF, stride=2), :][:, 0:1], few, c2[pl.ds(1, HALF, stride=2), :][:, 0:1], few], 0)
        state["shift1"] = jnp.broadcast_to(b1[...].reshape(1, 384), (8, 384)).T[:, 0:1]
        small[...] = jnp.zeros((SMALL, 768), F32)

    def join(received, own, dst):
        received[t] = own[t]
        spread(received, flat)
        few = jnp.zeros((GAP - HALF, 768), F32)
        for n in range(4):
            for start in (HALF, GAP + HALF):
                zs[n, start : start + GAP - HALF, :] = few

            def put(row, lane, v, n=n):
                zs[n, row : row + HALF, lane : lane + 128] = v

            join_groups(flat, n, put)
            dst[n] = zs[n].astype(BF16)

    def join_input():
        for p in line:
            remote(lr.at[p], lr.at[p], ln_send.at[0], ln_recv.at[p], (dp, t)).wait_recv()
        lall[...] = (lr[0] + lr[1]) + (lr[2] + lr[3])
        for p in line:
            remote(xr.at[p], xr.at[p], x_send.at[0], x_recv.at[p], (dp, t)).wait_recv()
        join(xr, xs, xb)

    def token_forward(start, stop):
        g1, s1, g2, s2 = lall[0:1], lall[1:2], lall[2:3], lall[3:4]
        shift1, shift2 = state["shift1"], state["shift2"]

        def body(n, carry):
            v = xb[n].astype(F32)
            xhat, _ = hat(v)
            a = (xhat * g1 + s1).astype(BF16)
            value, slope = gelu_pair(dot(w1t[...], a) + shift1)
            low = value.astype(BF16)
            h[n] = low
            ts[n] = slope.astype(BF16)
            r = v + dot(w2t[...], low) + shift2
            u[n] = r
            uhat, _ = hat(r)
            act[n] = (uhat * g2 + s2).astype(BF16)
            return carry

        lax.fori_loop(start, stop, body, 0)

    def block(k):
        tt = order[k]
        for name in "OXYD":
            arrived(owner(*chips[name], 1 - c), tt)
        bias = cb1[pl.ds(pl.multiple_of(tt * 768, 128), 768)].reshape(1, 768)

        def body(n, carry):
            value, slope = gelu_pair(dot(act[n], wv[0, tt].reshape(768, 768)) + bias)
            low = value.astype(BF16)
            g[tt, n] = low
            s[tt, n] = slope.astype(BF16)
            part = dot_nt(low, wv[1, tt].reshape(768, 768))
            if k == 0:
                zs[n] = part
            elif k < 3:
                zs[n] += part
            else:
                zs[n] = u[n] + (zs[n] + part + cb2[...].reshape(1, 768)).astype(BF16).astype(F32)
            return carry

        lax.fori_loop(0, 4, body, 0)

    def pack_output():
        for n in range(4):
            split_groups(lambda row, lane, n=n: zs[n, row : row + HALF, lane : lane + 128], flat, n)
        sent("x")
        pack(flat, xs)
        state["own_o"] = local(xs.at[t], o_out.at[t], own_sem.at[0])

    def send_output(n):
        p = line[n]
        go(remote(xs.at[p], o_out.at[t], o_send.at[n], o_recv.at[t], (dp, p)))

    def hidden_in():
        for n in range(4):
            hnt[:, n * ROWS : (n + 1) * ROWS] = act[n].T

    def join_grad():
        for p in line:
            remote(dr.at[p], dr.at[p], d_send.at[0], d_recv.at[p], (dp, t)).wait_recv()
        join(dr, ds, act)
        for n in range(4):
            dzt[:, n * ROWS : (n + 1) * ROWS] = act[n].T
        sent("w")
        for inside, copy in maybe:
            pl.when(inside)(copy.wait_send)
        maybe.clear()


    def hand_over(j, k):
        for name in "DXYO":
            n = slot[name]
            go(remote(wv.at[j, back[k], owner(*chips[name], 1 - c)], sib.at[j, k, n], sib_sem.at[j, k, n], sib_recv.at[j, k, n], (near["S"], t)))

    def chip_sum(j, k, name):
        n = slot[name]
        remote(sib.at[j, k, n], sib.at[j, k, n], sib_sem.at[j, k, n], sib_recv.at[j, k, n], (near["S"], t)).wait_recv()
        sib[j, k, n] = wv[j, back[k], owner(*chips[name], c)] + sib[j, k, n]

    def ways(k):
        return ("X", "Y") if k % 2 == 0 else ("Y", "X")

    def hop(j, k, src, dst, n, name):
        go(remote(src, dst, a_send.at[j, k, n], a_recv.at[j, k, n], (near[name], t)))

    def landed(j, k, dst, n):
        remote(dst, dst, a_send.at[j, k, n], a_recv.at[j, k, n], (near["S"], t)).wait_recv()

    def stage_one(j, k):
        f, s2 = ways(k)
        chip_sum(j, k, "D")
        hop(j, k, sib.at[j, k, 3], first.at[j, k], 0, s2)
        chip_sum(j, k, s2)
        hop(j, k, sib.at[j, k, slot[s2]], second.at[j, k], 1, s2)

    def stage_two(j, k):
        f, s2 = ways(k)
        n = slot[f]
        chip_sum(j, k, f)
        landed(j, k, first.at[j, k], 0)
        sib[j, k, n] = sib[j, k, n] + first[j, k]
        hop(j, k, sib.at[j, k, n], final.at[j, k], 2, f)

    def stage_three(j, k):
        chip_sum(j, k, "O")
        landed(j, k, second.at[j, k], 1)
        landed(j, k, final.at[j, k], 2)
        total = sib[j, k, 0].astype(F32) + second[j, k].astype(F32) + final[j, k].astype(F32)
        if k < 3:
            sib[j, k, 0] = total.astype(BF16)
            if j in DIRECT:
                go(remote(sib.at[j, k, 0], zz.at[j, t], z_send.at[j, k], z_recv.at[j, t], (dp, back[k])))
        else:
            w_grad[j] = total

    def along_in(j, n):
        remote(zz.at[j, n], zz.at[j, n], z_send.at[j, 0], z_recv.at[j, n], (dp, t)).wait_recv()

    def stage_four(j, k):
        p = back[k]
        piece = sib.at[j, k, 0]
        up = remote(piece, zz.at[j, p], z_send.at[j, k], z_recv.at[j, p], (dp, jnp.clip(t + 1, 0, 3)))
        n = jnp.where(t - 1 == p, 4, p)
        down = remote(piece, zz.at[j, n], z_send.at[j, k], z_recv.at[j, n], (dp, jnp.clip(t - 1, 0, 3)))

        @pl.when(((p > t) & (t > 0)) | ((p < t) & (t < 3)))
        def _():
            along_in(j, p)
            piece[...] = piece[...] + zz[j, p]

        pl.when(p > t)(up.start)
        pl.when(p < t)(down.start)
        maybe.append((p > t, up))
        maybe.append((p < t, down))

    def stage_five(j):
        if j in DIRECT:
            for p in line:
                along_in(j, p)
                w_grad[j] += zz[j, p].astype(F32)
            return

        @pl.when(t > 0)
        def _():
            along_in(j, t)
            w_grad[j] += zz[j, t].astype(F32)

        @pl.when(t < 3)
        def _():
            along_in(j, 4)
            w_grad[j] += zz[j, 4].astype(F32)

    def second_weight(k):
        wv[1, back[k]] = dot(dzt[...], g[back[k]].reshape(4 * ROWS, 768)).astype(BF16).reshape(8, 96, 768)
        hand_over(1, k)

    def data(k):
        tt = back[k]

        def body(n, bias):
            low = (dot(act[n], wv[1, tt].reshape(768, 768)) * s[tt, n].astype(F32)).astype(BF16)
            s[tt, n] = low
            part = dot_nt(low, wv[0, tt].reshape(768, 768))
            if k == 0:
                zs[n] = part
            else:
                zs[n] += part
            return bias + jnp.sum(low.astype(F32), 0, keepdims=True)

        small[pl.ds(HALF + 1 + tt, 1), :] = lax.fori_loop(0, 4, body, zero)

    def first_weight(k):
        wv[0, back[k]] = dot(hnt[...], s[back[k]].reshape(4 * ROWS, 768)).astype(BF16).reshape(8, 96, 768)
        hand_over(0, k)

    def token_backward(start, stop):
        g1, s1, g2 = lall[0:1], lall[1:2], lall[2:3]
        row = lax.broadcasted_iota(jnp.int32, (ROWS, 768), 0)
        ones = jnp.ones((8, 768), BF16)
        groups = lax.broadcasted_iota(jnp.int32, (GROUPS, 16), 0) == ids[...].reshape(1, 16)
        lane = lax.broadcasted_iota(jnp.int32, (GROUPS, 16), 1)

        def body(n, carry):
            sum_g1, sum_s1, sum_b2, sum_dz = carry
            d, grad = zs[n], act[n].astype(F32)
            uhat, inv_u = hat(u[n])
            member = jnp.sum(jnp.where(groups & (lane == 4 * t + n), 1.0, 0.0), -1, keepdims=True)
            small[208:272, :] += member * jnp.sum(d * uhat, 0, keepdims=True)
            small[272:336, :] += member * jnp.sum(d, 0, keepdims=True)
            e = d * g2
            du = grad + inv_u * (e - jnp.mean(e, -1, keepdims=True) - uhat * jnp.mean(e * uhat, -1, keepdims=True))
            low = du.astype(BF16)
            dpre = (dot(w2[...], low) * ts[n].astype(F32)).astype(BF16)
            xhat, inv_x = hat(xb[n].astype(F32))
            a = jnp.where(row == HALF, 1.0, xhat * g1 + s1).astype(BF16)
            tok1 = dot_nt(a, dpre)
            tok2 = dot_nt(low, h[n])
            for begin, size in ((0, HALF + 1), (GAP, HALF)):
                small[begin : begin + size, 0:384] += tok1[begin : begin + size]
            for begin, size in ((0, HALF), (GAP, HALF)):
                small[begin : begin + size, 384:768] += tok2[begin : begin + size]
            da = dot(w1[...], dpre)
            e1 = da * g1
            zs[n] = du + inv_x * (e1 - jnp.mean(e1, -1, keepdims=True) - xhat * jnp.mean(e1 * xhat, -1, keepdims=True))
            return (sum_g1 + jnp.sum(da * xhat, 0, keepdims=True), sum_s1 + jnp.sum(da, 0, keepdims=True),
                    sum_b2 + dot_nt(ones, low), sum_dz + jnp.sum(grad, 0, keepdims=True))

        sums = state.get("sums", (zero, zero, jnp.zeros((8, ROWS), F32), zero))
        state["sums"] = lax.fori_loop(start, stop, body, sums)

    def pack_dx():
        for n in range(4):
            split_groups(lambda r, lane, n=n: zs[n, r : r + HALF, lane : lane + 128], flat, n)
        sent("y")
        pack(flat, ds)
        state["own_x"] = local(ds.at[t], dx_out.at[t], own_sem.at[1])

    def send_dx(n):
        p = line[n]
        go(remote(ds.at[p], dx_out.at[t], y_send.at[n], y_recv.at[t], (dp, p)))

    chip = dp // 2
    far = [("X", near["X"] // 2), ("Y", near["Y"] // 2), ("D", near["D"] // 2)]

    def part(ref, core, q):
        return ref.at[pl.ds(pl.multiple_of((core * 4 + q) * PIECE, 8), PIECE)]

    def half(ref, core):
        return ref.at[pl.ds(pl.multiple_of(core * 4 * PIECE, 8), 4 * PIECE)]

    own = part(total_out, c, chip)

    def total_zero():
        sum_g1, sum_s1, sum_b2, sum_dz = state["sums"]
        small[202:203, :] = sum_g1
        small[203:204, :] = sum_s1
        small[204:205, 0:ROWS] = sum_b2[0:1]
        small[205:206, :] = sum_dz
        half(low, 1 - c)[...] = half(small, 1 - c)[...].astype(BF16)
        go(remote(half(low, 1 - c), t_sib, p_send, p_recv, (near["S"], t)))

    def total_one():
        remote(t_sib, t_sib, p_send, p_recv, (near["S"], t)).wait_recv()
        both = half(small, c)[...] + t_sib[...].astype(F32)
        half(small, c)[...] = both
        half(low, c)[...] = both.astype(BF16)
        for n, (name, q) in enumerate(far):
            go(remote(part(low, c, q), t_chip.at[n], c_send.at[n], c_recv.at[n], (near[name], t)))

    def total_two():
        total = part(small, c, chip)[...]
        for n in range(3):
            remote(t_chip.at[n], t_chip.at[n], c_send.at[n], c_recv.at[n], (near["S"], t)).wait_recv()
            total = total + t_chip[n].astype(F32)
        t_line[t] = total.astype(BF16)
        for n, p in enumerate(line):
            go(remote(t_line.at[t], t_line.at[t], l_send.at[n], l_recv.at[t], (dp, p)))

    def total_three():
        for p in line:
            remote(t_line.at[p], t_line.at[p], l_send.at[0], l_recv.at[p], (dp, t)).wait_recv()
        sums = [t_line[p].astype(F32) for p in range(4)]
        own[...] = (((sums[0] + sums[1]) + sums[2]) + sums[3]).astype(BF16)
        for n, (name, q) in enumerate(far):
            go(remote(own, own, b_send.at[n], b_recv.at[chip], (near[name], t)))
        go(remote(own, own, e_send.at[3], e_recv.at[chip], (near["S"], t)))

    def total_five():
        for n, (name, q) in enumerate(far):
            there = part(total_out, c, q)
            remote(there, there, b_send.at[0], b_recv.at[q], (dp, t)).wait_recv()
            go(remote(there, there, e_send.at[n], e_recv.at[q], (near["S"], t)))

    def total_six():
        for q in range(4):
            there = part(total_out, 1 - c, q)
            remote(there, there, e_send.at[0], e_recv.at[q], (dp, t)).wait_recv()

    weights()
    pack_input()
    column(1)
    neighbours(0)
    column(2)
    send_input(0)
    send_input(1)
    send_input(2)
    neighbours(1)
    diagonal(0)
    column(3)
    pack_grad()
    token_weights()
    neighbours(2)
    diagonal(1)
    neighbours(3)
    diagonal(2)
    diagonal(3)
    join_input()
    send_grad(0)
    send_grad(1)
    send_grad(2)
    token_forward(0, 4)
    block(0)
    block(1)
    block(2)
    block(3)
    pack_output()
    send_output(0)
    send_output(1)
    send_output(2)
    hidden_in()
    join_grad()
    data(0)
    second_weight(0)
    data(1)
    second_weight(1)
    stage_one(1, 0)
    data(2)
    second_weight(2)
    stage_one(1, 1)
    data(3)
    second_weight(3)
    stage_one(1, 2)
    stage_one(1, 3)
    stage_two(1, 0)
    token_backward(0, 2)
    stage_two(1, 1)
    stage_two(1, 2)
    token_backward(2, 4)
    pack_dx()
    send_dx(0)
    send_dx(1)
    send_dx(2)
    total_zero()
    stage_two(1, 3)
    stage_three(1, 0)
    first_weight(0)
    total_one()
    first_weight(1)
    stage_three(1, 1)
    stage_one(0, 0)
    first_weight(2)
    stage_one(0, 1)
    first_weight(3)
    stage_one(0, 2)
    stage_three(1, 2)
    stage_one(0, 3)
    total_two()
    stage_three(1, 3)
    stage_two(0, 0)
    stage_two(0, 1)
    total_three()
    stage_two(0, 2)
    stage_two(0, 3)
    stage_three(0, 0)
    stage_three(0, 1)
    stage_three(0, 2)
    stage_three(0, 3)
    total_five()
    stage_five(1)
    stage_five(0)
    total_six()

    state["own_o"].wait()
    state["own_x"].wait()
    for p in line:
        remote(o_out.at[p], o_out.at[p], o_send.at[0], o_recv.at[p], (dp, t)).wait_recv()
        remote(dx_out.at[p], dx_out.at[p], y_send.at[0], y_recv.at[p], (dp, t)).wait_recv()
    sent("")
    for inside, copy in maybe:
        pl.when(inside)(copy.wait_send)


def one_step(*operands):
    any_, vmem = pl.BlockSpec(memory_space=pl.ANY), pl.BlockSpec(memory_space=pltpu.VMEM)
    sds = jax.ShapeDtypeStruct
    dma = pltpu.SemaphoreType.DMA
    V = pltpu.VMEM
    wshape, act, tok, packed, piece = (2, 4, 8, 96, 768), (4, ROWS, 768), (4, 384, 768), (4, BLOCK, 384), (96, 768)
    return pl.pallas_call(step_kernel,
        out_shape=[sds(packed, BF16), sds(packed, BF16), sds((2,) + piece, F32), sds((SMALL, 768), BF16)],
        in_specs=[any_] * 4 + [vmem] * 11, out_specs=[any_] * 2 + [vmem] * 2,
        scratch_shapes=[V((2, 96, 768), F32), V((2, 96, 768), BF16), V(wshape, BF16), V((16, HALF * 384), BF16), V(packed, BF16), V(packed, BF16),
            V(packed, BF16), V(packed, BF16), V((3, 4 * BLOCK, 128), F32), V(act, BF16), V(act, F32), V(act, BF16), V((768, 4 * ROWS), BF16), V((768, 4 * ROWS), BF16),
            V((4,) + act, BF16), V((4,) + act, BF16), V(tok, BF16), V(tok, BF16), V(act, F32), V((4, 8, 768), F32), V((8, 768), F32),
            V((3, S, 128), F32), V((S, 128), F32), V((ROWS, 384), BF16), V((384, ROWS), BF16), V((384, ROWS), BF16), V((ROWS, 384), BF16),
            V((2, 4, 4) + piece, BF16), V((2, 4) + piece, BF16), V((2, 4) + piece, BF16), V((2, 4) + piece, BF16), V((2, 5) + piece, BF16),
            V((SMALL, 768), F32), V((SMALL, 768), BF16), V((4 * PIECE, 768), BF16), V((3, PIECE, 768), BF16), V((4, PIECE, 768), BF16),
            dma((28,)), dma((8, 4)), dma((5,)), dma((3,)), dma((4,)), dma((3,)), dma((4,)), dma((3,)), dma((4,)), dma((4,)), dma((2,)),
            dma((3,)), dma((4,)), dma((3,)), dma((4,)), dma((2, 4, 4)), dma((2, 4, 4)), dma((2, 4, 3)), dma((2, 4, 3)), dma((2, 4)), dma((2, 5)),
            dma, dma, dma((3,)), dma((3,)), dma((3,)), dma((4,)), dma((3,)), dma((4,)), dma((4,)), dma((4,))],
        compiler_params=pltpu.CompilerParams(collective_id=1, has_side_effects=True, vmem_limit_bytes=63 << 20))(*operands)


def finish_kernel(bound, o_in, dx_in, grads_in, total_in, o_stored, dx_stored, d1, d2, tok1, tok2, bias1, bias2, inner, outer, sizes, gain1, shift1, gain2, shift2, o, dx, grads, low, flat, wide, t3, total, sems):
    t = lax.axis_index("tp")
    copies = [pltpu.make_async_copy(src, dst, sems.at[n]) for n, (src, dst) in enumerate(((total_in, low), (o_in, o), (dx_in, dx), (grads_in, grads)))]
    for copy in copies:
        copy.start()
    for copy in copies:
        copy.wait()
    total[...] = low[...].astype(F32)
    spread(o, flat)
    to_stored(flat, o_stored)
    spread(dx, wide)
    to_stored(wide, dx_stored)
    d1[...] = grads[0]
    d2[...] = grads[1]
    for start, dst in ((0, tok1), (384, tok2)):
        for j in range(3):
            lanes = slice(start + 128 * j, start + 128 * j + 128)
            t3[j, pl.ds(0, HALF, stride=2), :] = total[0:HALF, lanes]
            t3[j, pl.ds(1, HALF, stride=2), :] = total[GAP : GAP + HALF, lanes]
        for j in range(3):
            dst[:, 128 * j : 128 * j + 128] = t3[j]
    bias1[...] = total[HALF : HALF + 1, 0:384].reshape(384)
    for k in range(4):
        inner[pl.ds(768 * k, 768)] = total[HALF + 1 + k : HALF + 2 + k, :].reshape(768)
    column = jnp.broadcast_to(total[204:205, 0:ROWS], (128, ROWS)).T
    t3[0, pl.ds(0, HALF, stride=2), :] = column[0:HALF]
    t3[0, pl.ds(1, HALF, stride=2), :] = column[GAP : GAP + HALF]
    bias2[...] = t3[0].T[0:1].reshape(S)
    outer[...] = total[205:206, :].reshape(768)
    gg, gb = total[208:272, :], total[272:336, :]
    size = jnp.sqrt(jnp.sum(gg * gg + gb * gb, -1, keepdims=True))
    factor = bound / jnp.maximum(size, bound)
    sizes[...] = jnp.broadcast_to(size, (GROUPS, 128)).T[0:1].reshape(GROUPS)

    def own(v, dst):
        picked = jnp.zeros((1, 192), F32)
        for q in range(4):
            picked = jnp.where(t == q, v[:, 192 * q : 192 * q + 192], picked)
        dst[...] = picked.reshape(192)

    own(total[202:203, :], gain1)
    own(total[203:204, :], shift1)
    own(jnp.sum(factor * gg, 0, keepdims=True), gain2)
    own(jnp.sum(factor * gb, 0, keepdims=True), shift2)


def finish(bound, *operands):
    vmem = pl.BlockSpec(memory_space=pltpu.VMEM)
    shapes = [(16, HALF * 384)] * 2 + [(96, 768)] * 2 + [(S, 384)] * 2 + [(384,), (S,), (3072,), (768,), (GROUPS,)] + [(192,)] * 4
    return pl.pallas_call(functools.partial(finish_kernel, bound),
        out_shape=[jax.ShapeDtypeStruct(v, BF16 if n < 2 else F32) for n, v in enumerate(shapes)],
        in_specs=[pl.BlockSpec(memory_space=pl.ANY)] * 4, out_specs=[vmem] * len(shapes),
        scratch_shapes=[pltpu.VMEM((4, BLOCK, 384), BF16), pltpu.VMEM((4, BLOCK, 384), BF16), pltpu.VMEM((2, 96, 768), F32), pltpu.VMEM((SMALL, 768), BF16),
            pltpu.VMEM((3, 4 * BLOCK, 128), F32), pltpu.VMEM((3, 4 * BLOCK, 128), F32), pltpu.VMEM((3, S, 128), F32), pltpu.VMEM((SMALL, 768), F32), pltpu.SemaphoreType.DMA((4,))],
        compiler_params=pltpu.CompilerParams(vmem_limit_bytes=32 << 20))(*operands)


epsilon = 1e-06
highest = lax.Precision.HIGHEST


def normalised(values):
    average = jnp.mean(values, -1, keepdims=True)
    inverse = lax.rsqrt(jnp.mean(values * values, -1, keepdims=True) - average * average + epsilon)
    return (values - average) * inverse, inverse


def norm_back(grad_hat, normed, inverse):
    return inverse * (
        grad_hat - jnp.mean(grad_hat, -1, keepdims=True) - normed * jnp.mean(grad_hat * normed, -1, keepdims=True)
    )


def general(block_in, ln1_gain, ln1_shift, tok_w1, tok_b1, tok_w2, tok_b2, ln2_gain, ln2_shift,
               ch_w1, ch_b1, ch_w2, ch_b2, group_ids, out_grad):
    f32 = jnp.float32
    bf16 = jnp.bfloat16
    tp = lax.axis_size("tp")
    dp = lax.axis_size("dp")
    held = block_in.shape[0]
    images = held // tp
    width = block_in.shape[2] // S
    full = width * tp
    t = lax.axis_index("tp")

    def whole_images(stored):
        got = lax.all_to_all(stored.reshape(tp, images, S * width), "tp", 0, 0, tiled=True)
        return got.reshape(tp, images, S, width).transpose(1, 2, 0, 3).reshape(images, S, full)

    def stored(values):
        parts = values.reshape(images, S, tp, width).transpose(2, 0, 1, 3).reshape(tp, images, S * width)
        return lax.all_to_all(parts, "tp", 0, 0, tiled=True).reshape(held, 1, S * width)

    rows = ch_w1.shape[0]
    shard = jnp.stack([ch_w1.astype(bf16), ch_w2.T.astype(bf16)])
    gathered = lax.all_gather(lax.all_gather(shard, "tp", axis=1), "dp", axis=2)
    gathered = gathered.reshape(2, tp, dp * rows, shard.shape[2])
    norms = lax.all_gather(jnp.stack([ln1_gain, ln1_shift, ln2_gain, ln2_shift]), "tp", axis=1, tiled=True)
    x = whole_images(block_in).astype(f32)
    dz_low = whole_images(out_grad)
    token_w1 = tok_w1.astype(bf16)
    token_w2 = tok_w2.astype(bf16)
    xhat, inv_x = normalised(x)
    mixed = (xhat * norms[0] + norms[1]).astype(bf16)
    pre = jnp.einsum("nsc,sk->nkc", mixed, token_w1, preferred_element_type=f32) + tok_b1[:, None]
    hidden, hidden_back = jax.vjp(jax.nn.gelu, pre)
    hidden = hidden.astype(bf16)
    u = x + jnp.einsum("nkc,ks->nsc", hidden, token_w2, preferred_element_type=f32) + tok_b2[:, None]
    uhat, inv_u = normalised(u)
    count = images * S
    hn = (uhat * norms[2] + norms[3]).astype(bf16).reshape(count, full)
    dz = dz_low.reshape(count, full)
    z = jnp.zeros((count, full), f32)
    dhn = jnp.zeros((count, full), f32)
    grads1, grads2, bias = [], [], []
    inner = shard.shape[2]
    for j in range(tp):
        q = jnp.dot(hn, gathered[0, j], preferred_element_type=f32) + ch_b1[j * inner : (j + 1) * inner]
        g, g_back = jax.vjp(jax.nn.gelu, q)
        g = g.astype(bf16)
        z = z + jnp.einsum("rh,ch->rc", g, gathered[1, j], preferred_element_type=f32)
        dg = jnp.dot(dz, gathered[1, j], preferred_element_type=f32)
        dq = g_back(dg)[0].astype(bf16)
        grads2.append(jnp.einsum("rc,rh->ch", dz, g, preferred_element_type=f32).astype(bf16))
        grads1.append(jnp.einsum("rc,rh->ch", hn, dq, preferred_element_type=f32).astype(bf16))
        bias.append(jnp.sum(dq.astype(f32), 0))
        dhn = dhn + jnp.einsum("rh,ch->rc", dq, gathered[0, j], preferred_element_type=f32)
    z = (z + ch_b2).astype(bf16).astype(f32).reshape(u.shape)
    block_out = stored((u + z).astype(bf16))
    dhn = dhn.reshape(u.shape)
    dz32 = dz_low.astype(f32)
    image_gain = jnp.sum(dhn * uhat, 1)
    image_shift = jnp.sum(dhn, 1)
    du = dz32 + norm_back(dhn * norms[2], uhat, inv_u)
    dp_low = du.astype(bf16)
    dh = jnp.einsum("nsc,ks->nkc", dp_low, token_w2, preferred_element_type=f32)
    d_tok_w2 = jnp.einsum("nkc,nsc->ks", hidden, dp_low, preferred_element_type=f32)
    d_tok_b2 = jnp.sum(dp_low.astype(f32), (0, 2))
    dpre = hidden_back(dh)[0].astype(bf16)
    d_tok_w1 = jnp.einsum("nsc,nkc->sk", mixed, dpre, preferred_element_type=f32)
    d_tok_b1 = jnp.sum(dpre.astype(f32), (0, 2))
    da = jnp.einsum("nkc,sk->nsc", dpre, token_w1, preferred_element_type=f32)
    d_gain1 = jnp.sum(da * xhat, (0, 1))
    d_shift1 = jnp.sum(da, (0, 1))
    dx = stored((du + norm_back(da * norms[0], xhat, inv_x)).astype(bf16))

    gradient = jnp.stack([jnp.stack(grads1), jnp.stack(grads2)]).reshape(2, tp, dp, rows, inner)
    owned = lax.psum_scatter(lax.psum_scatter(gradient, "tp", scatter_dimension=1, tiled=True).astype(bf16), "dp", scatter_dimension=2, tiled=True)
    owned = owned.astype(f32).reshape(2, rows, inner)

    ids = lax.dynamic_slice_in_dim(group_ids, t * images, images)
    member = (ids[:, None] == jnp.arange(GROUPS)[None, :]).astype(f32)
    groups = jnp.dot(member.T, jnp.concatenate([image_gain, image_shift], 1), precision=highest)
    flat = [d_tok_w1, d_tok_w2, jnp.stack(bias), jnp.sum(dz32, (0, 1)), d_gain1, d_shift1, d_tok_b1, d_tok_b2, groups]
    sizes = [v.size for v in flat]
    need = sum(sizes)
    unit = 64 * full
    padded = -(-need // unit) * unit
    packed = jnp.concatenate([v.reshape(-1) for v in flat] + [jnp.zeros((padded - need,), f32)]).reshape(-1, full)
    total = lax.psum(packed, ("dp", "tp"))
    total = total.reshape(-1)
    pieces, start = [], 0
    for v in flat:
        pieces.append(total[start : start + v.size].reshape(v.shape))
        start += v.size
    tw1, tw2, cb1, cb2, g1, s1, tb1, tb2, gg = pieces
    gg = gg.reshape(GROUPS, 2, full)
    group_norms = jnp.sqrt(jnp.sum(gg * gg, (1, 2)))
    bound = 2.0 * math.sqrt(held * dp * S * full / GROUPS)
    factor = bound / jnp.maximum(group_norms, bound)
    clipped = jnp.sum(factor[:, None, None] * gg, 0)

    def mine(v):
        return lax.dynamic_slice_in_dim(v, t * width, width)

    return (block_out, dx, group_norms, mine(g1), mine(s1), tw1, tb1, tw2, tb2, mine(clipped[0]), mine(clipped[1]),
            owned[0], cb1.reshape(-1), owned[1].T, cb2)


def blocked(block_in, ln1_gain, ln1_shift, tok_w1, tok_b1, tok_w2, tok_b2, ln2_gain, ln2_shift,
            ch_w1, ch_b1, ch_w2, ch_b2, group_ids, out_grad):
    held = block_in.shape[0]
    bound = 2.0 * math.sqrt(held * 8 * S * 768 / GROUPS)
    flat = (held, HALF * 384)
    out, dx, grads, total = one_step(
        ch_w1, ch_w2.T, block_in.reshape(flat), out_grad.reshape(flat), ln1_gain, ln1_shift, ln2_gain, ln2_shift,
        tok_w1, tok_w2.T, tok_b1, tok_b2, ch_b1, ch_b2, group_ids)
    out, dx, d1, d2, tok1, tok2, bias1, bias2, inner, outer, sizes, gain1, shift1, gain2, shift2 = finish(bound, out, dx, grads, total)
    shape = block_in.shape
    return (out.reshape(shape), dx.reshape(shape), sizes, gain1, shift1, tok1, bias1, tok2.T, bias2,
            gain2, shift2, d1, inner, d2.T, outer)


def solution(mesh):
    stored, own, copied = P("dp", "tp", None), P("tp"), P()
    in_specs = (stored, own, own, copied, copied, copied, copied, own, own, P("dp", "tp"), copied, P("tp", "dp"), copied, P("dp"), stored)
    out_specs = (stored, stored, copied, own, own, copied, copied, copied, copied, own, own, P("dp", "tp"), copied, P("tp", "dp"), copied)
    step = blocked if (mesh.shape["dp"], mesh.shape["tp"]) == (8, 4) else general
    return jax.shard_map(step, mesh=mesh, in_specs=in_specs, out_specs=out_specs, check_vma=False)
```

```python
import functools
import math

import jax
import jax.numpy as jnp
from jax import lax
from jax.experimental import pallas as pl
from jax.experimental.pallas import tpu as pltpu
from jax.sharding import PartitionSpec as P

MESH = pl.DeviceIdType.MESH


S = 196
GROUPS = 64
F32 = jnp.float32
BF16 = jnp.bfloat16
HALF = 98
GAP = 104
ROWS = 208
BLOCK = 4 * HALF
LOW = math.sqrt(2.0 / math.pi)
CUBE = 0.044715


def place():
    dp = lax.axis_index("dp")
    t = lax.axis_index("tp")
    c, x, y = dp % 2, (dp // 2) % 2, dp // 4
    near = dict(S=owner(y, x, 1 - c), X=owner(y, 1 - x, c), Y=owner(1 - y, x, c), D=owner(1 - y, 1 - x, c))
    return dp, t, near, (y, x, c)


def owner(y, x, c):
    return (y * 2 + x) * 2 + c


def others(t):
    first = jnp.where(t == 0, 1, jnp.where(t == 1, 0, jnp.where(t == 2, 3, 2)))
    second = jnp.where(t == 0, 2, jnp.where(t == 1, 2, 1))
    third = jnp.where(t < 2, 3, 0)
    return [first, second, third]


def meet(devices):
    barrier = pltpu.get_barrier_semaphore()
    for device in devices:
        pl.semaphore_signal(barrier, inc=1, device_id=device, device_id_type=MESH)
    pl.semaphore_wait(barrier, len(devices))


def remote(src, dst, ss, rs, device):
    return pltpu.make_async_remote_copy(src_ref=src, dst_ref=dst, send_sem=ss, recv_sem=rs, device_id=device, device_id_type=MESH)


def gelu_pair(v):
    square = v * v
    up = 0.5 * jnp.tanh(v * (LOW + (LOW * CUBE) * square)) + 0.5
    value = v * up
    slope = up + value * (1.0 - up) * (2.0 * LOW + (6.0 * LOW * CUBE) * square)
    return value, slope


def turn(v):
    return pltpu.roll(v, 64, 1)


def lane_low():
    return lax.broadcasted_iota(jnp.int32, (HALF, 128), 1) < 64


def join_groups(flat, image, store):
    low = lane_low()
    for p in range(2):
        a = [flat[j, pl.ds(2 * p * BLOCK + image * HALF, HALF), :] for j in range(3)]
        b = [flat[j, pl.ds((2 * p + 1) * BLOCK + image * HALF, HALF), :] for j in range(3)]
        a1, a2, b0, b1 = turn(a[1]), turn(a[2]), turn(b[0]), turn(b[1])
        even = [a[0], jnp.where(low, a[1], b0), jnp.where(low, b0, b1)]
        odd = [jnp.where(low, a1, a2), jnp.where(low, a2, b[1]), b[2]]
        for j in range(3):
            store(0, 384 * p + 128 * j, even[j])
            store(GAP, 384 * p + 128 * j, odd[j])


def split_groups(load, flat, image):
    low = lane_low()
    for p in range(2):
        e = [load(0, 384 * p + 128 * j) for j in range(3)]
        o = [load(GAP, 384 * p + 128 * j) for j in range(3)]
        e1, e2, o0, o1 = turn(e[1]), turn(e[2]), turn(o[0]), turn(o[1])
        a = [e[0], jnp.where(low, e[1], o0), jnp.where(low, o0, o1)]
        b = [jnp.where(low, e1, e2), jnp.where(low, e2, o[1]), o[2]]
        for j in range(3):
            flat[j, pl.ds(2 * p * BLOCK + image * HALF, HALF), :] = a[j]
            flat[j, pl.ds((2 * p + 1) * BLOCK + image * HALF, HALF), :] = b[j]


def spread(packed, flat):
    for k in range(4):
        for j in range(3):
            flat[j, pl.ds(k * BLOCK, BLOCK), :] = packed[k, :, 128 * j : 128 * j + 128].astype(F32)


def pack(flat, packed):
    for k in range(4):
        for j in range(3):
            packed[k, :, 128 * j : 128 * j + 128] = flat[j, pl.ds(k * BLOCK, BLOCK), :].astype(BF16)


def to_rows(stored, flat):
    for i in range(HALF):
        for j in range(3):
            start = 384 * i + 128 * j
            flat[j, pl.ds(i, 16, stride=HALF), :] = stored[:, start : start + 128].astype(F32)


def to_stored(flat, stored):
    for i in range(HALF):
        for j in range(3):
            start = 384 * i + 128 * j
            stored[:, start : start + 128] = flat[j, pl.ds(i, 16, stride=HALF), :].astype(BF16)


def hat(v):
    average = jnp.mean(v, -1, keepdims=True)
    inverse = lax.rsqrt(jnp.mean(v * v, -1, keepdims=True) - average * average + 1e-06)
    return (v - average) * inverse, inverse


def dot(a, b):
    return jnp.dot(a, b, preferred_element_type=F32)


def dot_nt(a, b):
    return lax.dot_general(a, b, (((1,), (1,)), ((), ())), preferred_element_type=F32)


PIECE = 48
SMALL = 8 * PIECE


def step_kernel(cw1, cw2, xin, din, p0, p1, p2, p3, tw1, tw2, b1, b2, cb1, cb2, ids,
                o_out, dx_out, w_grad, total_out,
                wf, shard, wv, stored, xs, ds, xr, dr, flat, xb, u, act, hnt, dzt, g, s, h, ts, zs, lr, lall, t3, c2, w1, w2, w1t, w2t,
                sib, first, second, final, zz, zi, small, low, t_sib, t_chip, t_line,
                send_sem, recv_sem, line_sem, x_send, x_recv, d_send, d_recv, ln_send, ln_recv, in_sem, own_sem,
                o_send, o_recv, y_send, y_recv, sib_sem, sib_recv, a_send, a_recv, z_send, z_recv, i_recv,
                p_send, p_recv, c_send, c_recv, l_send, l_recv, b_send, b_recv, e_send, e_recv):
    dp, t, near, (y, xx, c) = place()
    line = others(t)
    order = [t] + line
    back = [line[2], line[1], line[0], t]
    chips = {"O": (y, xx), "X": (y, 1 - xx), "Y": (1 - y, xx), "D": (1 - y, 1 - xx)}
    slot = {"O": 0, "X": 1, "Y": 2, "D": 3}
    started = {"w": [], "x": [], "y": [], "": []}
    maybe = []
    state = {}
    zero = jnp.zeros((1, 768), F32)

    def go(copy, kind=""):
        copy.start()
        started[kind].append(copy)

    def local(src, dst, sem):
        copy = pltpu.make_async_copy(src, dst, sem)
        copy.start()
        return copy

    def sent(kind):
        for copy in started[kind]:
            copy.wait_send()
        started[kind] = []

    in_w1, in_w2 = local(cw1, wf.at[0], in_sem.at[0]), local(cw2, wf.at[1], in_sem.at[1])
    state["in"] = local(xin, stored, in_sem.at[2])
    meet([(near["S"], t), (near["X"], t), (near["Y"], t), (near["D"], t)] + [(dp, p) for p in line])
    sends = [0, 0]


    def send(src, who, tt, device):
        go(remote(src, wv.at[:, tt, who], send_sem.at[sends[0]], recv_sem.at[who, tt], device), "w")
        sends[0] += 1

    def along(src, tt, target):
        inside = (target >= 0) & (target <= 3)
        copy = remote(src, wv.at[:, tt, dp], line_sem.at[sends[1]], recv_sem.at[dp, tt], (dp, jnp.clip(target, 0, 3)))
        sends[1] += 1
        pl.when(inside)(copy.start)
        maybe.append((inside, copy))

    def arrived(who, tt):
        ref = wv.at[:, tt, who]
        remote(ref, ref, send_sem.at[0], recv_sem.at[who, tt], (dp, t)).wait_recv()

    def weights():
        in_w1.wait()
        in_w2.wait()
        shard[...] = wf[...].astype(BF16)
        along(shard, t, t + 1)
        along(shard, t, t - 1)
        for name in "XYS":
            send(shard, dp, t, (near[name], t))
        wv[:, t, dp] = shard[...]
        for n, ref in enumerate((p0, p1, p2, p3)):
            row = ref[...].reshape(1, 192)
            wide = jnp.concatenate([row, row, row, row], 1)
            lane = lax.broadcasted_iota(jnp.int32, (1, 768), 1)
            lr[t, n : n + 1, :] = jnp.where((lane >= 192 * t) & (lane < 192 * t + 192), wide, 0.0)
        for n, p in enumerate(line):
            go(remote(lr.at[t], lr.at[t], ln_send.at[n], ln_recv.at[t], (dp, p)))

    def column(k):
        tt = order[k]
        arrived(dp, tt)
        src = wv.at[:, tt, dp]
        along(src, tt, jnp.where(tt < t, t + 1, t - 1))
        for name in "XYS":
            send(src, dp, tt, (near[name], t))

    def neighbours(k):
        tt = order[k]
        one, two = ("X", "Y") if k % 2 == 0 else ("Y", "X")
        arrived(near[one], tt)
        src = wv.at[:, tt, near[one]]
        send(src, near[one], tt, (near[two], t))
        send(src, near[one], tt, (near["S"], t))
        arrived(near[two], tt)
        send(wv.at[:, tt, near[two]], near[two], tt, (near["S"], t))

    def diagonal(k):
        tt = order[k]
        arrived(near["D"], tt)
        send(wv.at[:, tt, near["D"]], near["D"], tt, (near["S"], t))


    def pack_input():
        state["in"].wait()
        to_rows(stored, flat)
        pack(flat, xs)
        state["in"] = local(din, stored, in_sem.at[3])

    def send_input(n):
        p = line[n]
        go(remote(xs.at[p], xr.at[t], x_send.at[n], x_recv.at[t], (dp, p)), "x")

    def pack_grad():
        state["in"].wait()
        to_rows(stored, flat)
        pack(flat, ds)

    def send_grad(n):
        p = line[n]
        go(remote(ds.at[p], dr.at[t], d_send.at[n], d_recv.at[t], (dp, p)), "y")

    def token_weights():
        gap = jnp.zeros((GAP - HALF, 128), F32)
        for n, (src, dst) in enumerate(((tw1, w1), (tw2, w2t))):
            for j in range(3):
                t3[j] = src[:, 128 * j : 128 * j + 128]
            for j in range(3):
                even, odd = t3[j, pl.ds(0, HALF, stride=2), :], t3[j, pl.ds(1, HALF, stride=2), :]
                dst[:, 128 * j : 128 * j + 128] = jnp.concatenate([even, gap, odd, gap], 0).astype(BF16)
        w1t[...] = w1[...].T
        w2[...] = w2t[...].T
        c2[...] = jnp.broadcast_to(b2[...].reshape(1, S), (128, S)).T
        few = jnp.zeros((GAP - HALF, 1), F32)
        state["shift2"] = jnp.concatenate([c2[pl.ds(0, HALF, stride=2), :][:, 0:1], few, c2[pl.ds(1, HALF, stride=2), :][:, 0:1], few], 0)
        state["shift1"] = jnp.broadcast_to(b1[...].reshape(1, 384), (8, 384)).T[:, 0:1]
        small[...] = jnp.zeros((SMALL, 768), F32)

    def join(received, own, dst):
        received[t] = own[t]
        spread(received, flat)
        few = jnp.zeros((GAP - HALF, 768), F32)
        for n in range(4):
            for start in (HALF, GAP + HALF):
                zs[n, start : start + GAP - HALF, :] = few

            def put(row, lane, v, n=n):
                zs[n, row : row + HALF, lane : lane + 128] = v

            join_groups(flat, n, put)
            dst[n] = zs[n].astype(BF16)

    def join_input():
        for p in line:
            remote(lr.at[p], lr.at[p], ln_send.at[0], ln_recv.at[p], (dp, t)).wait_recv()
        lall[...] = (lr[0] + lr[1]) + (lr[2] + lr[3])
        for p in line:
            remote(xr.at[p], xr.at[p], x_send.at[0], x_recv.at[p], (dp, t)).wait_recv()
        join(xr, xs, xb)

    def token_forward(start, stop):
        g1, s1, g2, s2 = lall[0:1], lall[1:2], lall[2:3], lall[3:4]
        shift1, shift2 = state["shift1"], state["shift2"]

        def body(n, carry):
            v = xb[n].astype(F32)
            xhat, _ = hat(v)
            a = (xhat * g1 + s1).astype(BF16)
            value, slope = gelu_pair(dot(w1t[...], a) + shift1)
            low = value.astype(BF16)
            h[n] = low
            ts[n] = slope.astype(BF16)
            r = v + dot(w2t[...], low) + shift2
            u[n] = r
            uhat, _ = hat(r)
            act[n] = (uhat * g2 + s2).astype(BF16)
            return carry

        lax.fori_loop(start, stop, body, 0)

    def block(k):
        tt = order[k]
        for name in "OXYD":
            arrived(owner(*chips[name], 1 - c), tt)
        bias = cb1[pl.ds(pl.multiple_of(tt * 768, 128), 768)].reshape(1, 768)

        def body(n, carry):
            value, slope = gelu_pair(dot(act[n], wv[0, tt].reshape(768, 768)) + bias)
            low = value.astype(BF16)
            g[tt, n] = low
            s[tt, n] = slope.astype(BF16)
            part = dot_nt(low, wv[1, tt].reshape(768, 768))
            if k == 0:
                zs[n] = part
            elif k < 3:
                zs[n] += part
            else:
                zs[n] = u[n] + (zs[n] + part + cb2[...].reshape(1, 768)).astype(BF16).astype(F32)
            return carry

        lax.fori_loop(0, 4, body, 0)

    def pack_output():
        for n in range(4):
            split_groups(lambda row, lane, n=n: zs[n, row : row + HALF, lane : lane + 128], flat, n)
        sent("x")
        pack(flat, xs)
        state["own_o"] = local(xs.at[t], o_out.at[t], own_sem.at[0])

    def send_output(n):
        p = line[n]
        go(remote(xs.at[p], o_out.at[t], o_send.at[n], o_recv.at[t], (dp, p)))

    def hidden_in():
        for n in range(4):
            hnt[:, n * ROWS : (n + 1) * ROWS] = act[n].T

    def join_grad():
        for p in line:
            remote(dr.at[p], dr.at[p], d_send.at[0], d_recv.at[p], (dp, t)).wait_recv()
        join(dr, ds, act)
        for n in range(4):
            dzt[:, n * ROWS : (n + 1) * ROWS] = act[n].T
        sent("w")
        for inside, copy in maybe:
            pl.when(inside)(copy.wait_send)
        maybe.clear()


    def hand_over(j, k):
        for name in "DXYO":
            n = slot[name]
            go(remote(wv.at[j, back[k], owner(*chips[name], 1 - c)], sib.at[j, k, n], sib_sem.at[j, k, n], sib_recv.at[j, k, n], (near["S"], t)))

    def chip_sum(j, k, name):
        n = slot[name]
        remote(sib.at[j, k, n], sib.at[j, k, n], sib_sem.at[j, k, n], sib_recv.at[j, k, n], (near["S"], t)).wait_recv()
        sib[j, k, n] = wv[j, back[k], owner(*chips[name], c)] + sib[j, k, n]

    def ways(k):
        return ("X", "Y") if k % 2 == 0 else ("Y", "X")

    def hop(j, k, src, dst, n, name):
        go(remote(src, dst, a_send.at[j, k, n], a_recv.at[j, k, n], (near[name], t)))

    def landed(j, k, dst, n):
        remote(dst, dst, a_send.at[j, k, n], a_recv.at[j, k, n], (near["S"], t)).wait_recv()

    def stage_one(j, k):
        f, s2 = ways(k)
        chip_sum(j, k, "D")
        hop(j, k, sib.at[j, k, 3], first.at[j, k], 0, s2)
        chip_sum(j, k, s2)
        hop(j, k, sib.at[j, k, slot[s2]], second.at[j, k], 1, s2)

    def stage_two(j, k):
        f, s2 = ways(k)
        n = slot[f]
        chip_sum(j, k, f)
        landed(j, k, first.at[j, k], 0)
        sib[j, k, n] = sib[j, k, n] + first[j, k]
        hop(j, k, sib.at[j, k, n], final.at[j, k], 2, f)

    def stage_three(j, k):
        chip_sum(j, k, "O")
        landed(j, k, second.at[j, k], 1)
        landed(j, k, final.at[j, k], 2)
        total = sib[j, k, 0].astype(F32) + second[j, k].astype(F32) + final[j, k].astype(F32)
        if k < 3:
            sib[j, k, 0] = total.astype(BF16)
        else:
            w_grad[j] = total

    inner = (t == 1) | (t == 2)
    beside = back[2]
    across = jnp.where(t < 2, 2, 1)

    def along_in(j, n):
        remote(zz.at[j, n], zz.at[j, n], z_send.at[j, 0], z_recv.at[j, n], (dp, t)).wait_recv()

    def stage_four(j, k):
        piece, p = sib.at[j, k, 0], back[k]
        if k == 2:
            go(remote(piece, zz.at[j, t], z_send.at[j, k], z_recv.at[j, t], (dp, p)))
            return
        copy = remote(piece, zi.at[j, p % 2], z_send.at[j, k], i_recv.at[j, p % 2], (dp, beside))
        ends = jnp.logical_not(inner)
        pl.when(ends)(copy.start)
        maybe.append((ends, copy))

    def stage_five(j, k):
        piece, p = sib.at[j, k, 0], back[k]
        copy = remote(piece, zz.at[j, t], z_send.at[j, k], z_recv.at[j, t], (dp, p))

        @pl.when(inner)
        def _():
            there = zi.at[j, p % 2]
            remote(there, there, z_send.at[j, k], i_recv.at[j, p % 2], (dp, t)).wait_recv()
            piece[...] = piece[...] + there[...]
            copy.start()

        maybe.append((inner, copy))

    def stage_six(j):
        for n in (beside, across):
            along_in(j, n)
            w_grad[j] += zz[j, n].astype(F32)

    def second_weight(k):
        wv[1, back[k]] = dot(dzt[...], g[back[k]].reshape(4 * ROWS, 768)).astype(BF16).reshape(8, 96, 768)
        hand_over(1, k)

    def data(k):
        tt = back[k]

        def body(n, bias):
            low = (dot(act[n], wv[1, tt].reshape(768, 768)) * s[tt, n].astype(F32)).astype(BF16)
            s[tt, n] = low
            part = dot_nt(low, wv[0, tt].reshape(768, 768))
            if k == 0:
                zs[n] = part
            else:
                zs[n] += part
            return bias + jnp.sum(low.astype(F32), 0, keepdims=True)

        small[pl.ds(HALF + 1 + tt, 1), :] = lax.fori_loop(0, 4, body, zero)

    def first_weight(k):
        wv[0, back[k]] = dot(hnt[...], s[back[k]].reshape(4 * ROWS, 768)).astype(BF16).reshape(8, 96, 768)
        hand_over(0, k)

    def token_backward(start, stop):
        g1, s1, g2 = lall[0:1], lall[1:2], lall[2:3]
        row = lax.broadcasted_iota(jnp.int32, (ROWS, 768), 0)
        ones = jnp.ones((8, 768), BF16)
        groups = lax.broadcasted_iota(jnp.int32, (GROUPS, 16), 0) == ids[...].reshape(1, 16)
        lane = lax.broadcasted_iota(jnp.int32, (GROUPS, 16), 1)

        def body(n, carry):
            sum_g1, sum_s1, sum_b2, sum_dz = carry
            d, grad = zs[n], act[n].astype(F32)
            uhat, inv_u = hat(u[n])
            member = jnp.sum(jnp.where(groups & (lane == 4 * t + n), 1.0, 0.0), -1, keepdims=True)
            small[208:272, :] += member * jnp.sum(d * uhat, 0, keepdims=True)
            small[272:336, :] += member * jnp.sum(d, 0, keepdims=True)
            e = d * g2
            du = grad + inv_u * (e - jnp.mean(e, -1, keepdims=True) - uhat * jnp.mean(e * uhat, -1, keepdims=True))
            low = du.astype(BF16)
            dpre = (dot(w2[...], low) * ts[n].astype(F32)).astype(BF16)
            xhat, inv_x = hat(xb[n].astype(F32))
            a = jnp.where(row == HALF, 1.0, xhat * g1 + s1).astype(BF16)
            tok1 = dot_nt(a, dpre)
            tok2 = dot_nt(low, h[n])
            for begin, size in ((0, HALF + 1), (GAP, HALF)):
                small[begin : begin + size, 0:384] += tok1[begin : begin + size]
            for begin, size in ((0, HALF), (GAP, HALF)):
                small[begin : begin + size, 384:768] += tok2[begin : begin + size]
            da = dot(w1[...], dpre)
            e1 = da * g1
            zs[n] = du + inv_x * (e1 - jnp.mean(e1, -1, keepdims=True) - xhat * jnp.mean(e1 * xhat, -1, keepdims=True))
            return (sum_g1 + jnp.sum(da * xhat, 0, keepdims=True), sum_s1 + jnp.sum(da, 0, keepdims=True),
                    sum_b2 + dot_nt(ones, low), sum_dz + jnp.sum(grad, 0, keepdims=True))

        sums = state.get("sums", (zero, zero, jnp.zeros((8, ROWS), F32), zero))
        state["sums"] = lax.fori_loop(start, stop, body, sums)

    def pack_dx():
        for n in range(4):
            split_groups(lambda r, lane, n=n: zs[n, r : r + HALF, lane : lane + 128], flat, n)
        sent("y")
        pack(flat, ds)
        state["own_x"] = local(ds.at[t], dx_out.at[t], own_sem.at[1])

    def send_dx(n):
        p = line[n]
        go(remote(ds.at[p], dx_out.at[t], y_send.at[n], y_recv.at[t], (dp, p)))

    chip = dp // 2
    far = [("X", near["X"] // 2), ("Y", near["Y"] // 2), ("D", near["D"] // 2)]

    def part(ref, core, q):
        return ref.at[pl.ds(pl.multiple_of((core * 4 + q) * PIECE, 8), PIECE)]

    def half(ref, core):
        return ref.at[pl.ds(pl.multiple_of(core * 4 * PIECE, 8), 4 * PIECE)]

    own = part(total_out, c, chip)

    def total_zero():
        sum_g1, sum_s1, sum_b2, sum_dz = state["sums"]
        small[202:203, :] = sum_g1
        small[203:204, :] = sum_s1
        small[204:205, 0:ROWS] = sum_b2[0:1]
        small[205:206, :] = sum_dz
        half(low, 1 - c)[...] = half(small, 1 - c)[...].astype(BF16)
        go(remote(half(low, 1 - c), t_sib, p_send, p_recv, (near["S"], t)))

    def total_one():
        remote(t_sib, t_sib, p_send, p_recv, (near["S"], t)).wait_recv()
        both = half(small, c)[...] + t_sib[...].astype(F32)
        half(small, c)[...] = both
        half(low, c)[...] = both.astype(BF16)
        for n, (name, q) in enumerate(far):
            go(remote(part(low, c, q), t_chip.at[n], c_send.at[n], c_recv.at[n], (near[name], t)))

    def total_two():
        total = part(small, c, chip)[...]
        for n in range(3):
            remote(t_chip.at[n], t_chip.at[n], c_send.at[n], c_recv.at[n], (near["S"], t)).wait_recv()
            total = total + t_chip[n].astype(F32)
        t_line[t] = total.astype(BF16)
        for n, p in enumerate(line):
            go(remote(t_line.at[t], t_line.at[t], l_send.at[n], l_recv.at[t], (dp, p)))

    def total_three():
        for p in line:
            remote(t_line.at[p], t_line.at[p], l_send.at[0], l_recv.at[p], (dp, t)).wait_recv()
        sums = [t_line[p].astype(F32) for p in range(4)]
        own[...] = (((sums[0] + sums[1]) + sums[2]) + sums[3]).astype(BF16)
        for n, (name, q) in enumerate(far):
            go(remote(own, own, b_send.at[n], b_recv.at[chip], (near[name], t)))
        go(remote(own, own, e_send.at[3], e_recv.at[chip], (near["S"], t)))

    def total_five():
        for n, (name, q) in enumerate(far):
            there = part(total_out, c, q)
            remote(there, there, b_send.at[0], b_recv.at[q], (dp, t)).wait_recv()
            go(remote(there, there, e_send.at[n], e_recv.at[q], (near["S"], t)))

    def total_six():
        for q in range(4):
            there = part(total_out, 1 - c, q)
            remote(there, there, e_send.at[0], e_recv.at[q], (dp, t)).wait_recv()

    weights()
    pack_input()
    column(1)
    neighbours(0)
    column(2)
    send_input(0)
    send_input(1)
    send_input(2)
    neighbours(1)
    diagonal(0)
    column(3)
    pack_grad()
    token_weights()
    neighbours(2)
    diagonal(1)
    neighbours(3)
    diagonal(2)
    diagonal(3)
    join_input()
    send_grad(0)
    send_grad(1)
    send_grad(2)
    token_forward(0, 4)
    block(0)
    block(1)
    block(2)
    block(3)
    pack_output()
    send_output(0)
    send_output(1)
    send_output(2)
    hidden_in()
    join_grad()
    data(0)
    second_weight(0)
    data(1)
    second_weight(1)
    stage_one(1, 0)
    data(2)
    second_weight(2)
    stage_one(1, 1)
    data(3)
    second_weight(3)
    stage_one(1, 2)
    token_backward(0, 4)
    pack_dx()
    send_dx(0)
    send_dx(1)
    send_dx(2)
    stage_one(1, 3)
    total_zero()
    stage_two(1, 0)
    stage_two(1, 1)
    stage_two(1, 2)
    stage_two(1, 3)
    total_one()
    first_weight(0)
    first_weight(1)
    stage_one(0, 0)
    stage_three(1, 0)
    stage_four(1, 0)
    first_weight(2)
    stage_one(0, 1)
    stage_three(1, 1)
    stage_four(1, 1)
    first_weight(3)
    stage_one(0, 2)
    stage_three(1, 2)
    stage_four(1, 2)
    stage_one(0, 3)
    total_two()
    stage_three(1, 3)
    stage_two(0, 0)
    stage_two(0, 1)
    stage_two(0, 2)
    stage_two(0, 3)
    stage_five(1, 0)
    stage_five(1, 1)
    total_three()
    stage_three(0, 0)
    stage_four(0, 0)
    stage_three(0, 1)
    stage_four(0, 1)
    stage_three(0, 2)
    stage_four(0, 2)
    stage_three(0, 3)
    total_five()
    stage_five(0, 0)
    stage_five(0, 1)
    stage_six(1)
    stage_six(0)
    total_six()

    state["own_o"].wait()
    state["own_x"].wait()
    for p in line:
        remote(o_out.at[p], o_out.at[p], o_send.at[0], o_recv.at[p], (dp, t)).wait_recv()
        remote(dx_out.at[p], dx_out.at[p], y_send.at[0], y_recv.at[p], (dp, t)).wait_recv()
    sent("")
    for inside, copy in maybe:
        pl.when(inside)(copy.wait_send)


def one_step(*operands):
    any_, vmem = pl.BlockSpec(memory_space=pl.ANY), pl.BlockSpec(memory_space=pltpu.VMEM)
    sds = jax.ShapeDtypeStruct
    dma = pltpu.SemaphoreType.DMA
    V = pltpu.VMEM
    wshape, act, tok, packed, piece = (2, 4, 8, 96, 768), (4, ROWS, 768), (4, 384, 768), (4, BLOCK, 384), (96, 768)
    return pl.pallas_call(step_kernel,
        out_shape=[sds(packed, BF16), sds(packed, BF16), sds((2,) + piece, F32), sds((SMALL, 768), BF16)],
        in_specs=[any_] * 4 + [vmem] * 11, out_specs=[any_] * 2 + [vmem] * 2,
        scratch_shapes=[V((2, 96, 768), F32), V((2, 96, 768), BF16), V(wshape, BF16), V((16, HALF * 384), BF16), V(packed, BF16), V(packed, BF16),
            V(packed, BF16), V(packed, BF16), V((3, 4 * BLOCK, 128), F32), V(act, BF16), V(act, F32), V(act, BF16), V((768, 4 * ROWS), BF16), V((768, 4 * ROWS), BF16),
            V((4,) + act, BF16), V((4,) + act, BF16), V(tok, BF16), V(tok, BF16), V(act, F32), V((4, 8, 768), F32), V((8, 768), F32),
            V((3, S, 128), F32), V((S, 128), F32), V((ROWS, 384), BF16), V((384, ROWS), BF16), V((384, ROWS), BF16), V((ROWS, 384), BF16),
            V((2, 4, 4) + piece, BF16), V((2, 4) + piece, BF16), V((2, 4) + piece, BF16), V((2, 4) + piece, BF16), V((2, 4) + piece, BF16), V((2, 2) + piece, BF16),
            V((SMALL, 768), F32), V((SMALL, 768), BF16), V((4 * PIECE, 768), BF16), V((3, PIECE, 768), BF16), V((4, PIECE, 768), BF16),
            dma((28,)), dma((8, 4)), dma((5,)), dma((3,)), dma((4,)), dma((3,)), dma((4,)), dma((3,)), dma((4,)), dma((4,)), dma((2,)),
            dma((3,)), dma((4,)), dma((3,)), dma((4,)), dma((2, 4, 4)), dma((2, 4, 4)), dma((2, 4, 3)), dma((2, 4, 3)), dma((2, 4)), dma((2, 4)), dma((2, 2)),
            dma, dma, dma((3,)), dma((3,)), dma((3,)), dma((4,)), dma((3,)), dma((4,)), dma((4,)), dma((4,))],
        compiler_params=pltpu.CompilerParams(collective_id=1, has_side_effects=True, vmem_limit_bytes=63 << 20))(*operands)


def finish_kernel(bound, o_in, dx_in, grads_in, total_in, o_stored, dx_stored, d1, d2, tok1, tok2, bias1, bias2, inner, outer, sizes, gain1, shift1, gain2, shift2, o, dx, grads, low, flat, wide, t3, total, sems):
    t = lax.axis_index("tp")
    copies = [pltpu.make_async_copy(src, dst, sems.at[n]) for n, (src, dst) in enumerate(((total_in, low), (o_in, o), (dx_in, dx), (grads_in, grads)))]
    for copy in copies:
        copy.start()
    for copy in copies:
        copy.wait()
    total[...] = low[...].astype(F32)
    spread(o, flat)
    to_stored(flat, o_stored)
    spread(dx, wide)
    to_stored(wide, dx_stored)
    d1[...] = grads[0]
    d2[...] = grads[1]
    for start, dst in ((0, tok1), (384, tok2)):
        for j in range(3):
            lanes = slice(start + 128 * j, start + 128 * j + 128)
            t3[j, pl.ds(0, HALF, stride=2), :] = total[0:HALF, lanes]
            t3[j, pl.ds(1, HALF, stride=2), :] = total[GAP : GAP + HALF, lanes]
        for j in range(3):
            dst[:, 128 * j : 128 * j + 128] = t3[j]
    bias1[...] = total[HALF : HALF + 1, 0:384].reshape(384)
    for k in range(4):
        inner[pl.ds(768 * k, 768)] = total[HALF + 1 + k : HALF + 2 + k, :].reshape(768)
    column = jnp.broadcast_to(total[204:205, 0:ROWS], (128, ROWS)).T
    t3[0, pl.ds(0, HALF, stride=2), :] = column[0:HALF]
    t3[0, pl.ds(1, HALF, stride=2), :] = column[GAP : GAP + HALF]
    bias2[...] = t3[0].T[0:1].reshape(S)
    outer[...] = total[205:206, :].reshape(768)
    gg, gb = total[208:272, :], total[272:336, :]
    size = jnp.sqrt(jnp.sum(gg * gg + gb * gb, -1, keepdims=True))
    factor = bound / jnp.maximum(size, bound)
    sizes[...] = jnp.broadcast_to(size, (GROUPS, 128)).T[0:1].reshape(GROUPS)

    def own(v, dst):
        picked = jnp.zeros((1, 192), F32)
        for q in range(4):
            picked = jnp.where(t == q, v[:, 192 * q : 192 * q + 192], picked)
        dst[...] = picked.reshape(192)

    own(total[202:203, :], gain1)
    own(total[203:204, :], shift1)
    own(jnp.sum(factor * gg, 0, keepdims=True), gain2)
    own(jnp.sum(factor * gb, 0, keepdims=True), shift2)


def finish(bound, *operands):
    vmem = pl.BlockSpec(memory_space=pltpu.VMEM)
    shapes = [(16, HALF * 384)] * 2 + [(96, 768)] * 2 + [(S, 384)] * 2 + [(384,), (S,), (3072,), (768,), (GROUPS,)] + [(192,)] * 4
    return pl.pallas_call(functools.partial(finish_kernel, bound),
        out_shape=[jax.ShapeDtypeStruct(v, BF16 if n < 2 else F32) for n, v in enumerate(shapes)],
        in_specs=[pl.BlockSpec(memory_space=pl.ANY)] * 4, out_specs=[vmem] * len(shapes),
        scratch_shapes=[pltpu.VMEM((4, BLOCK, 384), BF16), pltpu.VMEM((4, BLOCK, 384), BF16), pltpu.VMEM((2, 96, 768), F32), pltpu.VMEM((SMALL, 768), BF16),
            pltpu.VMEM((3, 4 * BLOCK, 128), F32), pltpu.VMEM((3, 4 * BLOCK, 128), F32), pltpu.VMEM((3, S, 128), F32), pltpu.VMEM((SMALL, 768), F32), pltpu.SemaphoreType.DMA((4,))],
        compiler_params=pltpu.CompilerParams(vmem_limit_bytes=60 << 20))(*operands)


epsilon = 1e-06
highest = lax.Precision.HIGHEST


def normalised(values):
    average = jnp.mean(values, -1, keepdims=True)
    inverse = lax.rsqrt(jnp.mean(values * values, -1, keepdims=True) - average * average + epsilon)
    return (values - average) * inverse, inverse


def norm_back(grad_hat, normed, inverse):
    return inverse * (
        grad_hat - jnp.mean(grad_hat, -1, keepdims=True) - normed * jnp.mean(grad_hat * normed, -1, keepdims=True)
    )


def general(block_in, ln1_gain, ln1_shift, tok_w1, tok_b1, tok_w2, tok_b2, ln2_gain, ln2_shift,
               ch_w1, ch_b1, ch_w2, ch_b2, group_ids, out_grad):
    f32 = jnp.float32
    bf16 = jnp.bfloat16
    tp = lax.axis_size("tp")
    dp = lax.axis_size("dp")
    held = block_in.shape[0]
    images = held // tp
    width = block_in.shape[2] // S
    full = width * tp
    t = lax.axis_index("tp")

    def whole_images(stored):
        got = lax.all_to_all(stored.reshape(tp, images, S * width), "tp", 0, 0, tiled=True)
        return got.reshape(tp, images, S, width).transpose(1, 2, 0, 3).reshape(images, S, full)

    def stored(values):
        parts = values.reshape(images, S, tp, width).transpose(2, 0, 1, 3).reshape(tp, images, S * width)
        return lax.all_to_all(parts, "tp", 0, 0, tiled=True).reshape(held, 1, S * width)

    rows = ch_w1.shape[0]
    shard = jnp.stack([ch_w1.astype(bf16), ch_w2.T.astype(bf16)])
    gathered = lax.all_gather(lax.all_gather(shard, "tp", axis=1), "dp", axis=2)
    gathered = gathered.reshape(2, tp, dp * rows, shard.shape[2])
    norms = lax.all_gather(jnp.stack([ln1_gain, ln1_shift, ln2_gain, ln2_shift]), "tp", axis=1, tiled=True)
    x = whole_images(block_in).astype(f32)
    dz_low = whole_images(out_grad)
    token_w1 = tok_w1.astype(bf16)
    token_w2 = tok_w2.astype(bf16)
    xhat, inv_x = normalised(x)
    mixed = (xhat * norms[0] + norms[1]).astype(bf16)
    pre = jnp.einsum("nsc,sk->nkc", mixed, token_w1, preferred_element_type=f32) + tok_b1[:, None]
    hidden, hidden_back = jax.vjp(jax.nn.gelu, pre)
    hidden = hidden.astype(bf16)
    u = x + jnp.einsum("nkc,ks->nsc", hidden, token_w2, preferred_element_type=f32) + tok_b2[:, None]
    uhat, inv_u = normalised(u)
    count = images * S
    hn = (uhat * norms[2] + norms[3]).astype(bf16).reshape(count, full)
    dz = dz_low.reshape(count, full)
    z = jnp.zeros((count, full), f32)
    dhn = jnp.zeros((count, full), f32)
    grads1, grads2, bias = [], [], []
    inner = shard.shape[2]
    for j in range(tp):
        q = jnp.dot(hn, gathered[0, j], preferred_element_type=f32) + ch_b1[j * inner : (j + 1) * inner]
        g, g_back = jax.vjp(jax.nn.gelu, q)
        g = g.astype(bf16)
        z = z + jnp.einsum("rh,ch->rc", g, gathered[1, j], preferred_element_type=f32)
        dg = jnp.dot(dz, gathered[1, j], preferred_element_type=f32)
        dq = g_back(dg)[0].astype(bf16)
        grads2.append(jnp.einsum("rc,rh->ch", dz, g, preferred_element_type=f32).astype(bf16))
        grads1.append(jnp.einsum("rc,rh->ch", hn, dq, preferred_element_type=f32).astype(bf16))
        bias.append(jnp.sum(dq.astype(f32), 0))
        dhn = dhn + jnp.einsum("rh,ch->rc", dq, gathered[0, j], preferred_element_type=f32)
    z = (z + ch_b2).astype(bf16).astype(f32).reshape(u.shape)
    block_out = stored((u + z).astype(bf16))
    dhn = dhn.reshape(u.shape)
    dz32 = dz_low.astype(f32)
    image_gain = jnp.sum(dhn * uhat, 1)
    image_shift = jnp.sum(dhn, 1)
    du = dz32 + norm_back(dhn * norms[2], uhat, inv_u)
    dp_low = du.astype(bf16)
    dh = jnp.einsum("nsc,ks->nkc", dp_low, token_w2, preferred_element_type=f32)
    d_tok_w2 = jnp.einsum("nkc,nsc->ks", hidden, dp_low, preferred_element_type=f32)
    d_tok_b2 = jnp.sum(dp_low.astype(f32), (0, 2))
    dpre = hidden_back(dh)[0].astype(bf16)
    d_tok_w1 = jnp.einsum("nsc,nkc->sk", mixed, dpre, preferred_element_type=f32)
    d_tok_b1 = jnp.sum(dpre.astype(f32), (0, 2))
    da = jnp.einsum("nkc,sk->nsc", dpre, token_w1, preferred_element_type=f32)
    d_gain1 = jnp.sum(da * xhat, (0, 1))
    d_shift1 = jnp.sum(da, (0, 1))
    dx = stored((du + norm_back(da * norms[0], xhat, inv_x)).astype(bf16))

    gradient = jnp.stack([jnp.stack(grads1), jnp.stack(grads2)]).reshape(2, tp, dp, rows, inner)
    owned = lax.psum_scatter(lax.psum_scatter(gradient, "tp", scatter_dimension=1, tiled=True).astype(bf16), "dp", scatter_dimension=2, tiled=True)
    owned = owned.astype(f32).reshape(2, rows, inner)

    ids = lax.dynamic_slice_in_dim(group_ids, t * images, images)
    member = (ids[:, None] == jnp.arange(GROUPS)[None, :]).astype(f32)
    groups = jnp.dot(member.T, jnp.concatenate([image_gain, image_shift], 1), precision=highest)
    flat = [d_tok_w1, d_tok_w2, jnp.stack(bias), jnp.sum(dz32, (0, 1)), d_gain1, d_shift1, d_tok_b1, d_tok_b2, groups]
    sizes = [v.size for v in flat]
    need = sum(sizes)
    unit = 64 * full
    padded = -(-need // unit) * unit
    packed = jnp.concatenate([v.reshape(-1) for v in flat] + [jnp.zeros((padded - need,), f32)]).reshape(-1, full)
    total = lax.psum(packed, ("dp", "tp"))
    total = total.reshape(-1)
    pieces, start = [], 0
    for v in flat:
        pieces.append(total[start : start + v.size].reshape(v.shape))
        start += v.size
    tw1, tw2, cb1, cb2, g1, s1, tb1, tb2, gg = pieces
    gg = gg.reshape(GROUPS, 2, full)
    group_norms = jnp.sqrt(jnp.sum(gg * gg, (1, 2)))
    bound = 2.0 * math.sqrt(held * dp * S * full / GROUPS)
    factor = bound / jnp.maximum(group_norms, bound)
    clipped = jnp.sum(factor[:, None, None] * gg, 0)

    def mine(v):
        return lax.dynamic_slice_in_dim(v, t * width, width)

    return (block_out, dx, group_norms, mine(g1), mine(s1), tw1, tb1, tw2, tb2, mine(clipped[0]), mine(clipped[1]),
            owned[0], cb1.reshape(-1), owned[1].T, cb2)


def blocked(block_in, ln1_gain, ln1_shift, tok_w1, tok_b1, tok_w2, tok_b2, ln2_gain, ln2_shift,
            ch_w1, ch_b1, ch_w2, ch_b2, group_ids, out_grad):
    held = block_in.shape[0]
    bound = 2.0 * math.sqrt(held * 8 * S * 768 / GROUPS)
    flat = (held, HALF * 384)
    out, dx, grads, total = one_step(
        ch_w1, ch_w2.T, block_in.reshape(flat), out_grad.reshape(flat), ln1_gain, ln1_shift, ln2_gain, ln2_shift,
        tok_w1, tok_w2.T, tok_b1, tok_b2, ch_b1, ch_b2, group_ids)
    out, dx, d1, d2, tok1, tok2, bias1, bias2, inner, outer, sizes, gain1, shift1, gain2, shift2 = finish(bound, out, dx, grads, total)
    shape = block_in.shape
    return (out.reshape(shape), dx.reshape(shape), sizes, gain1, shift1, tok1, bias1, tok2.T, bias2,
            gain2, shift2, d1, inner, d2.T, outer)


def solution(mesh):
    stored, own, copied = P("dp", "tp", None), P("tp"), P()
    in_specs = (stored, own, own, copied, copied, copied, copied, own, own, P("dp", "tp"), copied, P("tp", "dp"), copied, P("dp"), stored)
    out_specs = (stored, stored, copied, own, own, copied, copied, copied, copied, own, own, P("dp", "tp"), copied, P("tp", "dp"), copied)
    step = blocked if (mesh.shape["dp"], mesh.shape["tp"]) == (8, 4) else general
    return jax.shard_map(step, mesh=mesh, in_specs=in_specs, out_specs=out_specs, check_vma=False)
```

```python
import functools
import math

import jax
import jax.numpy as jnp
from jax import lax
from jax.experimental import pallas as pl
from jax.experimental.pallas import tpu as pltpu
from jax.sharding import PartitionSpec as P

MESH = pl.DeviceIdType.MESH


S = 196
GROUPS = 64
F32 = jnp.float32
BF16 = jnp.bfloat16
HALF = 98
GAP = 104
ROWS = 208
BLOCK = 4 * HALF
LOW = math.sqrt(2.0 / math.pi)
CUBE = 0.044715


def place():
    dp = lax.axis_index("dp")
    t = lax.axis_index("tp")
    c, x, y = dp % 2, (dp // 2) % 2, dp // 4
    near = dict(S=owner(y, x, 1 - c), X=owner(y, 1 - x, c), Y=owner(1 - y, x, c), D=owner(1 - y, 1 - x, c))
    return dp, t, near, (y, x, c)


def owner(y, x, c):
    return (y * 2 + x) * 2 + c


def others(t):
    first = jnp.where(t == 0, 1, jnp.where(t == 1, 0, jnp.where(t == 2, 3, 2)))
    second = jnp.where(t == 0, 2, jnp.where(t == 1, 2, 1))
    third = jnp.where(t < 2, 3, 0)
    return [first, second, third]


def meet(devices):
    barrier = pltpu.get_barrier_semaphore()
    for device in devices:
        pl.semaphore_signal(barrier, inc=1, device_id=device, device_id_type=MESH)
    pl.semaphore_wait(barrier, len(devices))


def remote(src, dst, ss, rs, device):
    return pltpu.make_async_remote_copy(src_ref=src, dst_ref=dst, send_sem=ss, recv_sem=rs, device_id=device, device_id_type=MESH)


def gelu_pair(v):
    square = v * v
    up = 0.5 * jnp.tanh(v * (LOW + (LOW * CUBE) * square)) + 0.5
    value = v * up
    slope = up + value * (1.0 - up) * (2.0 * LOW + (6.0 * LOW * CUBE) * square)
    return value, slope


def turn(v):
    return pltpu.roll(v, 64, 1)


def lane_low():
    return lax.broadcasted_iota(jnp.int32, (HALF, 128), 1) < 64


def join_groups(flat, image, store):
    low = lane_low()
    for p in range(2):
        a = [flat[j, pl.ds(2 * p * BLOCK + image * HALF, HALF), :] for j in range(3)]
        b = [flat[j, pl.ds((2 * p + 1) * BLOCK + image * HALF, HALF), :] for j in range(3)]
        a1, a2, b0, b1 = turn(a[1]), turn(a[2]), turn(b[0]), turn(b[1])
        even = [a[0], jnp.where(low, a[1], b0), jnp.where(low, b0, b1)]
        odd = [jnp.where(low, a1, a2), jnp.where(low, a2, b[1]), b[2]]
        for j in range(3):
            store(0, 384 * p + 128 * j, even[j])
            store(GAP, 384 * p + 128 * j, odd[j])


def split_groups(load, flat, image):
    low = lane_low()
    for p in range(2):
        e = [load(0, 384 * p + 128 * j) for j in range(3)]
        o = [load(GAP, 384 * p + 128 * j) for j in range(3)]
        e1, e2, o0, o1 = turn(e[1]), turn(e[2]), turn(o[0]), turn(o[1])
        a = [e[0], jnp.where(low, e[1], o0), jnp.where(low, o0, o1)]
        b = [jnp.where(low, e1, e2), jnp.where(low, e2, o[1]), o[2]]
        for j in range(3):
            flat[j, pl.ds(2 * p * BLOCK + image * HALF, HALF), :] = a[j]
            flat[j, pl.ds((2 * p + 1) * BLOCK + image * HALF, HALF), :] = b[j]


def spread(packed, flat):
    for k in range(4):
        for j in range(3):
            flat[j, pl.ds(k * BLOCK, BLOCK), :] = packed[k, :, 128 * j : 128 * j + 128].astype(F32)


def pack(flat, packed):
    for k in range(4):
        for j in range(3):
            packed[k, :, 128 * j : 128 * j + 128] = flat[j, pl.ds(k * BLOCK, BLOCK), :].astype(BF16)


def to_rows(stored, flat):
    for i in range(HALF):
        for j in range(3):
            start = 384 * i + 128 * j
            flat[j, pl.ds(i, 16, stride=HALF), :] = stored[:, start : start + 128].astype(F32)


def to_stored(flat, stored):
    for i in range(HALF):
        for j in range(3):
            start = 384 * i + 128 * j
            stored[:, start : start + 128] = flat[j, pl.ds(i, 16, stride=HALF), :].astype(BF16)


def hat(v):
    average = jnp.mean(v, -1, keepdims=True)
    inverse = lax.rsqrt(jnp.mean(v * v, -1, keepdims=True) - average * average + 1e-06)
    return (v - average) * inverse, inverse


def dot(a, b):
    return jnp.dot(a, b, preferred_element_type=F32)


def dot_nt(a, b):
    return lax.dot_general(a, b, (((1,), (1,)), ((), ())), preferred_element_type=F32)


PIECE = 48
DIRECT = (0,)
SMALL = 8 * PIECE


def step_kernel(cw1, cw2, xin, din, p0, p1, p2, p3, tw1, tw2, b1, b2, cb1, cb2, ids,
                o_out, dx_out, o_fin, dx_fin, w_grad, total_out,
                wf, shard, wv, stored, xs, ds, xr, dr, flat, xb, u, act, hnt, dzt, g, s, h, ts, zs, lr, lall, t3, c2, w1, w2, w1t, w2t,
                sib, first, second, final, zz, zi, small, low, t_sib, t_chip, t_line,
                send_sem, recv_sem, line_sem, x_send, x_recv, d_send, d_recv, ln_send, ln_recv, in_sem, own_sem,
                o_send, o_recv, y_send, y_recv, sib_sem, sib_recv, a_send, a_recv, z_send, z_recv, i_recv,
                p_send, p_recv, c_send, c_recv, l_send, l_recv, b_send, b_recv, e_send, e_recv):
    dp, t, near, (y, xx, c) = place()
    line = others(t)
    order = [t] + line
    back = [line[2], line[1], line[0], t]
    chips = {"O": (y, xx), "X": (y, 1 - xx), "Y": (1 - y, xx), "D": (1 - y, 1 - xx)}
    slot = {"O": 0, "X": 1, "Y": 2, "D": 3}
    started = {"w": [], "x": [], "y": [], "": []}
    maybe = []
    state = {}
    zero = jnp.zeros((1, 768), F32)

    def go(copy, kind=""):
        copy.start()
        started[kind].append(copy)

    def local(src, dst, sem):
        copy = pltpu.make_async_copy(src, dst, sem)
        copy.start()
        return copy

    def sent(kind):
        for copy in started[kind]:
            copy.wait_send()
        started[kind] = []

    in_w1, in_w2 = local(cw1, wf.at[0], in_sem.at[0]), local(cw2, wf.at[1], in_sem.at[1])
    state["in"] = local(xin, stored, in_sem.at[2])
    meet([(near["S"], t), (near["X"], t), (near["Y"], t), (near["D"], t)] + [(dp, p) for p in line])
    sends = [0, 0]


    def send(src, who, tt, device):
        go(remote(src, wv.at[:, tt, who], send_sem.at[sends[0]], recv_sem.at[who, tt], device), "w")
        sends[0] += 1

    def along(src, tt, target):
        inside = (target >= 0) & (target <= 3)
        copy = remote(src, wv.at[:, tt, dp], line_sem.at[sends[1]], recv_sem.at[dp, tt], (dp, jnp.clip(target, 0, 3)))
        sends[1] += 1
        pl.when(inside)(copy.start)
        maybe.append((inside, copy))

    def arrived(who, tt):
        ref = wv.at[:, tt, who]
        remote(ref, ref, send_sem.at[0], recv_sem.at[who, tt], (dp, t)).wait_recv()

    def weights():
        in_w1.wait()
        in_w2.wait()
        shard[...] = wf[...].astype(BF16)
        along(shard, t, t + 1)
        along(shard, t, t - 1)
        for name in "XYS":
            send(shard, dp, t, (near[name], t))
        wv[:, t, dp] = shard[...]
        for n, ref in enumerate((p0, p1, p2, p3)):
            row = ref[...].reshape(1, 192)
            wide = jnp.concatenate([row, row, row, row], 1)
            lane = lax.broadcasted_iota(jnp.int32, (1, 768), 1)
            lr[t, n : n + 1, :] = jnp.where((lane >= 192 * t) & (lane < 192 * t + 192), wide, 0.0)
        for n, p in enumerate(line):
            go(remote(lr.at[t], lr.at[t], ln_send.at[n], ln_recv.at[t], (dp, p)))

    def column(k):
        tt = order[k]
        arrived(dp, tt)
        src = wv.at[:, tt, dp]
        along(src, tt, jnp.where(tt < t, t + 1, t - 1))
        for name in "XYS":
            send(src, dp, tt, (near[name], t))

    def neighbours(k):
        tt = order[k]
        one, two = ("X", "Y") if k % 2 == 0 else ("Y", "X")
        arrived(near[one], tt)
        src = wv.at[:, tt, near[one]]
        send(src, near[one], tt, (near[two], t))
        send(src, near[one], tt, (near["S"], t))
        arrived(near[two], tt)
        send(wv.at[:, tt, near[two]], near[two], tt, (near["S"], t))

    def diagonal(k):
        tt = order[k]
        arrived(near["D"], tt)
        send(wv.at[:, tt, near["D"]], near["D"], tt, (near["S"], t))


    def pack_input():
        state["in"].wait()
        to_rows(stored, flat)
        pack(flat, xs)
        state["in"] = local(din, stored, in_sem.at[3])

    def send_input(n):
        p = line[n]
        go(remote(xs.at[p], xr.at[t], x_send.at[n], x_recv.at[t], (dp, p)), "x")

    def pack_grad():
        state["in"].wait()
        to_rows(stored, flat)
        pack(flat, ds)

    def send_grad(n):
        p = line[n]
        go(remote(ds.at[p], dr.at[t], d_send.at[n], d_recv.at[t], (dp, p)), "y")

    def token_weights():
        gap = jnp.zeros((GAP - HALF, 128), F32)
        for n, (src, dst) in enumerate(((tw1, w1), (tw2, w2t))):
            for j in range(3):
                t3[j] = src[:, 128 * j : 128 * j + 128]
            for j in range(3):
                even, odd = t3[j, pl.ds(0, HALF, stride=2), :], t3[j, pl.ds(1, HALF, stride=2), :]
                dst[:, 128 * j : 128 * j + 128] = jnp.concatenate([even, gap, odd, gap], 0).astype(BF16)
        w1t[...] = w1[...].T
        w2[...] = w2t[...].T
        c2[...] = jnp.broadcast_to(b2[...].reshape(1, S), (128, S)).T
        few = jnp.zeros((GAP - HALF, 1), F32)
        state["shift2"] = jnp.concatenate([c2[pl.ds(0, HALF, stride=2), :][:, 0:1], few, c2[pl.ds(1, HALF, stride=2), :][:, 0:1], few], 0)
        state["shift1"] = jnp.broadcast_to(b1[...].reshape(1, 384), (8, 384)).T[:, 0:1]
        small[...] = jnp.zeros((SMALL, 768), F32)

    def join(received, own, dst):
        received[t] = own[t]
        spread(received, flat)
        few = jnp.zeros((GAP - HALF, 768), F32)
        for n in range(4):
            for start in (HALF, GAP + HALF):
                zs[n, start : start + GAP - HALF, :] = few

            def put(row, lane, v, n=n):
                zs[n, row : row + HALF, lane : lane + 128] = v

            join_groups(flat, n, put)
            dst[n] = zs[n].astype(BF16)

    def join_input():
        for p in line:
            remote(lr.at[p], lr.at[p], ln_send.at[0], ln_recv.at[p], (dp, t)).wait_recv()
        lall[...] = (lr[0] + lr[1]) + (lr[2] + lr[3])
        for p in line:
            remote(xr.at[p], xr.at[p], x_send.at[0], x_recv.at[p], (dp, t)).wait_recv()
        join(xr, xs, xb)

    def token_forward(start, stop):
        g1, s1, g2, s2 = lall[0:1], lall[1:2], lall[2:3], lall[3:4]
        shift1, shift2 = state["shift1"], state["shift2"]

        def body(n, carry):
            v = xb[n].astype(F32)
            xhat, _ = hat(v)
            a = (xhat * g1 + s1).astype(BF16)
            value, slope = gelu_pair(dot(w1t[...], a) + shift1)
            low = value.astype(BF16)
            h[n] = low
            ts[n] = slope.astype(BF16)
            r = v + dot(w2t[...], low) + shift2
            u[n] = r
            uhat, _ = hat(r)
            act[n] = (uhat * g2 + s2).astype(BF16)
            return carry

        lax.fori_loop(start, stop, body, 0)

    def block(k):
        tt = order[k]
        for name in "OXYD":
            arrived(owner(*chips[name], 1 - c), tt)
        bias = cb1[pl.ds(pl.multiple_of(tt * 768, 128), 768)].reshape(1, 768)

        def body(n, carry):
            value, slope = gelu_pair(dot(act[n], wv[0, tt].reshape(768, 768)) + bias)
            low = value.astype(BF16)
            g[tt, n] = low
            s[tt, n] = slope.astype(BF16)
            part = dot_nt(low, wv[1, tt].reshape(768, 768))
            if k == 0:
                zs[n] = part
            elif k < 3:
                zs[n] += part
            else:
                zs[n] = u[n] + (zs[n] + part + cb2[...].reshape(1, 768)).astype(BF16).astype(F32)
            return carry

        lax.fori_loop(0, 4, body, 0)

    def pack_output():
        for n in range(4):
            split_groups(lambda row, lane, n=n: zs[n, row : row + HALF, lane : lane + 128], flat, n)
        sent("x")
        pack(flat, xs)
        state["own_o"] = local(xs.at[t], o_out.at[t], own_sem.at[0])

    def send_output(n):
        p = line[n]
        go(remote(xs.at[p], o_out.at[t], o_send.at[n], o_recv.at[t], (dp, p)))

    def hidden_in():
        for n in range(4):
            hnt[:, n * ROWS : (n + 1) * ROWS] = act[n].T

    def join_grad():
        for p in line:
            remote(dr.at[p], dr.at[p], d_send.at[0], d_recv.at[p], (dp, t)).wait_recv()
        join(dr, ds, act)
        for n in range(4):
            dzt[:, n * ROWS : (n + 1) * ROWS] = act[n].T
        sent("w")
        for inside, copy in maybe:
            pl.when(inside)(copy.wait_send)
        maybe.clear()


    def hand_over(j, k):
        for name in "DXYO":
            n = slot[name]
            go(remote(wv.at[j, back[k], owner(*chips[name], 1 - c)], sib.at[j, k, n], sib_sem.at[j, k, n], sib_recv.at[j, k, n], (near["S"], t)))

    def chip_sum(j, k, name):
        n = slot[name]
        remote(sib.at[j, k, n], sib.at[j, k, n], sib_sem.at[j, k, n], sib_recv.at[j, k, n], (near["S"], t)).wait_recv()
        sib[j, k, n] = wv[j, back[k], owner(*chips[name], c)] + sib[j, k, n]

    def ways(k):
        return ("X", "Y") if k % 2 == 0 else ("Y", "X")

    def hop(j, k, src, dst, n, name):
        go(remote(src, dst, a_send.at[j, k, n], a_recv.at[j, k, n], (near[name], t)))

    def landed(j, k, dst, n):
        remote(dst, dst, a_send.at[j, k, n], a_recv.at[j, k, n], (near["S"], t)).wait_recv()

    def stage_one(j, k):
        f, s2 = ways(k)
        chip_sum(j, k, "D")
        hop(j, k, sib.at[j, k, 3], first.at[j, k], 0, s2)
        chip_sum(j, k, s2)
        hop(j, k, sib.at[j, k, slot[s2]], second.at[j, k], 1, s2)

    def stage_two(j, k):
        f, s2 = ways(k)
        n = slot[f]
        chip_sum(j, k, f)
        landed(j, k, first.at[j, k], 0)
        sib[j, k, n] = sib[j, k, n] + first[j, k]
        hop(j, k, sib.at[j, k, n], final.at[j, k], 2, f)

    def stage_three(j, k):
        chip_sum(j, k, "O")
        landed(j, k, second.at[j, k], 1)
        landed(j, k, final.at[j, k], 2)
        total = sib[j, k, 0].astype(F32) + second[j, k].astype(F32) + final[j, k].astype(F32)
        if k < 3:
            sib[j, k, 0] = total.astype(BF16)
        else:
            w_grad[j] = total

    inner = (t == 1) | (t == 2)
    ends = jnp.logical_not(inner)
    beside = back[2]
    across = jnp.where(t < 2, 2, 1)

    def along_in(j, n):
        remote(zz.at[j, n], zz.at[j, n], z_send.at[j, 0], z_recv.at[j, n], (dp, t)).wait_recv()

    def stage_four(j, k):
        piece, p = sib.at[j, k, 0], back[k]
        if k == 2 or j in DIRECT:
            go(remote(piece, zz.at[j, t], z_send.at[j, k], z_recv.at[j, t], (dp, p)))
            return
        copy = remote(piece, zi.at[j, p % 2], z_send.at[j, k], i_recv.at[j, p % 2], (dp, beside))
        pl.when(ends)(copy.start)
        maybe.append((ends, copy))

    def stage_five(j, k):
        piece, p = sib.at[j, k, 0], back[k]
        copy = remote(piece, zz.at[j, t], z_send.at[j, k], z_recv.at[j, t], (dp, p))

        @pl.when(inner)
        def _():
            there = zi.at[j, p % 2]
            remote(there, there, z_send.at[j, k], i_recv.at[j, p % 2], (dp, t)).wait_recv()
            piece[...] = piece[...] + there[...]
            copy.start()

        maybe.append((inner, copy))

    def stage_six(j):
        for n in line if j in DIRECT else (beside, across):
            along_in(j, n)
            w_grad[j] += zz[j, n].astype(F32)

    def second_weight(k):
        wv[1, back[k]] = dot(dzt[...], g[back[k]].reshape(4 * ROWS, 768)).astype(BF16).reshape(8, 96, 768)
        hand_over(1, k)

    def data(k):
        tt = back[k]

        def body(n, bias):
            low = (dot(act[n], wv[1, tt].reshape(768, 768)) * s[tt, n].astype(F32)).astype(BF16)
            s[tt, n] = low
            part = dot_nt(low, wv[0, tt].reshape(768, 768))
            if k == 0:
                zs[n] = part
            else:
                zs[n] += part
            return bias + jnp.sum(low.astype(F32), 0, keepdims=True)

        small[pl.ds(HALF + 1 + tt, 1), :] = lax.fori_loop(0, 4, body, zero)

    def first_weight(k):
        wv[0, back[k]] = dot(hnt[...], s[back[k]].reshape(4 * ROWS, 768)).astype(BF16).reshape(8, 96, 768)
        hand_over(0, k)

    def token_backward(start, stop):
        g1, s1, g2 = lall[0:1], lall[1:2], lall[2:3]
        row = lax.broadcasted_iota(jnp.int32, (ROWS, 768), 0)
        ones = jnp.ones((8, 768), BF16)
        groups = lax.broadcasted_iota(jnp.int32, (GROUPS, 16), 0) == ids[...].reshape(1, 16)
        lane = lax.broadcasted_iota(jnp.int32, (GROUPS, 16), 1)

        def body(n, carry):
            sum_g1, sum_s1, sum_b2, sum_dz = carry
            d, grad = zs[n], act[n].astype(F32)
            uhat, inv_u = hat(u[n])
            member = jnp.sum(jnp.where(groups & (lane == 4 * t + n), 1.0, 0.0), -1, keepdims=True)
            small[208:272, :] += member * jnp.sum(d * uhat, 0, keepdims=True)
            small[272:336, :] += member * jnp.sum(d, 0, keepdims=True)
            e = d * g2
            du = grad + inv_u * (e - jnp.mean(e, -1, keepdims=True) - uhat * jnp.mean(e * uhat, -1, keepdims=True))
            low = du.astype(BF16)
            dpre = (dot(w2[...], low) * ts[n].astype(F32)).astype(BF16)
            xhat, inv_x = hat(xb[n].astype(F32))
            a = jnp.where(row == HALF, 1.0, xhat * g1 + s1).astype(BF16)
            tok1 = dot_nt(a, dpre)
            tok2 = dot_nt(low, h[n])
            for begin, size in ((0, HALF + 1), (GAP, HALF)):
                small[begin : begin + size, 0:384] += tok1[begin : begin + size]
            for begin, size in ((0, HALF), (GAP, HALF)):
                small[begin : begin + size, 384:768] += tok2[begin : begin + size]
            da = dot(w1[...], dpre)
            e1 = da * g1
            zs[n] = du + inv_x * (e1 - jnp.mean(e1, -1, keepdims=True) - xhat * jnp.mean(e1 * xhat, -1, keepdims=True))
            return (sum_g1 + jnp.sum(da * xhat, 0, keepdims=True), sum_s1 + jnp.sum(da, 0, keepdims=True),
                    sum_b2 + dot_nt(ones, low), sum_dz + jnp.sum(grad, 0, keepdims=True))

        sums = state.get("sums", (zero, zero, jnp.zeros((8, ROWS), F32), zero))
        state["sums"] = lax.fori_loop(start, stop, body, sums)

    def pack_dx():
        for n in range(4):
            split_groups(lambda r, lane, n=n: zs[n, r : r + HALF, lane : lane + 128], flat, n)
        sent("y")
        pack(flat, ds)
        state["own_x"] = local(ds.at[t], dx_out.at[t], own_sem.at[2])

    def send_dx(n):
        p = line[n]
        go(remote(ds.at[p], dx_out.at[t], y_send.at[n], y_recv.at[t], (dp, p)))

    def unpack_output():
        state["own_o"].wait()
        for p in line:
            remote(o_out.at[p], o_out.at[p], o_send.at[0], o_recv.at[p], (dp, t)).wait_recv()
        local(o_out, dr, own_sem.at[0]).wait()
        spread(dr, flat)
        to_stored(flat, stored)
        state["out"] = local(stored, o_fin, own_sem.at[1])

    def unpack_dx():
        state["own_x"].wait()
        for p in line:
            remote(dx_out.at[p], dx_out.at[p], y_send.at[0], y_recv.at[p], (dp, t)).wait_recv()
        local(dx_out, xr, own_sem.at[0]).wait()
        spread(xr, flat)
        state["out"].wait()
        to_stored(flat, stored)
        state["out"] = local(stored, dx_fin, own_sem.at[1])

    chip = dp // 2
    far = [("X", near["X"] // 2), ("Y", near["Y"] // 2), ("D", near["D"] // 2)]

    def part(ref, core, q):
        return ref.at[pl.ds(pl.multiple_of((core * 4 + q) * PIECE, 8), PIECE)]

    def half(ref, core):
        return ref.at[pl.ds(pl.multiple_of(core * 4 * PIECE, 8), 4 * PIECE)]

    own = part(total_out, c, chip)

    def total_zero():
        sum_g1, sum_s1, sum_b2, sum_dz = state["sums"]
        small[202:203, :] = sum_g1
        small[203:204, :] = sum_s1
        small[204:205, 0:ROWS] = sum_b2[0:1]
        small[205:206, :] = sum_dz
        half(low, 1 - c)[...] = half(small, 1 - c)[...].astype(BF16)
        go(remote(half(low, 1 - c), t_sib, p_send, p_recv, (near["S"], t)))

    def total_one():
        remote(t_sib, t_sib, p_send, p_recv, (near["S"], t)).wait_recv()
        both = half(small, c)[...] + t_sib[...].astype(F32)
        half(small, c)[...] = both
        half(low, c)[...] = both.astype(BF16)
        for n, (name, q) in enumerate(far):
            go(remote(part(low, c, q), t_chip.at[n], c_send.at[n], c_recv.at[n], (near[name], t)))

    def total_two():
        total = part(small, c, chip)[...]
        for n in range(3):
            remote(t_chip.at[n], t_chip.at[n], c_send.at[n], c_recv.at[n], (near["S"], t)).wait_recv()
            total = total + t_chip[n].astype(F32)
        part(small, c, chip)[...] = total
        copy = remote(t_line.at[3], t_line.at[0], l_send.at[0], l_recv.at[0], (dp, beside))

        @pl.when(ends)
        def _():
            t_line[3] = total.astype(BF16)
            copy.start()

        maybe.append((ends, copy))

    def line_wait(n):
        remote(t_line.at[n], t_line.at[n], l_send.at[0], l_recv.at[n], (dp, t)).wait_recv()

    def total_pair():
        copy = remote(t_line.at[2], t_line.at[1], l_send.at[1], l_recv.at[1], (dp, across))

        @pl.when(inner)
        def _():
            line_wait(0)
            t_line[2] = (part(small, c, chip)[...] + t_line[0].astype(F32)).astype(BF16)
            copy.start()

        maybe.append((inner, copy))

    def total_line():
        copy = remote(own, own, l_send.at[2], l_recv.at[2], (dp, beside))

        @pl.when(inner)
        def _():
            line_wait(1)
            own[...] = (t_line[2].astype(F32) + t_line[1].astype(F32)).astype(BF16)
            copy.start()

        maybe.append((inner, copy))

    def total_three():
        @pl.when(ends)
        def _():
            remote(own, own, l_send.at[2], l_recv.at[2], (dp, t)).wait_recv()

        for n, (name, q) in enumerate(far):
            go(remote(own, own, b_send.at[n], b_recv.at[chip], (near[name], t)))
        go(remote(own, own, e_send.at[3], e_recv.at[chip], (near["S"], t)))

    def total_five():
        for n, (name, q) in enumerate(far):
            there = part(total_out, c, q)
            remote(there, there, b_send.at[0], b_recv.at[q], (dp, t)).wait_recv()
            go(remote(there, there, e_send.at[n], e_recv.at[q], (near["S"], t)))

    def total_six():
        for q in range(4):
            there = part(total_out, 1 - c, q)
            remote(there, there, e_send.at[0], e_recv.at[q], (dp, t)).wait_recv()

    weights()
    pack_input()
    column(1)
    neighbours(0)
    column(2)
    send_input(0)
    send_input(1)
    send_input(2)
    neighbours(1)
    diagonal(0)
    column(3)
    pack_grad()
    token_weights()
    neighbours(2)
    diagonal(1)
    neighbours(3)
    diagonal(2)
    diagonal(3)
    send_grad(0)
    send_grad(1)
    send_grad(2)
    join_input()
    token_forward(0, 4)
    block(0)
    block(1)
    block(2)
    block(3)
    pack_output()
    send_output(0)
    send_output(1)
    send_output(2)
    hidden_in()
    join_grad()
    data(0)
    second_weight(0)
    data(1)
    second_weight(1)
    stage_one(1, 0)
    data(2)
    second_weight(2)
    stage_one(1, 1)
    data(3)
    second_weight(3)
    stage_one(1, 2)
    token_backward(0, 4)
    pack_dx()
    total_zero()
    send_dx(0)
    send_dx(1)
    send_dx(2)
    stage_one(1, 3)
    total_one()
    stage_two(1, 0)
    stage_two(1, 1)
    stage_two(1, 2)
    stage_two(1, 3)
    first_weight(0)
    first_weight(1)
    stage_one(0, 0)
    total_two()
    stage_three(1, 0)
    stage_four(1, 0)
    first_weight(2)
    stage_one(0, 1)
    stage_three(1, 1)
    stage_four(1, 1)
    first_weight(3)
    stage_one(0, 2)
    stage_three(1, 2)
    stage_four(1, 2)
    stage_one(0, 3)
    stage_three(1, 3)
    stage_two(0, 0)
    stage_two(0, 1)
    unpack_output()
    stage_two(0, 2)
    stage_two(0, 3)
    total_pair()
    stage_five(1, 0)
    stage_five(1, 1)
    stage_three(0, 0)
    stage_four(0, 0)
    total_line()
    stage_three(0, 1)
    stage_four(0, 1)
    total_three()
    stage_three(0, 2)
    stage_four(0, 2)
    stage_three(0, 3)
    unpack_dx()
    total_five()
    stage_six(1)
    stage_six(0)
    total_six()

    state["out"].wait()
    sent("")
    for inside, copy in maybe:
        pl.when(inside)(copy.wait_send)


def one_step(*operands):
    any_, vmem = pl.BlockSpec(memory_space=pl.ANY), pl.BlockSpec(memory_space=pltpu.VMEM)
    sds = jax.ShapeDtypeStruct
    dma = pltpu.SemaphoreType.DMA
    V = pltpu.VMEM
    wshape, act, tok, packed, piece = (2, 4, 8, 96, 768), (4, ROWS, 768), (4, 384, 768), (4, BLOCK, 384), (96, 768)
    return pl.pallas_call(step_kernel,
        out_shape=[sds(packed, BF16), sds(packed, BF16), sds((16, HALF * 384), BF16), sds((16, HALF * 384), BF16), sds((2,) + piece, F32), sds((SMALL, 768), BF16)],
        in_specs=[any_] * 4 + [vmem] * 11, out_specs=[any_] * 4 + [vmem] * 2,
        scratch_shapes=[V((2, 96, 768), F32), V((2, 96, 768), BF16), V(wshape, BF16), V((16, HALF * 384), BF16), V(packed, BF16), V(packed, BF16),
            V(packed, BF16), V(packed, BF16), V((3, 4 * BLOCK, 128), F32), V(act, BF16), V(act, F32), V(act, BF16), V((768, 4 * ROWS), BF16), V((768, 4 * ROWS), BF16),
            V((4,) + act, BF16), V((4,) + act, BF16), V(tok, BF16), V(tok, BF16), V(act, F32), V((4, 8, 768), F32), V((8, 768), F32),
            V((3, S, 128), F32), V((S, 128), F32), V((ROWS, 384), BF16), V((384, ROWS), BF16), V((384, ROWS), BF16), V((ROWS, 384), BF16),
            V((2, 4, 4) + piece, BF16), V((2, 4) + piece, BF16), V((2, 4) + piece, BF16), V((2, 4) + piece, BF16), V((2, 4) + piece, BF16), V((2, 2) + piece, BF16),
            V((SMALL, 768), F32), V((SMALL, 768), BF16), V((4 * PIECE, 768), BF16), V((3, PIECE, 768), BF16), V((4, PIECE, 768), BF16),
            dma((28,)), dma((8, 4)), dma((5,)), dma((3,)), dma((4,)), dma((3,)), dma((4,)), dma((3,)), dma((4,)), dma((4,)), dma((3,)),
            dma((3,)), dma((4,)), dma((3,)), dma((4,)), dma((2, 4, 4)), dma((2, 4, 4)), dma((2, 4, 3)), dma((2, 4, 3)), dma((2, 4)), dma((2, 4)), dma((2, 2)),
            dma, dma, dma((3,)), dma((3,)), dma((3,)), dma((4,)), dma((3,)), dma((4,)), dma((4,)), dma((4,))],
        compiler_params=pltpu.CompilerParams(collective_id=1, has_side_effects=True, vmem_limit_bytes=63 << 20))(*operands)


def finish_kernel(bound, o_in, dx_in, grads_in, total_in, o_out, dx_out, d1, d2, tok1, tok2, bias1, bias2, inner, outer, sizes, gain1, shift1, gain2, shift2, o, dx, grads, low, t3, total, sems):
    t = lax.axis_index("tp")
    copies = [pltpu.make_async_copy(src, dst, sems.at[n]) for n, (src, dst) in enumerate(((o_in, o), (dx_in, dx), (total_in, low), (grads_in, grads)))]
    for copy in copies:
        copy.start()
    for n, (src, dst) in enumerate(((o, o_out), (dx, dx_out))):
        copies[n].wait()
        copies[n] = pltpu.make_async_copy(src, dst, sems.at[4 + n])
        copies[n].start()
    copies[2].wait()
    copies[3].wait()
    total[...] = low[...].astype(F32)
    d1[...] = grads[0]
    d2[...] = grads[1]
    for start, dst in ((0, tok1), (384, tok2)):
        for j in range(3):
            lanes = slice(start + 128 * j, start + 128 * j + 128)
            t3[j, pl.ds(0, HALF, stride=2), :] = total[0:HALF, lanes]
            t3[j, pl.ds(1, HALF, stride=2), :] = total[GAP : GAP + HALF, lanes]
        for j in range(3):
            dst[:, 128 * j : 128 * j + 128] = t3[j]
    bias1[...] = total[HALF : HALF + 1, 0:384].reshape(384)
    for k in range(4):
        inner[pl.ds(768 * k, 768)] = total[HALF + 1 + k : HALF + 2 + k, :].reshape(768)
    column = jnp.broadcast_to(total[204:205, 0:ROWS], (128, ROWS)).T
    t3[0, pl.ds(0, HALF, stride=2), :] = column[0:HALF]
    t3[0, pl.ds(1, HALF, stride=2), :] = column[GAP : GAP + HALF]
    bias2[...] = t3[0].T[0:1].reshape(S)
    outer[...] = total[205:206, :].reshape(768)
    gg, gb = total[208:272, :], total[272:336, :]
    size = jnp.sqrt(jnp.sum(gg * gg + gb * gb, -1, keepdims=True))
    factor = bound / jnp.maximum(size, bound)
    sizes[...] = jnp.broadcast_to(size, (GROUPS, 128)).T[0:1].reshape(GROUPS)

    def own(v, dst):
        picked = jnp.zeros((1, 192), F32)
        for q in range(4):
            picked = jnp.where(t == q, v[:, 192 * q : 192 * q + 192], picked)
        dst[...] = picked.reshape(192)

    own(total[202:203, :], gain1)
    own(total[203:204, :], shift1)
    own(jnp.sum(factor * gg, 0, keepdims=True), gain2)
    own(jnp.sum(factor * gb, 0, keepdims=True), shift2)
    copies[0].wait()
    copies[1].wait()


def finish(bound, *operands):
    vmem = pl.BlockSpec(memory_space=pltpu.VMEM)
    shapes = [(16, HALF * 384)] * 2 + [(96, 768)] * 2 + [(S, 384)] * 2 + [(384,), (S,), (3072,), (768,), (GROUPS,)] + [(192,)] * 4
    return pl.pallas_call(functools.partial(finish_kernel, bound),
        out_shape=[jax.ShapeDtypeStruct(v, BF16 if n < 2 else F32) for n, v in enumerate(shapes)],
        in_specs=[pl.BlockSpec(memory_space=pl.ANY)] * 4, out_specs=[pl.BlockSpec(memory_space=pl.ANY)] * 2 + [vmem] * (len(shapes) - 2),
        scratch_shapes=[pltpu.VMEM((16, HALF * 384), BF16), pltpu.VMEM((16, HALF * 384), BF16), pltpu.VMEM((2, 96, 768), F32), pltpu.VMEM((SMALL, 768), BF16), pltpu.VMEM((3, S, 128), F32), pltpu.VMEM((SMALL, 768), F32), pltpu.SemaphoreType.DMA((6,))],
        compiler_params=pltpu.CompilerParams(vmem_limit_bytes=60 << 20))(*operands)


epsilon = 1e-06
highest = lax.Precision.HIGHEST


def normalised(values):
    average = jnp.mean(values, -1, keepdims=True)
    inverse = lax.rsqrt(jnp.mean(values * values, -1, keepdims=True) - average * average + epsilon)
    return (values - average) * inverse, inverse


def norm_back(grad_hat, normed, inverse):
    return inverse * (
        grad_hat - jnp.mean(grad_hat, -1, keepdims=True) - normed * jnp.mean(grad_hat * normed, -1, keepdims=True)
    )


def general(block_in, ln1_gain, ln1_shift, tok_w1, tok_b1, tok_w2, tok_b2, ln2_gain, ln2_shift,
               ch_w1, ch_b1, ch_w2, ch_b2, group_ids, out_grad):
    f32 = jnp.float32
    bf16 = jnp.bfloat16
    tp = lax.axis_size("tp")
    dp = lax.axis_size("dp")
    held = block_in.shape[0]
    images = held // tp
    width = block_in.shape[2] // S
    full = width * tp
    t = lax.axis_index("tp")

    def whole_images(stored):
        got = lax.all_to_all(stored.reshape(tp, images, S * width), "tp", 0, 0, tiled=True)
        return got.reshape(tp, images, S, width).transpose(1, 2, 0, 3).reshape(images, S, full)

    def stored(values):
        parts = values.reshape(images, S, tp, width).transpose(2, 0, 1, 3).reshape(tp, images, S * width)
        return lax.all_to_all(parts, "tp", 0, 0, tiled=True).reshape(held, 1, S * width)

    rows = ch_w1.shape[0]
    shard = jnp.stack([ch_w1.astype(bf16), ch_w2.T.astype(bf16)])
    gathered = lax.all_gather(lax.all_gather(shard, "tp", axis=1), "dp", axis=2)
    gathered = gathered.reshape(2, tp, dp * rows, shard.shape[2])
    norms = lax.all_gather(jnp.stack([ln1_gain, ln1_shift, ln2_gain, ln2_shift]), "tp", axis=1, tiled=True)
    x = whole_images(block_in).astype(f32)
    dz_low = whole_images(out_grad)
    token_w1 = tok_w1.astype(bf16)
    token_w2 = tok_w2.astype(bf16)
    xhat, inv_x = normalised(x)
    mixed = (xhat * norms[0] + norms[1]).astype(bf16)
    pre = jnp.einsum("nsc,sk->nkc", mixed, token_w1, preferred_element_type=f32) + tok_b1[:, None]
    hidden, hidden_back = jax.vjp(jax.nn.gelu, pre)
    hidden = hidden.astype(bf16)
    u = x + jnp.einsum("nkc,ks->nsc", hidden, token_w2, preferred_element_type=f32) + tok_b2[:, None]
    uhat, inv_u = normalised(u)
    count = images * S
    hn = (uhat * norms[2] + norms[3]).astype(bf16).reshape(count, full)
    dz = dz_low.reshape(count, full)
    z = jnp.zeros((count, full), f32)
    dhn = jnp.zeros((count, full), f32)
    grads1, grads2, bias = [], [], []
    inner = shard.shape[2]
    for j in range(tp):
        q = jnp.dot(hn, gathered[0, j], preferred_element_type=f32) + ch_b1[j * inner : (j + 1) * inner]
        g, g_back = jax.vjp(jax.nn.gelu, q)
        g = g.astype(bf16)
        z = z + jnp.einsum("rh,ch->rc", g, gathered[1, j], preferred_element_type=f32)
        dg = jnp.dot(dz, gathered[1, j], preferred_element_type=f32)
        dq = g_back(dg)[0].astype(bf16)
        grads2.append(jnp.einsum("rc,rh->ch", dz, g, preferred_element_type=f32).astype(bf16))
        grads1.append(jnp.einsum("rc,rh->ch", hn, dq, preferred_element_type=f32).astype(bf16))
        bias.append(jnp.sum(dq.astype(f32), 0))
        dhn = dhn + jnp.einsum("rh,ch->rc", dq, gathered[0, j], preferred_element_type=f32)
    z = (z + ch_b2).astype(bf16).astype(f32).reshape(u.shape)
    block_out = stored((u + z).astype(bf16))
    dhn = dhn.reshape(u.shape)
    dz32 = dz_low.astype(f32)
    image_gain = jnp.sum(dhn * uhat, 1)
    image_shift = jnp.sum(dhn, 1)
    du = dz32 + norm_back(dhn * norms[2], uhat, inv_u)
    dp_low = du.astype(bf16)
    dh = jnp.einsum("nsc,ks->nkc", dp_low, token_w2, preferred_element_type=f32)
    d_tok_w2 = jnp.einsum("nkc,nsc->ks", hidden, dp_low, preferred_element_type=f32)
    d_tok_b2 = jnp.sum(dp_low.astype(f32), (0, 2))
    dpre = hidden_back(dh)[0].astype(bf16)
    d_tok_w1 = jnp.einsum("nsc,nkc->sk", mixed, dpre, preferred_element_type=f32)
    d_tok_b1 = jnp.sum(dpre.astype(f32), (0, 2))
    da = jnp.einsum("nkc,sk->nsc", dpre, token_w1, preferred_element_type=f32)
    d_gain1 = jnp.sum(da * xhat, (0, 1))
    d_shift1 = jnp.sum(da, (0, 1))
    dx = stored((du + norm_back(da * norms[0], xhat, inv_x)).astype(bf16))

    gradient = jnp.stack([jnp.stack(grads1), jnp.stack(grads2)]).reshape(2, tp, dp, rows, inner)
    owned = lax.psum_scatter(lax.psum_scatter(gradient, "tp", scatter_dimension=1, tiled=True).astype(bf16), "dp", scatter_dimension=2, tiled=True)
    owned = owned.astype(f32).reshape(2, rows, inner)

    ids = lax.dynamic_slice_in_dim(group_ids, t * images, images)
    member = (ids[:, None] == jnp.arange(GROUPS)[None, :]).astype(f32)
    groups = jnp.dot(member.T, jnp.concatenate([image_gain, image_shift], 1), precision=highest)
    flat = [d_tok_w1, d_tok_w2, jnp.stack(bias), jnp.sum(dz32, (0, 1)), d_gain1, d_shift1, d_tok_b1, d_tok_b2, groups]
    sizes = [v.size for v in flat]
    need = sum(sizes)
    unit = 64 * full
    padded = -(-need // unit) * unit
    packed = jnp.concatenate([v.reshape(-1) for v in flat] + [jnp.zeros((padded - need,), f32)]).reshape(-1, full)
    total = lax.psum(packed, ("dp", "tp"))
    total = total.reshape(-1)
    pieces, start = [], 0
    for v in flat:
        pieces.append(total[start : start + v.size].reshape(v.shape))
        start += v.size
    tw1, tw2, cb1, cb2, g1, s1, tb1, tb2, gg = pieces
    gg = gg.reshape(GROUPS, 2, full)
    group_norms = jnp.sqrt(jnp.sum(gg * gg, (1, 2)))
    bound = 2.0 * math.sqrt(held * dp * S * full / GROUPS)
    factor = bound / jnp.maximum(group_norms, bound)
    clipped = jnp.sum(factor[:, None, None] * gg, 0)

    def mine(v):
        return lax.dynamic_slice_in_dim(v, t * width, width)

    return (block_out, dx, group_norms, mine(g1), mine(s1), tw1, tb1, tw2, tb2, mine(clipped[0]), mine(clipped[1]),
            owned[0], cb1.reshape(-1), owned[1].T, cb2)


def blocked(block_in, ln1_gain, ln1_shift, tok_w1, tok_b1, tok_w2, tok_b2, ln2_gain, ln2_shift,
            ch_w1, ch_b1, ch_w2, ch_b2, group_ids, out_grad):
    held = block_in.shape[0]
    bound = 2.0 * math.sqrt(held * 8 * S * 768 / GROUPS)
    flat = (held, HALF * 384)
    _, _, out, dx, grads, total = one_step(
        ch_w1, ch_w2.T, block_in.reshape(flat), out_grad.reshape(flat), ln1_gain, ln1_shift, ln2_gain, ln2_shift,
        tok_w1, tok_w2.T, tok_b1, tok_b2, ch_b1, ch_b2, group_ids)
    out, dx, d1, d2, tok1, tok2, bias1, bias2, inner, outer, sizes, gain1, shift1, gain2, shift2 = finish(bound, out, dx, grads, total)
    shape = block_in.shape
    return (out.reshape(shape), dx.reshape(shape), sizes, gain1, shift1, tok1, bias1, tok2.T, bias2,
            gain2, shift2, d1, inner, d2.T, outer)


def solution(mesh):
    stored, own, copied = P("dp", "tp", None), P("tp"), P()
    in_specs = (stored, own, own, copied, copied, copied, copied, own, own, P("dp", "tp"), copied, P("tp", "dp"), copied, P("dp"), stored)
    out_specs = (stored, stored, copied, own, own, copied, copied, copied, copied, own, own, P("dp", "tp"), copied, P("tp", "dp"), copied)
    step = blocked if (mesh.shape["dp"], mesh.shape["tp"]) == (8, 4) else general
    return jax.shard_map(step, mesh=mesh, in_specs=in_specs, out_specs=out_specs, check_vma=False)
```
